32 devices in a mesh: ctx: 8 (over z, x), fsdp: 4 (over y, core).
Axes of the slice: x: 2, y: 2, z: 4, core: 2. Of those that a mesh axis runs over, the one named last changes fastest.
Arguments:
- tokens: bfloat16 [4, 1024, 768], P('fsdp', 'ctx'), may hold values from -6 to 6
- block_order: int32 [4, 16], P('fsdp'), may hold values from 0 to 15, each once within a row
- attn_gain: bfloat16 [1, 768], P(None, ('ctx', 'fsdp')), may hold values from 0.5 to 1.5
- attn_shift: bfloat16 [1, 768], P(None, ('ctx', 'fsdp')), may hold values from -3 to 3
- w_qkv: bfloat16 [1, 768, 2304], P(None, ('ctx', 'fsdp')), may hold values from -2 to 2, as said below
- query_bias: bfloat16 [1, 768], P(None, ('ctx', 'fsdp')), may hold values from -3 to 3
- value_bias: bfloat16 [1, 768], P(None, ('ctx', 'fsdp')), may hold values from -0.59765625 to 0.59765625
- w_out: bfloat16 [1, 768, 768], P(None, ('ctx', 'fsdp')), may hold values from -1.75 to 1.75
- out_bias: bfloat16 [1, 768], P(None, ('ctx', 'fsdp')), may hold values from -4 to 4
- mlp_gain: bfloat16 [1, 768], P(None, ('ctx', 'fsdp')), may hold values from 0.5 to 1.5
- mlp_shift: bfloat16 [1, 768], P(None, ('ctx', 'fsdp')), may hold values from -3 to 3
- w_fc: bfloat16 [1, 768, 3072], P(None, ('ctx', 'fsdp')), may hold values from -0.21875 to 0.21875
- fc_bias: bfloat16 [1, 3072], P(None, ('ctx', 'fsdp')), may hold values from -3 to 3
- w_proj: bfloat16 [1, 3072, 768], P(None, ('ctx', 'fsdp')), may hold values from -0.109375 to 0.109375
- proj_bias: bfloat16 [1, 768], P(None, ('ctx', 'fsdp')), may hold values from -4 to 4
- cotangent: float32 [4, 1024, 768], P('fsdp', 'ctx'), may hold values from -6 to 6
Outputs:
- block_out: bfloat16 [4, 1024, 768], P('fsdp', 'ctx')
- input_grad: float32 [4, 1024, 768], P('fsdp', 'ctx')
- grad_attn_gain: float32 [1, 768], P(None, ('ctx', 'fsdp'))
- grad_attn_shift: float32 [1, 768], P(None, ('ctx', 'fsdp'))
- grad_w_qkv: float32 [1, 768, 2304], P(None, ('ctx', 'fsdp'))
- grad_query_bias: float32 [1, 768], P(None, ('ctx', 'fsdp'))
- grad_value_bias: float32 [1, 768], P(None, ('ctx', 'fsdp'))
- grad_w_out: float32 [1, 768, 768], P(None, ('ctx', 'fsdp'))
- grad_out_bias: float32 [1, 768], P(None, ('ctx', 'fsdp'))
- grad_mlp_gain: float32 [1, 768], P(None, ('ctx', 'fsdp'))
- grad_mlp_shift: float32 [1, 768], P(None, ('ctx', 'fsdp'))
- grad_w_fc: float32 [1, 768, 3072], P(None, ('ctx', 'fsdp'))
- grad_fc_bias: float32 [1, 3072], P(None, ('ctx', 'fsdp'))
- grad_w_proj: float32 [1, 3072, 768], P(None, ('ctx', 'fsdp'))
- grad_proj_bias: float32 [1, 768], P(None, ('ctx', 'fsdp'))
The draws below stay inside these ranges and needn't reach their ends.
Inputs may be any that keep to these rules, and one draw needn't show every extreme that they name: `block_order`: each row is a permutation: every one of the 16 position blocks of a sequence is stored exactly once. `w_qkv`: entries are of order 768 ** -0.5.
All inputs are finite; a program needn't handle non-finite values.
Results may differ from the reference program's by a relative error of at most 0.02.
Values may be sent and summed in bfloat16 or wider, within the bound.
No kernel may reach another device: no remote copies, remote signals or barrier semaphores. Data moves between devices by JAX's collectives and lax.ppermute only.
A program may use at most 192 MiB of HBM per device.

```python
import jax
import jax.numpy as jnp
from jax import lax

D = 768
FF = 3072
HEADS = 12
HEAD_DIM = 64
LAYERS = 1
TOK_DEV = 128
HALF = 64
NBLK = 16
L = 1024
SEQS = 4


def draw_w_qkv(key, part):
    first_key = jax.random.fold_in(key, 17)
    base = jax.random.truncated_normal(first_key, -4.0, 4.0, (LAYERS, D, 3 * D), jnp.float32) * D ** (-0.5)
    return jnp.clip(base, -2.0, 2.0).astype(jnp.bfloat16)


def shard_levels(stream_key, dims, split, low, largest):
    level, own = 1.0, jax.random.fold_in(stream_key, 6)
    for axis_at, shards_of in split:
        steps = jnp.exp(jax.random.uniform(jax.random.fold_in(own, axis_at), (shards_of,), jnp.float32, low / len(split), largest / len(split)))
        level = level * jnp.repeat(steps, dims[axis_at] // shards_of).reshape([-1 if axis == axis_at else 1 for axis in range(len(dims))])
    return level


def scatter_about(rng, dims, width, reach, pieces=(), kind=jnp.bfloat16):
    entries = jax.random.normal(rng, dims, jnp.float32) * width
    if len(pieces) > 0:
        entries = shard_levels(rng, dims, pieces, -0.22, 0.18) * entries
    return jnp.clip(entries, min=-reach, max=reach).astype(kind)


def setup_inputs(seed: int = 0) -> dict:
    streams_of = jax.random.split(jax.random.key(seed), 17)
    tokens = scatter_about(streams_of[0], (SEQS, L, D), 1.0, 6.0, ((0, 4), (1, 8)))
    block_order = jax.vmap(lambda own: jax.random.permutation(own, NBLK))(jax.random.split(streams_of[1], SEQS)).reshape((SEQS, NBLK)).astype(jnp.int32)
    attn_gain = jnp.clip(1.0 + 0.1 * jax.random.normal(streams_of[2], (LAYERS, D), jnp.float32), 0.5, 1.5).astype(jnp.bfloat16)
    attn_shift = scatter_about(streams_of[3], (LAYERS, D), 0.5, 3.0, ((1, 32),))
    w_qkv = draw_w_qkv(jax.random.fold_in(streams_of[16], 71), 0)
    query_bias = scatter_about(streams_of[5], (LAYERS, D), 0.5, 3.0, ((1, 32),))
    value_bias = scatter_about(streams_of[6], (LAYERS, D), 0.1, 0.59765625, ((1, 32),))
    w_out = scatter_about(streams_of[7], (LAYERS, D, D), (D // 64) ** -0.5, 1.75, ((1, 32),))
    out_bias = scatter_about(streams_of[8], (LAYERS, D), 1.0, 4.0, ((1, 32),))
    mlp_gain = jnp.clip(0.5 + 1.0 * jax.random.uniform(streams_of[9], (LAYERS, D), jnp.float32) ** shard_levels(streams_of[9], (LAYERS, D), ((1, 32),), -0.2, 0.2), 0.5, 1.5).astype(jnp.bfloat16)
    mlp_shift = scatter_about(streams_of[10], (LAYERS, D), 0.5, 3.0, ((1, 32),))
    w_fc = scatter_about(streams_of[11], (LAYERS, D, FF), D ** -0.5, 0.21875, ((1, 32),))
    fc_bias = scatter_about(streams_of[12], (LAYERS, FF), 0.5, 3.0, ((1, 32),))
    w_proj = scatter_about(streams_of[13], (LAYERS, FF, D), FF ** -0.5, 0.109375, ((1, 32),))
    proj_bias = scatter_about(streams_of[14], (LAYERS, D), 1.0, 4.0, ((1, 32),))
    cotangent = scatter_about(streams_of[15], (SEQS, L, D), 1.0, 6.0, ((0, 4), (1, 8)), jnp.float32)
    return dict(tokens=tokens, block_order=block_order, attn_gain=attn_gain, attn_shift=attn_shift, w_qkv=w_qkv, query_bias=query_bias, value_bias=value_bias, w_out=w_out, out_bias=out_bias, mlp_gain=mlp_gain, mlp_shift=mlp_shift, w_fc=w_fc, fc_bias=fc_bias, w_proj=w_proj, proj_bias=proj_bias, cotangent=cotangent)


EPSILON = 1e-05
GELU_SCALE = 0.7978845608028654
GELU_CUBIC = 0.044715

def gelu_value(value):
    return 0.5 * value * (1.0 + jnp.tanh(GELU_SCALE * (value + GELU_CUBIC * value * value * value)))

def gelu_slope(value):
    tangent = jnp.tanh(GELU_SCALE * (value + GELU_CUBIC * value * value * value))
    return 0.5 * (1.0 + tangent) + 0.5 * value * (1.0 - tangent * tangent) * GELU_SCALE * (1.0 + 3.0 * GELU_CUBIC * value * value)

def round_half(value):
    return lax.optimization_barrier(value.astype(jnp.bfloat16)).astype(jnp.float32)

def true_positions(order, first, count, half):
    rows = first + jnp.arange(count, dtype=jnp.int32)
    blocks = rows // half
    table = blocks[:, None] == jnp.arange(order.shape[0], dtype=jnp.int32)[None, :]
    return lax.optimization_barrier(jnp.sum(jnp.where(table, order[None, :], 0), axis=1)).astype(jnp.int32) * half + rows % half

def norm_forward(state, gain, shift):
    centre = state - lax.optimization_barrier(jnp.mean(state, axis=-1, keepdims=True))
    inverse = lax.rsqrt(lax.optimization_barrier(jnp.mean(centre * centre, axis=-1, keepdims=True)) + EPSILON)
    normed = centre * inverse
    return (normed * gain.astype(jnp.float32) + shift.astype(jnp.float32), normed, inverse)

def norm_backward(grad_out, normed, inverse, gain):
    scaled = grad_out * gain.astype(jnp.float32)
    return inverse * (scaled - lax.optimization_barrier(jnp.mean(scaled, axis=-1, keepdims=True)) - normed * lax.optimization_barrier(jnp.mean(scaled * normed, axis=-1, keepdims=True)))

def attention_forward(query, keys, values, positions):
    blocks = L // TOK_DEV
    scale = HEAD_DIM ** (-0.5)
    key_float = keys.reshape(L, HEADS, HEAD_DIM).astype(jnp.float32)
    value_float = values.reshape(L, HEADS, HEAD_DIM).astype(jnp.float32)
    query_blocks = query.reshape(blocks, TOK_DEV, HEADS, HEAD_DIM)
    pos_blocks = positions.reshape(blocks, TOK_DEV)

    def one_block(args):
        query_part, query_pos = args
        scores = jnp.einsum('qhd,khd->hqk', query_part.astype(jnp.float32), key_float) * scale
        allowed = query_pos[:, None] >= positions[None, :]
        scores = jnp.where(allowed[None], scores, -jnp.inf)
        top = lax.optimization_barrier(jnp.max(scores, axis=2))
        probs = jnp.exp(scores - top[:, :, None])
        total = lax.optimization_barrier(jnp.sum(probs, axis=2))
        weighted = jnp.einsum('hqk,khd->hqd', round_half(probs), value_float) / total[:, :, None]
        return (jnp.transpose(weighted, (1, 0, 2)), top + jnp.log(total))
    mixed, log_total = lax.map(one_block, (query_blocks, pos_blocks))
    return (mixed.reshape(L, D), log_total)

def attention_backward(query, keys, values, positions, log_total, delta, grad_mixed):
    blocks = L // TOK_DEV
    scale = HEAD_DIM ** (-0.5)
    key_float = keys.reshape(L, HEADS, HEAD_DIM).astype(jnp.float32)
    value_float = values.reshape(L, HEADS, HEAD_DIM).astype(jnp.float32)
    query_blocks = query.reshape(blocks, TOK_DEV, HEADS, HEAD_DIM)
    grad_blocks = grad_mixed.reshape(blocks, TOK_DEV, HEADS, HEAD_DIM)
    pos_blocks = positions.reshape(blocks, TOK_DEV)

    def one_block(carry, args):
        grad_keys, grad_values = carry
        query_part, query_pos, lse_part, delta_part, grad_part = args
        query_float = query_part.astype(jnp.float32)
        grad_float = grad_part.astype(jnp.float32)
        scores = jnp.einsum('qhd,khd->hqk', query_float, key_float) * scale
        allowed = query_pos[:, None] >= positions[None, :]
        probs = jnp.where(allowed[None], jnp.exp(scores - lse_part[:, :, None]), 0.0)
        grad_probs = jnp.einsum('qhd,khd->hqk', grad_float, value_float)
        grad_scores = probs * (grad_probs - delta_part[:, :, None])
        probs_round = round_half(probs)
        scores_round = round_half(grad_scores)
        grad_values = grad_values + jnp.einsum('hqk,qhd->khd', probs_round, grad_float)
        grad_keys = grad_keys + jnp.einsum('hqk,qhd->khd', scores_round, query_float) * scale
        grad_query = jnp.einsum('hqk,khd->qhd', scores_round, key_float) * scale
        return ((grad_keys, grad_values), grad_query)
    zero_heads = jnp.zeros((L, HEADS, HEAD_DIM), jnp.float32)
    (grad_keys, grad_values), grad_query = lax.scan(one_block, (zero_heads, zero_heads), (query_blocks, pos_blocks, log_total, delta, grad_blocks))
    return (grad_query.reshape(L, D), grad_keys.reshape(L, D), grad_values.reshape(L, D))

def layer_forward(state, weights, positions):
    attn_gain, attn_shift, w_qkv, query_bias, value_bias, w_out, out_bias, mlp_gain, mlp_shift, w_fc, fc_bias, w_proj, proj_bias = weights
    normed_in, normed_one, inverse_one = norm_forward(state, attn_gain, attn_shift)
    first = normed_in.astype(jnp.bfloat16)
    joint = jnp.dot(first, w_qkv, preferred_element_type=jnp.float32)
    query = (joint[:, :D] + query_bias.astype(jnp.float32)).astype(jnp.bfloat16)
    keys = joint[:, D:2 * D].astype(jnp.bfloat16)
    values = (joint[:, 2 * D:] + value_bias.astype(jnp.float32)).astype(jnp.bfloat16)
    mixed, log_total = attention_forward(query, keys, values, positions)
    mixed_round = mixed.astype(jnp.bfloat16)
    middle = state + jnp.dot(mixed_round, w_out, preferred_element_type=jnp.float32) + out_bias.astype(jnp.float32)
    normed_mid, normed_two, inverse_two = norm_forward(middle, mlp_gain, mlp_shift)
    second = normed_mid.astype(jnp.bfloat16)
    pre = jnp.dot(second, w_fc, preferred_element_type=jnp.float32) + fc_bias.astype(jnp.float32)
    hidden = gelu_value(pre).astype(jnp.bfloat16)
    result = middle + jnp.dot(hidden, w_proj, preferred_element_type=jnp.float32) + proj_bias.astype(jnp.float32)
    keep = (normed_one, inverse_one, first, query, keys, values, mixed, mixed_round, log_total, normed_two, inverse_two, second, pre, hidden)
    return (result, keep)

def layer_backward(grad_state, weights, keep, positions):
    attn_gain, attn_shift, w_qkv, query_bias, value_bias, w_out, out_bias, mlp_gain, mlp_shift, w_fc, fc_bias, w_proj, proj_bias = weights
    normed_one, inverse_one, first, query, keys, values, mixed, mixed_round, log_total, normed_two, inverse_two, second, pre, hidden = keep
    blocks = L // TOK_DEV
    grad_proj_bias = lax.optimization_barrier(jnp.sum(grad_state, axis=0))
    grad_round = grad_state.astype(jnp.bfloat16)
    grad_w_proj = jnp.dot(hidden.T, grad_round, preferred_element_type=jnp.float32)
    grad_pre = jnp.dot(grad_round, w_proj.T, preferred_element_type=jnp.float32) * gelu_slope(pre)
    grad_fc_bias = lax.optimization_barrier(jnp.sum(grad_pre, axis=0))
    grad_pre_round = grad_pre.astype(jnp.bfloat16)
    grad_w_fc = jnp.dot(second.T, grad_pre_round, preferred_element_type=jnp.float32)
    grad_second = jnp.dot(grad_pre_round, w_fc.T, preferred_element_type=jnp.float32)
    grad_mlp_gain = lax.optimization_barrier(jnp.sum(grad_second * normed_two, axis=0))
    grad_mlp_shift = lax.optimization_barrier(jnp.sum(grad_second, axis=0))
    grad_middle = grad_state + norm_backward(grad_second, normed_two, inverse_two, mlp_gain)
    grad_out_bias = lax.optimization_barrier(jnp.sum(grad_middle, axis=0))
    middle_round = grad_middle.astype(jnp.bfloat16)
    grad_w_out = jnp.dot(mixed_round.T, middle_round, preferred_element_type=jnp.float32)
    grad_mixed = jnp.dot(middle_round, w_out.T, preferred_element_type=jnp.float32).astype(jnp.bfloat16)
    delta = lax.optimization_barrier(jnp.sum(grad_mixed.reshape(L, HEADS, HEAD_DIM).astype(jnp.float32) * mixed.reshape(L, HEADS, HEAD_DIM), axis=2))
    delta = jnp.transpose(delta.reshape(blocks, TOK_DEV, HEADS), (0, 2, 1))
    grad_query, grad_keys, grad_values = attention_backward(query, keys, values, positions, log_total, delta, grad_mixed)
    grad_query_bias = lax.optimization_barrier(jnp.sum(grad_query, axis=0))
    grad_value_bias = lax.optimization_barrier(jnp.sum(grad_values, axis=0))
    grad_joint = jnp.concatenate([grad_query, grad_keys, grad_values], axis=1).astype(jnp.bfloat16)
    grad_w_qkv = jnp.dot(first.T, grad_joint, preferred_element_type=jnp.float32)
    grad_first = jnp.dot(grad_joint, w_qkv.T, preferred_element_type=jnp.float32)
    grad_attn_gain = lax.optimization_barrier(jnp.sum(grad_first * normed_one, axis=0))
    grad_attn_shift = lax.optimization_barrier(jnp.sum(grad_first, axis=0))
    grad_in = grad_middle + norm_backward(grad_first, normed_one, inverse_one, attn_gain)
    grads = (grad_attn_gain, grad_attn_shift, grad_w_qkv, grad_query_bias, grad_value_bias, grad_w_out, grad_out_bias, grad_mlp_gain, grad_mlp_shift, grad_w_fc, grad_fc_bias, grad_w_proj, grad_proj_bias)
    return (grad_in, grads)

def reference(tokens, block_order, attn_gain, attn_shift, w_qkv, query_bias, value_bias, w_out, out_bias, mlp_gain, mlp_shift, w_fc, fc_bias, w_proj, proj_bias, cotangent):
    params = (attn_gain, attn_shift, w_qkv, query_bias, value_bias, w_out, out_bias, mlp_gain, mlp_shift, w_fc, fc_bias, w_proj, proj_bias)
    zeros = tuple((jnp.zeros(item.shape, jnp.float32) for item in params))

    def one_sequence(grads, args):
        sequence, order, grad_seq = args
        positions = true_positions(order, 0, L, HALF)
        state = sequence.astype(jnp.float32)
        saved = []
        for layer in range(LAYERS):
            weights = tuple((item[layer] for item in params))
            state, keep = layer_forward(state, weights, positions)
            saved.append(keep)
        result = state.astype(jnp.bfloat16)
        grad_state = grad_seq.astype(jnp.float32)
        per_layer = [None] * LAYERS
        for layer in reversed(range(LAYERS)):
            weights = tuple((item[layer] for item in params))
            grad_state, per_layer[layer] = layer_backward(grad_state, weights, saved[layer], positions)
        stacked = tuple((jnp.stack([per_layer[layer][index] for layer in range(LAYERS)]) for index in range(len(params))))
        return (tuple((left + right for left, right in zip(grads, stacked))), (result, grad_state))
    grads, (outputs, input_grad) = lax.scan(one_sequence, zeros, (tokens, block_order, cotangent))
    return (outputs, input_grad, grads[0], grads[1], grads[2], grads[3], grads[4], grads[5], grads[6], grads[7], grads[8], grads[9], grads[10], grads[11], grads[12])
```

```python
import jax
import jax.numpy as jnp
from jax import lax
from jax.experimental import pallas as pl
from jax.experimental.pallas import tpu as pltpu
from jax.sharding import PartitionSpec as P

D = 768
HEADS = 12
HEAD_DIM = 64


EPSILON = 1e-05
GELU_SCALE = 0.7978845608028654
GELU_CUBIC = 0.044715


def gelu_value(value):
    return 0.5 * value * (1.0 + jnp.tanh(GELU_SCALE * (value + GELU_CUBIC * value * value * value)))


def gelu_slope(value):
    tangent = jnp.tanh(GELU_SCALE * (value + GELU_CUBIC * value * value * value))
    return 0.5 * (1.0 + tangent) + 0.5 * value * (1.0 - tangent * tangent) * GELU_SCALE * (
        1.0 + 3.0 * GELU_CUBIC * value * value
    )


def true_positions(order, first, count, half):
    rows = first + jnp.arange(count, dtype=jnp.int32)
    blocks = rows // half
    table = blocks[:, None] == jnp.arange(order.shape[0], dtype=jnp.int32)[None, :]
    return jnp.sum(jnp.where(table, order[None, :], 0), axis=1) * half + rows % half


def norm_forward(state, gain, shift):
    centre = state - jnp.mean(state, axis=-1, keepdims=True)
    inverse = lax.rsqrt(jnp.mean(centre * centre, axis=-1, keepdims=True) + EPSILON)
    normed = centre * inverse
    return (normed * gain.astype(jnp.float32) + shift.astype(jnp.float32), normed, inverse)


def norm_backward(grad_out, normed, inverse, gain):
    scaled = grad_out * gain.astype(jnp.float32)
    return inverse * (
        scaled
        - jnp.mean(scaled, axis=-1, keepdims=True)
        - normed * jnp.mean(scaled * normed, axis=-1, keepdims=True)
    )


BF = jnp.bfloat16
F32 = jnp.float32
EXT = 128
AXES = ("ctx", "fsdp")


class Grid:
    def __init__(self, mesh):
        ctx, fsdp = mesh.shape["ctx"], mesh.shape["fsdp"]
        self.z = 4
        self.x = ctx // self.z
        self.y = fsdp // 2
        self.n = ctx * fsdp
        assert self.x == self.y and self.x * self.z == ctx

    def here(self):
        c, f = lax.axis_index("ctx"), lax.axis_index("fsdp")
        return c // self.x, c % self.x, f // 2, f % 2

    def index(self, z, x, y, k):
        return ((z % self.z * self.x + x % self.x) * self.y + y % self.y) * 2 + k % 2

    def send(self, value, move):
        pairs = [
            (self.index(z, x, y, k), self.index(*move(z, x, y, k)))
            for z in range(self.z)
            for x in range(self.x)
            for y in range(self.y)
            for k in range(2)
        ]
        return lax.ppermute(value, AXES, pairs)

    def core(self, value):
        return self.send(value, lambda z, x, y, k: (z, x, y, 1 - k))

    def along_z(self, value, step):
        return self.send(value, lambda z, x, y, k: (z + step, x, y, k))

    def along_x(self, value, step):
        return self.send(value, lambda z, x, y, k: (z, x + step, y, k))

    def first(self, value, step):
        return self.send(value, lambda z, x, y, k: (z, x + step, y, k) if k == 0 else (z, x, y + step, k))

    def second(self, value, step):
        return self.send(value, lambda z, x, y, k: (z, x, y + step, k) if k == 0 else (z, x + step, y, k))

    def z_far(self, value):
        return self.send(value, lambda z, x, y, k: (z, x, y, k) if k == 0 else (z + 2, x, y, k))

    def z_near(self, value):
        return self.send(value, lambda z, x, y, k: (z + 1, x, y, k) if k == 0 else (z + 3, x, y, k))


def gather(grid, shard, widths):
    rows, _ = shard.shape
    core = grid.here()[3]
    other = grid.core(shard)
    pair = jnp.where(core == 0, jnp.stack([shard, other]), jnp.stack([other, shard]))
    base = jnp.stack([grid.z_far(pair), grid.z_near(pair)])
    reached = {}
    for i in range(grid.x):
        reached[i, 0] = base if i == 0 else grid.first(base, i)
        for j in range(1, grid.y):
            reached[i, j] = grid.second(reached[i, 0], j)
    own = [reached[i, j] for i in range(grid.x) for j in range(grid.y)]
    parts = own + [grid.core(part) for part in own]
    offsets = [sum(widths[:at]) for at in range(len(widths))]
    X, Y, Z = grid.x, grid.y, grid.z

    def kernel(*refs):
        ins, outs, sem = refs[: len(parts)], refs[len(parts) : -1], refs[-1]
        z, x, y, k = grid.here()
        copies = []
        for at, part in enumerate(ins):
            route = k if at < len(own) else 1 - k
            i, j = (at % len(own)) // Y, (at % len(own)) % Y
            dx = jnp.where(route == 0, i, j)
            dy = jnp.where(route == 0, j, i)
            sx, sy = (x - dx + X) % X, (y - dy + Y) % Y
            for near in range(2):
                sz = (z - near - 2 * route + Z) % Z
                place = (sz * X + sx) * Y + sy
                for out, low, width in zip(outs, offsets, widths):
                    copies.append(
                        pltpu.make_async_copy(
                            part.at[near, :, :, pl.ds(low, width)],
                            out.at[place],
                            sem.at[len(copies)],
                        )
                    )
        for copy in copies:
            copy.start()
        for copy in copies:
            copy.wait()

    whole = pl.pallas_call(
        kernel,
        in_specs=[pl.BlockSpec(memory_space=pl.ANY)] * len(parts),
        out_specs=[pl.BlockSpec(memory_space=pl.ANY)] * len(widths),
        out_shape=[jax.ShapeDtypeStruct((grid.n // 2, 2, rows, width), shard.dtype) for width in widths],
        scratch_shapes=[pltpu.SemaphoreType.DMA((len(parts) * 2 * len(widths),))],
    )(*parts)
    return [item.reshape(grid.n * rows, width) for item, width in zip(whole, widths)]


def scatter(grid, parts):
    n = grid.n
    X, Y, Z = grid.x, grid.y, grid.z
    rows = parts[0].shape[0] // n
    widths = [part.shape[1] for part in parts]
    offsets = [sum(widths[:at]) for at in range(len(widths))]
    blocks = [part.reshape(n // 2, 2, rows, width) for part, width in zip(parts, widths)]

    def kernel(*refs):
        ins, outs, sem = refs[: len(parts)], refs[len(parts) : -1], refs[-1]
        z, x, y, k = grid.here()
        copies = []
        for at, out in enumerate(outs):
            route = k if at == 0 else 1 - k
            for i in range(X):
                for j in range(Y):
                    dx = jnp.where(route == 0, i, j)
                    dy = jnp.where(route == 0, j, i)
                    tx, ty = (x + dx) % X, (y + dy) % Y
                    for near in range(2):
                        tz = (z + near + 2 * route) % Z
                        place = (tz * X + tx) * Y + ty
                        for part, low, width in zip(ins, offsets, widths):
                            copies.append(
                                pltpu.make_async_copy(
                                    part.at[place],
                                    out.at[i, j, near, :, :, pl.ds(low, width)],
                                    sem.at[len(copies)],
                                )
                            )
        for copy in copies:
            copy.start()
        for copy in copies:
            copy.wait()

    shape = jax.ShapeDtypeStruct((X, Y, 2, 2, rows, sum(widths)), BF)
    mine, theirs = pl.pallas_call(
        kernel,
        in_specs=[pl.BlockSpec(memory_space=pl.ANY)] * len(parts),
        out_specs=[pl.BlockSpec(memory_space=pl.ANY)] * 2,
        out_shape=[shape] * 2,
        scratch_shapes=[pltpu.SemaphoreType.DMA((n * len(parts),))],
    )(*blocks)
    came = grid.core(theirs)

    def add(*items):
        total = items[0].astype(F32)
        for item in items[1:]:
            total = total + item.astype(F32)
        return total

    one = [add(mine[i], came[i]) for i in range(X)]
    two = [one[0]] + [grid.first(one[i].astype(BF), i) for i in range(1, X)]
    two = [add(*(item[j] for item in two)) for j in range(Y)]
    three = [two[0]] + [grid.second(two[j].astype(BF), j) for j in range(1, Y)]
    three = add(*three).astype(BF)
    four = add(grid.z_far(three[0]), grid.z_near(three[1]))
    core = grid.here()[3]
    kept = jnp.where(core == 0, four[0], four[1])
    sent = jnp.where(core == 0, four[1], four[0]).astype(BF)
    return kept + grid.core(sent).astype(F32)


def local_step(
    grid,
    tokens,
    block_order,
    attn_gain,
    attn_shift,
    w_qkv,
    query_bias,
    value_bias,
    w_out,
    out_bias,
    mlp_gain,
    mlp_shift,
    w_fc,
    fc_bias,
    w_proj,
    proj_bias,
    cotangent,
):
    count = tokens.shape[1]
    half = count // 2
    scale = HEAD_DIM ** (-0.5)
    order = block_order[0]
    Z, X = grid.z, grid.x
    z, x, _, _ = grid.here()
    group = D // Z
    heads = HEADS // Z

    rows = w_qkv.shape[1]
    small = [attn_gain, attn_shift, query_bias, value_bias, out_bias, mlp_gain, mlp_shift, proj_bias]
    extra = jnp.concatenate([jnp.stack([item[0] for item in small], axis=1), fc_bias.reshape(rows, -1)], axis=1)
    used = extra.shape[1]
    extra = jnp.pad(extra, ((0, 0), (0, EXT - used)))
    w_joint, extra = gather(grid, jnp.concatenate([w_qkv[0], extra], axis=1), [3 * D, EXT])
    w_mix, w_up = gather(grid, jnp.concatenate([w_out[0], w_fc[0]], axis=1), [D, w_fc.shape[2]])
    (w_down,) = gather(grid, w_proj[0], [D])
    extra = extra[:, :used].T
    gain_one, shift_one, bias_query, bias_value, bias_mix, gain_two, shift_two, bias_down = [extra[i] for i in range(8)]
    bias_up = extra[8:].T.reshape(-1)

    def positions(dz, dx):
        owner = (z - dz + Z) % Z * X + (x - dx + X) % X
        return true_positions(order, owner * count, count, half)

    query_pos = jnp.concatenate([positions(dz, 0) for dz in range(Z)])
    key_pos = jnp.concatenate([positions(dz, dx) for dx in range(X) for dz in range(Z)])
    allowed = query_pos[:, None] >= key_pos[None, :]

    def spread(piece):
        doubled = jnp.concatenate([piece, piece], axis=0)
        moved = [lax.dynamic_index_in_dim(doubled, z + dz, 0, keepdims=False) for dz in range(Z)]
        return jnp.stack([moved[0]] + [grid.along_z(moved[dz], dz) for dz in range(1, Z)])

    def collect(piece):
        came = [piece[0]] + [grid.along_z(piece[dz], -dz) for dz in range(1, Z)]
        came = jnp.stack(came + came)
        return lax.dynamic_slice_in_dim(came, (Z - z) % Z, Z, 0)

    state = tokens[0].astype(F32)
    normed_in, normed_one, inverse_one = norm_forward(state, gain_one, shift_one)
    first = normed_in.astype(BF)
    joint = jnp.dot(first, w_joint, preferred_element_type=F32)
    query = (joint[:, :D] + bias_query.astype(F32)).astype(BF)
    keys = joint[:, D : 2 * D].astype(BF)
    values = (joint[:, 2 * D :] + bias_value.astype(F32)).astype(BF)

    def by_group(item):
        return jnp.transpose(item.reshape(count, Z, group), (1, 0, 2))

    packed = spread(jnp.concatenate([by_group(query), by_group(keys), by_group(values)], axis=2))
    packed_keys = packed[:, :, group:]
    all_keys = jnp.concatenate([packed_keys[None]] + [grid.along_x(packed_keys, dx)[None] for dx in range(1, X)])
    q = packed[:, :, :group].reshape(Z * count, heads, HEAD_DIM)
    k = all_keys[..., :group].reshape(X * Z * count, heads, HEAD_DIM)
    v = all_keys[..., group:].reshape(X * Z * count, heads, HEAD_DIM)
    scores = jnp.einsum("qhd,khd->hqk", q, k, preferred_element_type=F32) * scale
    scores = jnp.where(allowed[None], scores, -jnp.inf)
    top = jnp.max(scores, axis=2)
    probs = jnp.exp(scores - top[:, :, None])
    total = jnp.sum(probs, axis=2)
    mixed_local = jnp.einsum("hqk,khd->hqd", probs.astype(BF), v, preferred_element_type=F32) / total[:, :, None]
    log_total = top + jnp.log(total)
    mixed_send = jnp.transpose(mixed_local, (1, 0, 2)).reshape(Z, count, group).astype(BF)
    mixed_round = jnp.transpose(collect(mixed_send), (1, 0, 2)).reshape(count, D)

    middle = state + jnp.dot(mixed_round, w_mix, preferred_element_type=F32) + bias_mix.astype(F32)
    normed_mid, normed_two, inverse_two = norm_forward(middle, gain_two, shift_two)
    second = normed_mid.astype(BF)
    pre = jnp.dot(second, w_up, preferred_element_type=F32) + bias_up.astype(F32)
    hidden = gelu_value(pre).astype(BF)
    result = middle + jnp.dot(hidden, w_down, preferred_element_type=F32) + bias_down.astype(F32)
    block_out = result.astype(BF)[None]

    grad_state = cotangent[0]
    grad_proj_bias = jnp.sum(grad_state, axis=0)
    grad_round = grad_state.astype(BF)
    grad_w_proj = jnp.einsum("tf,td->fd", hidden, grad_round, preferred_element_type=F32)
    shard_proj = scatter(grid, [grad_w_proj.astype(BF)])
    grad_pre = jnp.einsum("td,fd->tf", grad_round, w_down, preferred_element_type=F32) * gelu_slope(pre)
    grad_fc_bias = jnp.sum(grad_pre, axis=0)
    grad_pre_round = grad_pre.astype(BF)
    grad_w_fc = jnp.einsum("td,tf->df", second, grad_pre_round, preferred_element_type=F32)
    grad_second = jnp.einsum("tf,df->td", grad_pre_round, w_up, preferred_element_type=F32)
    grad_mlp_gain = jnp.sum(grad_second * normed_two, axis=0)
    grad_mlp_shift = jnp.sum(grad_second, axis=0)
    grad_middle = grad_state + norm_backward(grad_second, normed_two, inverse_two, gain_two)
    grad_out_bias = jnp.sum(grad_middle, axis=0)
    middle_round = grad_middle.astype(BF)
    grad_w_out = jnp.einsum("tc,td->cd", mixed_round, middle_round, preferred_element_type=F32)
    shard_mid = scatter(grid, [grad_w_out.astype(BF), grad_w_fc.astype(BF)])
    grad_mixed = jnp.einsum("td,cd->tc", middle_round, w_mix, preferred_element_type=F32).astype(BF)

    grad_local = spread(by_group(grad_mixed)).reshape(Z * count, heads, HEAD_DIM)
    delta = jnp.sum(jnp.transpose(grad_local.astype(F32), (1, 0, 2)) * mixed_local, axis=2)
    again = jnp.einsum("qhd,khd->hqk", q, k, preferred_element_type=F32) * scale
    soft = jnp.where(allowed[None], jnp.exp(again - log_total[:, :, None]), 0.0)
    grad_probs = jnp.einsum("qhd,khd->hqk", grad_local, v, preferred_element_type=F32)
    grad_scores = (soft * (grad_probs - delta[:, :, None])).astype(BF)
    grad_v = jnp.einsum("hqk,qhd->khd", soft.astype(BF), grad_local, preferred_element_type=F32)
    grad_k = jnp.einsum("hqk,qhd->khd", grad_scores, q, preferred_element_type=F32) * scale
    grad_q = jnp.einsum("hqk,khd->qhd", grad_scores, k, preferred_element_type=F32) * scale
    pair = jnp.concatenate([grad_k.reshape(X, Z, count, group), grad_v.reshape(X, Z, count, group)], axis=3)
    held = pair[0]
    for dx in range(1, X):
        held = held + grid.along_x(pair[dx].astype(BF), -dx).astype(F32)
    back = jnp.concatenate([grad_q.reshape(Z, count, group).astype(BF), held.astype(BF)], axis=2)
    back = collect(back).reshape(Z, count, 3, group)
    grad_joint = jnp.transpose(back, (1, 2, 0, 3)).reshape(count, 3 * D)
    grad_query_bias = jnp.sum(grad_joint[:, :D].astype(F32), axis=0)
    grad_value_bias = jnp.sum(grad_joint[:, 2 * D :].astype(F32), axis=0)
    grad_w_qkv = jnp.einsum("td,te->de", first, grad_joint, preferred_element_type=F32)
    grad_first = jnp.einsum("te,de->td", grad_joint, w_joint, preferred_element_type=F32)
    grad_attn_gain = jnp.sum(grad_first * normed_one, axis=0)
    grad_attn_shift = jnp.sum(grad_first, axis=0)
    grad_in = grad_middle + norm_backward(grad_first, normed_one, inverse_one, gain_one)

    vectors = [
        grad_attn_gain,
        grad_attn_shift,
        grad_query_bias,
        grad_value_bias,
        grad_out_bias,
        grad_mlp_gain,
        grad_mlp_shift,
        grad_proj_bias,
    ]
    columns = jnp.concatenate([jnp.stack(vectors, axis=1), grad_fc_bias.reshape(D, -1)], axis=1)
    columns = jnp.pad(columns, ((0, 0), (0, EXT - used))).astype(BF)
    shard_first = scatter(grid, [grad_w_qkv.astype(BF), columns])
    shard_qkv, ends = shard_first[:, : 3 * D], shard_first[:, 3 * D :]
    small = [ends[:, i][None] for i in range(8)]
    return (
        block_out,
        grad_in[None],
        small[0],
        small[1],
        shard_qkv[None],
        small[2],
        small[3],
        shard_mid[None, :, :D],
        small[4],
        small[5],
        small[6],
        shard_mid[None, :, D:],
        ends[:, 8:used].reshape(1, -1),
        shard_proj[None],
        small[7],
    )


def solution(mesh):
    grid = Grid(mesh)

    def local(*args):
        return local_step(grid, *args)

    placed = (
        P("fsdp", "ctx", None),
        P("fsdp", None),
        P(None, ("ctx", "fsdp")),
        P(None, ("ctx", "fsdp")),
        P(None, ("ctx", "fsdp"), None),
        P(None, ("ctx", "fsdp")),
        P(None, ("ctx", "fsdp")),
        P(None, ("ctx", "fsdp"), None),
        P(None, ("ctx", "fsdp")),
        P(None, ("ctx", "fsdp")),
        P(None, ("ctx", "fsdp")),
        P(None, ("ctx", "fsdp"), None),
        P(None, ("ctx", "fsdp")),
        P(None, ("ctx", "fsdp"), None),
        P(None, ("ctx", "fsdp")),
        P("fsdp", "ctx", None),
    )
    return jax.shard_map(
        local,
        mesh=mesh,
        in_specs=placed,
        out_specs=(
            P("fsdp", "ctx", None),
            P("fsdp", "ctx", None),
            P(None, ("ctx", "fsdp")),
            P(None, ("ctx", "fsdp")),
            P(None, ("ctx", "fsdp"), None),
            P(None, ("ctx", "fsdp")),
            P(None, ("ctx", "fsdp")),
            P(None, ("ctx", "fsdp"), None),
            P(None, ("ctx", "fsdp")),
            P(None, ("ctx", "fsdp")),
            P(None, ("ctx", "fsdp")),
            P(None, ("ctx", "fsdp"), None),
            P(None, ("ctx", "fsdp")),
            P(None, ("ctx", "fsdp"), None),
            P(None, ("ctx", "fsdp")),
        ),
        check_vma=False,
    )
```

```python
import jax
import jax.numpy as jnp
from jax import lax
from jax.experimental import pallas as pl
from jax.experimental.pallas import tpu as pltpu
from jax.sharding import PartitionSpec as P

D = 768
HEADS = 12
HEAD_DIM = 64


EPSILON = 1e-05
GELU_SCALE = 0.7978845608028654
GELU_CUBIC = 0.044715


def gelu_value(value):
    return 0.5 * value * (1.0 + jnp.tanh(GELU_SCALE * (value + GELU_CUBIC * value * value * value)))


def gelu_slope(value):
    tangent = jnp.tanh(GELU_SCALE * (value + GELU_CUBIC * value * value * value))
    return 0.5 * (1.0 + tangent) + 0.5 * value * (1.0 - tangent * tangent) * GELU_SCALE * (
        1.0 + 3.0 * GELU_CUBIC * value * value
    )


def true_positions(order, first, count, half):
    rows = first + jnp.arange(count, dtype=jnp.int32)
    blocks = rows // half
    table = blocks[:, None] == jnp.arange(order.shape[0], dtype=jnp.int32)[None, :]
    return jnp.sum(jnp.where(table, order[None, :], 0), axis=1) * half + rows % half


def norm_forward(state, gain, shift):
    centre = state - jnp.mean(state, axis=-1, keepdims=True)
    inverse = lax.rsqrt(jnp.mean(centre * centre, axis=-1, keepdims=True) + EPSILON)
    normed = centre * inverse
    return (normed * gain.astype(jnp.float32) + shift.astype(jnp.float32), normed, inverse)


def norm_backward(grad_out, normed, inverse, gain):
    scaled = grad_out * gain.astype(jnp.float32)
    return inverse * (
        scaled
        - jnp.mean(scaled, axis=-1, keepdims=True)
        - normed * jnp.mean(scaled * normed, axis=-1, keepdims=True)
    )


BF = jnp.bfloat16
F32 = jnp.float32
EXT = 128
AXES = ("ctx", "fsdp")


class Grid:
    def __init__(self, mesh):
        ctx, fsdp = mesh.shape["ctx"], mesh.shape["fsdp"]
        self.z = 4
        self.x = ctx // self.z
        self.y = fsdp // 2
        self.n = ctx * fsdp
        assert self.x == self.y and self.x * self.z == ctx

    def here(self):
        c, f = lax.axis_index("ctx"), lax.axis_index("fsdp")
        return c // self.x, c % self.x, f // 2, f % 2

    def index(self, z, x, y, k):
        return ((z % self.z * self.x + x % self.x) * self.y + y % self.y) * 2 + k % 2

    def send(self, value, move):
        pairs = [
            (self.index(z, x, y, k), self.index(*move(z, x, y, k)))
            for z in range(self.z)
            for x in range(self.x)
            for y in range(self.y)
            for k in range(2)
        ]
        return lax.ppermute(value, AXES, pairs)

    def core(self, value):
        return self.send(value, lambda z, x, y, k: (z, x, y, 1 - k))

    def along_z(self, value, step):
        return self.send(value, lambda z, x, y, k: (z + step, x, y, k))

    def along_x(self, value, step):
        return self.send(value, lambda z, x, y, k: (z, x + step, y, k))

    def first(self, value, step):
        return self.send(value, lambda z, x, y, k: (z, x + step, y, k) if k == 0 else (z, x, y + step, k))

    def second(self, value, step):
        return self.send(value, lambda z, x, y, k: (z, x, y + step, k) if k == 0 else (z, x + step, y, k))

    def z_far(self, value):
        return self.send(value, lambda z, x, y, k: (z, x, y, k) if k == 0 else (z + 2, x, y, k))

    def z_near(self, value):
        return self.send(value, lambda z, x, y, k: (z + 1, x, y, k) if k == 0 else (z + 3, x, y, k))


def gather(grid, shard, widths):
    rows, _ = shard.shape
    core = grid.here()[3]
    other = grid.core(shard)
    pair = jnp.where(core == 0, jnp.stack([shard, other]), jnp.stack([other, shard]))
    base = jnp.stack([grid.z_far(pair), grid.z_near(pair)])
    reached = {}
    for i in range(grid.x):
        reached[i, 0] = base if i == 0 else grid.first(base, i)
        for j in range(1, grid.y):
            reached[i, j] = grid.second(reached[i, 0], j)
    own = [reached[i, j] for i in range(grid.x) for j in range(grid.y)]
    parts = own + [grid.core(part) for part in own]
    offsets = [sum(widths[:at]) for at in range(len(widths))]
    X, Y, Z = grid.x, grid.y, grid.z

    def kernel(*refs):
        ins, outs, sem = refs[: len(parts)], refs[len(parts) : -1], refs[-1]
        z, x, y, k = grid.here()
        copies = []
        for at, part in enumerate(ins):
            route = k if at < len(own) else 1 - k
            i, j = (at % len(own)) // Y, (at % len(own)) % Y
            dx = jnp.where(route == 0, i, j)
            dy = jnp.where(route == 0, j, i)
            sx, sy = (x - dx + X) % X, (y - dy + Y) % Y
            for near in range(2):
                sz = (z - near - 2 * route + Z) % Z
                place = (sz * X + sx) * Y + sy
                for out, low, width in zip(outs, offsets, widths):
                    copies.append(
                        pltpu.make_async_copy(
                            part.at[near, :, :, pl.ds(low, width)],
                            out.at[place],
                            sem.at[len(copies)],
                        )
                    )
        for copy in copies:
            copy.start()
        for copy in copies:
            copy.wait()

    whole = pl.pallas_call(
        kernel,
        in_specs=[pl.BlockSpec(memory_space=pl.ANY)] * len(parts),
        out_specs=[pl.BlockSpec(memory_space=pltpu.VMEM)] * len(widths),
        out_shape=[jax.ShapeDtypeStruct((grid.n // 2, 2, rows, width), shard.dtype) for width in widths],
        scratch_shapes=[pltpu.SemaphoreType.DMA((len(parts) * 2 * len(widths),))],
    )(*parts)
    return [item.reshape(grid.n * rows, width) for item, width in zip(whole, widths)]


def scatter(grid, pairs, extra=None):
    n = grid.n
    X, Y, Z = grid.x, grid.y, grid.z
    rows = pairs[0][0].shape[1] // n
    chunk = 2 * Y * rows
    widths = [right.shape[1] for _, right in pairs]
    offsets = [sum(widths[:at]) for at in range(len(widths))]
    lefts = [left.T for left, _ in pairs]
    rights = [right for _, right in pairs]
    tails = [] if extra is None else [extra.reshape(n, rows, extra.shape[1])]
    total = sum(widths) + sum(tail.shape[2] for tail in tails)

    def kernel(*refs):
        left_refs, right_refs = refs[: len(pairs)], refs[len(pairs) : 2 * len(pairs)]
        tail_refs, outs = refs[2 * len(pairs) : -2], refs[-2:]
        z, x, y, k = grid.here()
        for other, out in enumerate(outs):
            route = k if other == 0 else 1 - k
            for near in range(2):
                for dx in range(X):
                    tz, tx = (z + near + 2 * route) % Z, (x + dx) % X
                    base = tz * X + tx
                    spots = []
                    for ty in range(Y):
                        dy = (ty - y + Y) % Y
                        i = jnp.where(route == 0, dx, dy)
                        j = jnp.where(route == 0, dy, dx)
                        spots += [((i * Y + j) * 2 + near) * 2, ((i * Y + j) * 2 + near) * 2 + 1]
                    for left, right, low, width in zip(left_refs, right_refs, offsets, widths):
                        if rows % 8 == 0:
                            part = left[pl.ds(pl.multiple_of(base * chunk, chunk), chunk), :]
                        else:
                            part = left[pl.ds(base * chunk, chunk), :]
                        made = jnp.dot(part, right[...], preferred_element_type=F32)
                        for at, spot in enumerate(spots):
                            out[spot, :, low : low + width] = made[at * rows : (at + 1) * rows].astype(BF)
                    for tail in tail_refs:
                        for at, spot in enumerate(spots):
                            out[spot, :, sum(widths) :] = tail[base * 2 * Y + at]

    shape = jax.ShapeDtypeStruct((X * Y * 4, rows, total), BF)
    vmem = pl.BlockSpec(memory_space=pltpu.VMEM)
    mine, theirs = pl.pallas_call(
        kernel,
        in_specs=[vmem] * (2 * len(pairs) + len(tails)),
        out_specs=[vmem] * 2,
        out_shape=[shape] * 2,
        compiler_params=pltpu.CompilerParams(vmem_limit_bytes=48 * 1024 * 1024),
    )(*lefts, *rights, *tails)
    mine = mine.reshape(X, Y, 2, 2, rows, total)
    theirs = theirs.reshape(X, Y, 2, 2, rows, total)
    came = grid.core(theirs)

    def add(*items):
        total = items[0].astype(F32)
        for item in items[1:]:
            total = total + item.astype(F32)
        return total

    one = [add(mine[i], came[i]) for i in range(X)]
    two = [one[0]] + [grid.first(one[i].astype(BF), i) for i in range(1, X)]
    two = [add(*(item[j] for item in two)) for j in range(Y)]
    three = [two[0]] + [grid.second(two[j].astype(BF), j) for j in range(1, Y)]
    three = add(*three).astype(BF)
    four = add(grid.z_far(three[0]), grid.z_near(three[1]))
    core = grid.here()[3]
    kept = jnp.where(core == 0, four[0], four[1])
    sent = jnp.where(core == 0, four[1], four[0]).astype(BF)
    return kept + grid.core(sent).astype(F32)


def local_step(
    grid,
    tokens,
    block_order,
    attn_gain,
    attn_shift,
    w_qkv,
    query_bias,
    value_bias,
    w_out,
    out_bias,
    mlp_gain,
    mlp_shift,
    w_fc,
    fc_bias,
    w_proj,
    proj_bias,
    cotangent,
):
    count = tokens.shape[1]
    half = count // 2
    scale = HEAD_DIM ** (-0.5)
    order = block_order[0]
    Z, X = grid.z, grid.x
    z, x, _, _ = grid.here()
    group = D // Z
    heads = HEADS // Z

    rows = w_qkv.shape[1]
    small = [attn_gain, attn_shift, query_bias, value_bias, out_bias, mlp_gain, mlp_shift, proj_bias]
    extra = jnp.concatenate([jnp.stack([item[0] for item in small], axis=1), fc_bias.reshape(rows, -1)], axis=1)
    used = extra.shape[1]
    extra = jnp.pad(extra, ((0, 0), (0, EXT - used)))
    w_joint, extra = gather(grid, jnp.concatenate([w_qkv[0], extra], axis=1), [3 * D, EXT])
    w_mix, w_up = gather(grid, jnp.concatenate([w_out[0], w_fc[0]], axis=1), [D, w_fc.shape[2]])
    (w_down,) = gather(grid, w_proj[0], [D])
    extra = extra[:, :used].T
    gain_one, shift_one, bias_query, bias_value, bias_mix, gain_two, shift_two, bias_down = [extra[i] for i in range(8)]
    bias_up = extra[8:].T.reshape(-1)

    def positions(dz, dx):
        owner = (z - dz + Z) % Z * X + (x - dx + X) % X
        return true_positions(order, owner * count, count, half)

    query_pos = jnp.concatenate([positions(dz, 0) for dz in range(Z)])
    key_pos = jnp.concatenate([positions(dz, dx) for dx in range(X) for dz in range(Z)])
    allowed = query_pos[:, None] >= key_pos[None, :]

    def spread(piece):
        doubled = jnp.concatenate([piece, piece], axis=0)
        moved = [lax.dynamic_index_in_dim(doubled, z + dz, 0, keepdims=False) for dz in range(Z)]
        return jnp.stack([moved[0]] + [grid.along_z(moved[dz], dz) for dz in range(1, Z)])

    def collect(piece):
        came = [piece[0]] + [grid.along_z(piece[dz], -dz) for dz in range(1, Z)]
        came = jnp.stack(came + came)
        return lax.dynamic_slice_in_dim(came, (Z - z) % Z, Z, 0)

    state = tokens[0].astype(F32)
    normed_in, normed_one, inverse_one = norm_forward(state, gain_one, shift_one)
    first = normed_in.astype(BF)
    joint = jnp.dot(first, w_joint, preferred_element_type=F32)
    query = (joint[:, :D] + bias_query.astype(F32)).astype(BF)
    keys = joint[:, D : 2 * D].astype(BF)
    values = (joint[:, 2 * D :] + bias_value.astype(F32)).astype(BF)

    def by_group(item):
        return jnp.transpose(item.reshape(count, Z, group), (1, 0, 2))

    packed = spread(jnp.concatenate([by_group(query), by_group(keys), by_group(values)], axis=2))
    packed_keys = packed[:, :, group:]
    all_keys = jnp.concatenate([packed_keys[None]] + [grid.along_x(packed_keys, dx)[None] for dx in range(1, X)])
    q = packed[:, :, :group].reshape(Z * count, heads, HEAD_DIM)
    k = all_keys[..., :group].reshape(X * Z * count, heads, HEAD_DIM)
    v = all_keys[..., group:].reshape(X * Z * count, heads, HEAD_DIM)
    scores = jnp.einsum("qhd,khd->hqk", q, k, preferred_element_type=F32) * scale
    scores = jnp.where(allowed[None], scores, -jnp.inf)
    top = jnp.max(scores, axis=2)
    probs = jnp.exp(scores - top[:, :, None])
    total = jnp.sum(probs, axis=2)
    mixed_local = jnp.einsum("hqk,khd->hqd", probs.astype(BF), v, preferred_element_type=F32) / total[:, :, None]
    log_total = top + jnp.log(total)
    mixed_send = jnp.transpose(mixed_local, (1, 0, 2)).reshape(Z, count, group).astype(BF)
    mixed_round = jnp.transpose(collect(mixed_send), (1, 0, 2)).reshape(count, D)

    middle = state + jnp.dot(mixed_round, w_mix, preferred_element_type=F32) + bias_mix.astype(F32)
    normed_mid, normed_two, inverse_two = norm_forward(middle, gain_two, shift_two)
    second = normed_mid.astype(BF)
    pre = jnp.dot(second, w_up, preferred_element_type=F32) + bias_up.astype(F32)
    hidden = gelu_value(pre).astype(BF)
    result = middle + jnp.dot(hidden, w_down, preferred_element_type=F32) + bias_down.astype(F32)
    block_out = result.astype(BF)[None]

    grad_state = cotangent[0]
    grad_proj_bias = jnp.sum(grad_state, axis=0)
    grad_round = grad_state.astype(BF)
    shard_proj = scatter(grid, [(hidden, grad_round)])
    grad_pre = jnp.einsum("td,fd->tf", grad_round, w_down, preferred_element_type=F32) * gelu_slope(pre)
    grad_fc_bias = jnp.sum(grad_pre, axis=0)
    grad_pre_round = grad_pre.astype(BF)
    grad_second = jnp.einsum("tf,df->td", grad_pre_round, w_up, preferred_element_type=F32)
    grad_mlp_gain = jnp.sum(grad_second * normed_two, axis=0)
    grad_mlp_shift = jnp.sum(grad_second, axis=0)
    grad_middle = grad_state + norm_backward(grad_second, normed_two, inverse_two, gain_two)
    grad_out_bias = jnp.sum(grad_middle, axis=0)
    middle_round = grad_middle.astype(BF)
    shard_mid = scatter(grid, [(mixed_round, middle_round), (second, grad_pre_round)])
    grad_mixed = jnp.einsum("td,cd->tc", middle_round, w_mix, preferred_element_type=F32).astype(BF)

    grad_local = spread(by_group(grad_mixed)).reshape(Z * count, heads, HEAD_DIM)
    delta = jnp.sum(jnp.transpose(grad_local.astype(F32), (1, 0, 2)) * mixed_local, axis=2)
    again = jnp.einsum("qhd,khd->hqk", q, k, preferred_element_type=F32) * scale
    soft = jnp.where(allowed[None], jnp.exp(again - log_total[:, :, None]), 0.0)
    grad_probs = jnp.einsum("qhd,khd->hqk", grad_local, v, preferred_element_type=F32)
    grad_scores = (soft * (grad_probs - delta[:, :, None])).astype(BF)
    grad_v = jnp.einsum("hqk,qhd->khd", soft.astype(BF), grad_local, preferred_element_type=F32)
    grad_k = jnp.einsum("hqk,qhd->khd", grad_scores, q, preferred_element_type=F32) * scale
    grad_q = jnp.einsum("hqk,khd->qhd", grad_scores, k, preferred_element_type=F32) * scale
    pair = jnp.concatenate([grad_k.reshape(X, Z, count, group), grad_v.reshape(X, Z, count, group)], axis=3)
    held = pair[0]
    for dx in range(1, X):
        held = held + grid.along_x(pair[dx].astype(BF), -dx).astype(F32)
    back = jnp.concatenate([grad_q.reshape(Z, count, group).astype(BF), held.astype(BF)], axis=2)
    back = collect(back).reshape(Z, count, 3, group)
    grad_joint = jnp.transpose(back, (1, 2, 0, 3)).reshape(count, 3 * D)
    grad_query_bias = jnp.sum(grad_joint[:, :D].astype(F32), axis=0)
    grad_value_bias = jnp.sum(grad_joint[:, 2 * D :].astype(F32), axis=0)
    grad_first = jnp.einsum("te,de->td", grad_joint, w_joint, preferred_element_type=F32)
    grad_attn_gain = jnp.sum(grad_first * normed_one, axis=0)
    grad_attn_shift = jnp.sum(grad_first, axis=0)
    grad_in = grad_middle + norm_backward(grad_first, normed_one, inverse_one, gain_one)

    vectors = [
        grad_attn_gain,
        grad_attn_shift,
        grad_query_bias,
        grad_value_bias,
        grad_out_bias,
        grad_mlp_gain,
        grad_mlp_shift,
        grad_proj_bias,
    ]
    columns = jnp.concatenate([jnp.stack(vectors, axis=1), grad_fc_bias.reshape(D, -1)], axis=1)
    columns = jnp.pad(columns, ((0, 0), (0, EXT - used))).astype(BF)
    shard_first = scatter(grid, [(first, grad_joint)], columns)
    shard_qkv, ends = shard_first[:, : 3 * D], shard_first[:, 3 * D :]
    small = [ends[:, i][None] for i in range(8)]
    return (
        block_out,
        grad_in[None],
        small[0],
        small[1],
        shard_qkv[None],
        small[2],
        small[3],
        shard_mid[None, :, :D],
        small[4],
        small[5],
        small[6],
        shard_mid[None, :, D:],
        ends[:, 8:used].reshape(1, -1),
        shard_proj[None],
        small[7],
    )


def solution(mesh):
    grid = Grid(mesh)

    def local(*args):
        return local_step(grid, *args)

    placed = (
        P("fsdp", "ctx", None),
        P("fsdp", None),
        P(None, ("ctx", "fsdp")),
        P(None, ("ctx", "fsdp")),
        P(None, ("ctx", "fsdp"), None),
        P(None, ("ctx", "fsdp")),
        P(None, ("ctx", "fsdp")),
        P(None, ("ctx", "fsdp"), None),
        P(None, ("ctx", "fsdp")),
        P(None, ("ctx", "fsdp")),
        P(None, ("ctx", "fsdp")),
        P(None, ("ctx", "fsdp"), None),
        P(None, ("ctx", "fsdp")),
        P(None, ("ctx", "fsdp"), None),
        P(None, ("ctx", "fsdp")),
        P("fsdp", "ctx", None),
    )
    return jax.shard_map(
        local,
        mesh=mesh,
        in_specs=placed,
        out_specs=(
            P("fsdp", "ctx", None),
            P("fsdp", "ctx", None),
            P(None, ("ctx", "fsdp")),
            P(None, ("ctx", "fsdp")),
            P(None, ("ctx", "fsdp"), None),
            P(None, ("ctx", "fsdp")),
            P(None, ("ctx", "fsdp")),
            P(None, ("ctx", "fsdp"), None),
            P(None, ("ctx", "fsdp")),
            P(None, ("ctx", "fsdp")),
            P(None, ("ctx", "fsdp")),
            P(None, ("ctx", "fsdp"), None),
            P(None, ("ctx", "fsdp")),
            P(None, ("ctx", "fsdp"), None),
            P(None, ("ctx", "fsdp")),
        ),
        check_vma=False,
    )
```

```python
import jax
import jax.numpy as jnp
from jax import lax
from jax.experimental import pallas as pl
from jax.experimental.pallas import tpu as pltpu
from jax.sharding import PartitionSpec as P


D = 768
HEADS = 12
HEAD_DIM = 64


EPSILON = 1e-05
GELU_SCALE = 0.7978845608028654
GELU_CUBIC = 0.044715


def gelu_value(value):
    return 0.5 * value * (1.0 + jnp.tanh(GELU_SCALE * (value + GELU_CUBIC * value * value * value)))


def gelu_slope(value):
    tangent = jnp.tanh(GELU_SCALE * (value + GELU_CUBIC * value * value * value))
    return 0.5 * (1.0 + tangent) + 0.5 * value * (1.0 - tangent * tangent) * GELU_SCALE * (
        1.0 + 3.0 * GELU_CUBIC * value * value
    )


def true_positions(order, first, count, half):
    rows = first + jnp.arange(count, dtype=jnp.int32)
    blocks = rows // half
    table = blocks[:, None] == jnp.arange(order.shape[0], dtype=jnp.int32)[None, :]
    return jnp.sum(jnp.where(table, order[None, :], 0), axis=1) * half + rows % half


def norm_forward(state, gain, shift):
    centre = state - jnp.mean(state, axis=-1, keepdims=True)
    inverse = lax.rsqrt(jnp.mean(centre * centre, axis=-1, keepdims=True) + EPSILON)
    normed = centre * inverse
    return (normed * gain.astype(jnp.float32) + shift.astype(jnp.float32), normed, inverse)


def norm_backward(grad_out, normed, inverse, gain):
    scaled = grad_out * gain.astype(jnp.float32)
    return inverse * (
        scaled
        - jnp.mean(scaled, axis=-1, keepdims=True)
        - normed * jnp.mean(scaled * normed, axis=-1, keepdims=True)
    )


BF = jnp.bfloat16
F32 = jnp.float32
EXT = 128
AXES = ("ctx", "fsdp")


class Grid:
    def __init__(self, mesh):
        ctx, fsdp = mesh.shape["ctx"], mesh.shape["fsdp"]
        self.z = 4
        self.x = ctx // self.z
        self.y = fsdp // 2
        self.n = ctx * fsdp
        assert self.x == self.y and self.x * self.z == ctx

    def here(self):
        c, f = lax.axis_index("ctx"), lax.axis_index("fsdp")
        return c // self.x, c % self.x, f // 2, f % 2

    def index(self, z, x, y, k):
        return ((z % self.z * self.x + x % self.x) * self.y + y % self.y) * 2 + k % 2

    def send(self, value, move):
        pairs = [
            (self.index(z, x, y, k), self.index(*move(z, x, y, k)))
            for z in range(self.z)
            for x in range(self.x)
            for y in range(self.y)
            for k in range(2)
        ]
        return lax.ppermute(value, AXES, pairs)

    def core(self, value):
        return self.send(value, lambda z, x, y, k: (z, x, y, 1 - k))

    def along_z(self, value, step):
        return self.send(value, lambda z, x, y, k: (z + step, x, y, k))

    def along_x(self, value, step):
        return self.send(value, lambda z, x, y, k: (z, x + step, y, k))

    def first(self, value, step):
        return self.send(value, lambda z, x, y, k: (z, x + step, y, k) if k == 0 else (z, x, y + step, k))

    def second(self, value, step):
        return self.send(value, lambda z, x, y, k: (z, x, y + step, k) if k == 0 else (z, x + step, y, k))

    def z_far(self, value):
        return self.send(value, lambda z, x, y, k: (z, x, y, k) if k == 0 else (z + 2, x, y, k))

    def z_near(self, value):
        return self.send(value, lambda z, x, y, k: (z + 1, x, y, k) if k == 0 else (z + 3, x, y, k))


def gather(grid, shard, widths):
    rows, _ = shard.shape
    core = grid.here()[3]
    other = grid.core(shard)
    pair = jnp.where(core == 0, jnp.stack([shard, other]), jnp.stack([other, shard]))
    base = jnp.stack([grid.z_far(pair), grid.z_near(pair)])
    reached = {}
    for i in range(grid.x):
        reached[i, 0] = base if i == 0 else grid.first(base, i)
        for j in range(1, grid.y):
            reached[i, j] = grid.second(reached[i, 0], j)
    own = [reached[i, j] for i in range(grid.x) for j in range(grid.y)]
    parts = own + [grid.core(part) for part in own]
    offsets = [sum(widths[:at]) for at in range(len(widths))]
    X, Y, Z = grid.x, grid.y, grid.z

    def kernel(*refs):
        ins, outs, sem = refs[: len(parts)], refs[len(parts) : -1], refs[-1]
        z, x, y, k = grid.here()
        copies = []
        for at, part in enumerate(ins):
            route = k if at < len(own) else 1 - k
            i, j = (at % len(own)) // Y, (at % len(own)) % Y
            dx = jnp.where(route == 0, i, j)
            dy = jnp.where(route == 0, j, i)
            sx, sy = (x - dx + X) % X, (y - dy + Y) % Y
            for near in range(2):
                sz = (z - near - 2 * route + Z) % Z
                place = (sz * X + sx) * Y + sy
                for out, low, width in zip(outs, offsets, widths):
                    copies.append(
                        pltpu.make_async_copy(
                            part.at[near, :, :, pl.ds(low, width)],
                            out.at[place],
                            sem.at[len(copies)],
                        )
                    )
        for copy in copies:
            copy.start()
        for copy in copies:
            copy.wait()

    whole = pl.pallas_call(
        kernel,
        in_specs=[pl.BlockSpec(memory_space=pl.ANY)] * len(parts),
        out_specs=[pl.BlockSpec(memory_space=pltpu.VMEM)] * len(widths),
        out_shape=[jax.ShapeDtypeStruct((grid.n // 2, 2, rows, width), shard.dtype) for width in widths],
        scratch_shapes=[pltpu.SemaphoreType.DMA((len(parts) * 2 * len(widths),))],
    )(*parts)
    return [item.reshape(grid.n * rows, width) for item, width in zip(whole, widths)]


def scatter(grid, pairs, extra=None):
    n = grid.n
    X, Y, Z = grid.x, grid.y, grid.z
    rows = pairs[0][0].shape[1] // n
    chunk = 2 * Y * rows
    widths = [right.shape[1] for _, right in pairs]
    offsets = [sum(widths[:at]) for at in range(len(widths))]
    lefts = [left.T for left, _ in pairs]
    rights = [right for _, right in pairs]
    tails = [] if extra is None else [extra.reshape(n, rows, extra.shape[1])]
    total = sum(widths) + sum(tail.shape[2] for tail in tails)

    def kernel(*refs):
        left_refs, right_refs = refs[: len(pairs)], refs[len(pairs) : 2 * len(pairs)]
        tail_refs, outs = refs[2 * len(pairs) : -2], refs[-2:]
        z, x, y, k = grid.here()
        for other, out in enumerate(outs):
            route = k if other == 0 else 1 - k
            for near in range(2):
                for dx in range(X):
                    tz, tx = (z + near + 2 * route) % Z, (x + dx) % X
                    base = tz * X + tx
                    spots = []
                    for ty in range(Y):
                        dy = (ty - y + Y) % Y
                        i = jnp.where(route == 0, dx, dy)
                        j = jnp.where(route == 0, dy, dx)
                        spots += [((i * Y + j) * 2 + near) * 2, ((i * Y + j) * 2 + near) * 2 + 1]
                    for left, right, low, width in zip(left_refs, right_refs, offsets, widths):
                        if rows % 8 == 0:
                            part = left[pl.ds(pl.multiple_of(base * chunk, chunk), chunk), :]
                        else:
                            part = left[pl.ds(base * chunk, chunk), :]
                        made = jnp.dot(part, right[...], preferred_element_type=F32)
                        for at, spot in enumerate(spots):
                            out[spot, :, low : low + width] = made[at * rows : (at + 1) * rows].astype(BF)
                    for tail in tail_refs:
                        for at, spot in enumerate(spots):
                            out[spot, :, sum(widths) :] = tail[base * 2 * Y + at]

    shape = jax.ShapeDtypeStruct((X * Y * 4, rows, total), BF)
    vmem = pl.BlockSpec(memory_space=pltpu.VMEM)
    mine, theirs = pl.pallas_call(
        kernel,
        in_specs=[vmem] * (2 * len(pairs) + len(tails)),
        out_specs=[vmem] * 2,
        out_shape=[shape] * 2,
        compiler_params=pltpu.CompilerParams(vmem_limit_bytes=48 * 1024 * 1024),
    )(*lefts, *rights, *tails)
    mine = mine.reshape(X, Y, 2, 2, rows, total)
    theirs = theirs.reshape(X, Y, 2, 2, rows, total)
    came = grid.core(theirs)

    def add(*items):
        total = items[0].astype(F32)
        for item in items[1:]:
            total = total + item.astype(F32)
        return total

    one = [add(mine[i], came[i]) for i in range(X)]
    two = [one[0]] + [grid.first(one[i].astype(BF), i) for i in range(1, X)]
    two = [add(*(item[j] for item in two)) for j in range(Y)]
    three = [two[0]] + [grid.second(two[j].astype(BF), j) for j in range(1, Y)]
    three = add(*three).astype(BF)
    four = add(grid.z_far(three[0]), grid.z_near(three[1]))
    core = grid.here()[3]
    kept = jnp.where(core == 0, four[0], four[1])
    sent = jnp.where(core == 0, four[1], four[0]).astype(BF)
    return kept + grid.core(sent).astype(F32)


def product(left, right, dims):
    return lax.dot_general(left, right, (dims, ((), ())), preferred_element_type=F32)


def attend(packed, all_keys, query_pos, key_pos, heads, step):
    count = packed.shape[0]
    group = heads * HEAD_DIM
    scale = HEAD_DIM ** (-0.5)

    def kernel(packed_ref, keys_ref, row_ref, col_ref, mixed_ref, lse_ref):
        for head in range(heads):
            low = head * HEAD_DIM
            k = keys_ref[:, low : low + HEAD_DIM]
            v = keys_ref[:, group + low : group + low + HEAD_DIM]
            for at in range(0, count, step):
                rows = slice(at, at + step)
                q = packed_ref[rows, low : low + HEAD_DIM]
                allowed = row_ref[rows] >= col_ref[...]
                scores = jnp.where(allowed, product(q, k, ((1,), (1,))) * scale, -jnp.inf)
                top = jnp.max(scores, axis=1, keepdims=True)
                probs = jnp.exp(scores - top)
                total = jnp.sum(probs, axis=1, keepdims=True)
                mixed_ref[rows, low : low + HEAD_DIM] = product(probs.astype(BF), v, ((1,), (0,))) / total
                lse_ref[rows, head : head + 1] = top + jnp.log(total)

    vmem = pl.BlockSpec(memory_space=pltpu.VMEM)
    return pl.pallas_call(
        kernel,
        in_specs=[vmem] * 4,
        out_specs=[vmem] * 2,
        out_shape=[jax.ShapeDtypeStruct((count, group), F32), jax.ShapeDtypeStruct((count, heads), F32)],
        compiler_params=pltpu.CompilerParams(vmem_limit_bytes=48 * 1024 * 1024),
    )(packed, all_keys, query_pos[:, None], key_pos[None])


def attend_back(packed, all_keys, query_pos, key_pos, mixed, lse, grad, heads, step, far):
    count, size = packed.shape[0], all_keys.shape[0]
    group = heads * HEAD_DIM
    scale = HEAD_DIM ** (-0.5)
    own = size // far

    def kernel(packed_ref, keys_ref, row_ref, col_ref, mixed_ref, lse_ref, grad_ref, dq_ref, own_ref, far_ref):
        for head in range(heads):
            low = head * HEAD_DIM
            cols = slice(low, low + HEAD_DIM)
            k = keys_ref[:, cols]
            v = keys_ref[:, group + low : group + low + HEAD_DIM]
            dk = jnp.zeros((size, HEAD_DIM), F32)
            dv = jnp.zeros((size, HEAD_DIM), F32)
            for at in range(0, count, step):
                rows = slice(at, at + step)
                q = packed_ref[rows, cols]
                g = grad_ref[rows, cols]
                delta = jnp.sum(g.astype(F32) * mixed_ref[rows, cols], axis=1, keepdims=True)
                allowed = row_ref[rows] >= col_ref[...]
                scores = product(q, k, ((1,), (1,))) * scale
                soft = jnp.where(allowed, jnp.exp(scores - lse_ref[rows, head : head + 1]), 0.0)
                inner = product(g, v, ((1,), (1,)))
                slope = (soft * (inner - delta)).astype(BF)
                dq_ref[rows, cols] = (product(slope, k, ((1,), (0,))) * scale).astype(BF)
                dk = dk + product(slope, q, ((0,), (0,)))
                dv = dv + product(soft.astype(BF), g, ((0,), (0,)))
            dk = dk * scale
            own_ref[:, cols] = dk[:own]
            own_ref[:, group + low : group + low + HEAD_DIM] = dv[:own]
            for at in range(far - 1):
                piece = slice((at + 1) * own, (at + 2) * own)
                far_ref[at, :, cols] = dk[piece].astype(BF)
                far_ref[at, :, group + low : group + low + HEAD_DIM] = dv[piece].astype(BF)

    vmem = pl.BlockSpec(memory_space=pltpu.VMEM)
    return pl.pallas_call(
        kernel,
        in_specs=[vmem] * 7,
        out_specs=[vmem] * 3,
        out_shape=[
            jax.ShapeDtypeStruct((count, group), BF),
            jax.ShapeDtypeStruct((own, 2 * group), F32),
            jax.ShapeDtypeStruct((far - 1, own, 2 * group), BF),
        ],
        compiler_params=pltpu.CompilerParams(vmem_limit_bytes=48 * 1024 * 1024),
    )(packed, all_keys, query_pos[:, None], key_pos[None], mixed, lse, grad)


def local_step(
    grid,
    tokens,
    block_order,
    attn_gain,
    attn_shift,
    w_qkv,
    query_bias,
    value_bias,
    w_out,
    out_bias,
    mlp_gain,
    mlp_shift,
    w_fc,
    fc_bias,
    w_proj,
    proj_bias,
    cotangent,
):
    count = tokens.shape[1]
    half = count // 2
    order = block_order[0]
    Z, X = grid.z, grid.x
    z, x, _, _ = grid.here()
    group = D // Z
    heads = HEADS // Z

    rows = w_qkv.shape[1]
    small = [attn_gain, attn_shift, query_bias, value_bias, out_bias, mlp_gain, mlp_shift, proj_bias]
    extra = jnp.concatenate([jnp.stack([item[0] for item in small], axis=1), fc_bias.reshape(rows, -1)], axis=1)
    used = extra.shape[1]
    extra = jnp.pad(extra, ((0, 0), (0, EXT - used)))
    w_joint, extra = gather(grid, jnp.concatenate([w_qkv[0], extra], axis=1), [3 * D, EXT])
    w_mix, w_up = gather(grid, jnp.concatenate([w_out[0], w_fc[0]], axis=1), [D, w_fc.shape[2]])
    (w_down,) = gather(grid, w_proj[0], [D])
    extra = extra[:, :used].T
    gain_one, shift_one, bias_query, bias_value, bias_mix, gain_two, shift_two, bias_down = [extra[i] for i in range(8)]
    bias_up = extra[8:].T.reshape(-1)

    def positions(dz, dx):
        owner = (z - dz + Z) % Z * X + (x - dx + X) % X
        return true_positions(order, owner * count, count, half)

    query_pos = jnp.concatenate([positions(dz, 0) for dz in range(Z)])
    key_pos = jnp.concatenate([positions(dz, dx) for dx in range(X) for dz in range(Z)])

    def spread(piece):
        doubled = jnp.concatenate([piece, piece], axis=0)
        moved = [lax.dynamic_index_in_dim(doubled, z + dz, 0, keepdims=False) for dz in range(Z)]
        return jnp.stack([moved[0]] + [grid.along_z(moved[dz], dz) for dz in range(1, Z)])

    def collect(piece):
        came = [piece[0]] + [grid.along_z(piece[dz], -dz) for dz in range(1, Z)]
        came = jnp.stack(came + came)
        return lax.dynamic_slice_in_dim(came, (Z - z) % Z, Z, 0)

    state = tokens[0].astype(F32)
    normed_in, normed_one, inverse_one = norm_forward(state, gain_one, shift_one)
    first = normed_in.astype(BF)
    joint = jnp.dot(first, w_joint, preferred_element_type=F32)
    query = (joint[:, :D] + bias_query.astype(F32)).astype(BF)
    keys = joint[:, D : 2 * D].astype(BF)
    values = (joint[:, 2 * D :] + bias_value.astype(F32)).astype(BF)

    def by_group(item):
        return jnp.transpose(item.reshape(count, Z, group), (1, 0, 2))

    packed = spread(jnp.concatenate([by_group(query), by_group(keys), by_group(values)], axis=2))
    packed_keys = packed[:, :, group:]
    all_keys = jnp.concatenate([packed_keys[None]] + [grid.along_x(packed_keys, dx)[None] for dx in range(1, X)])
    all_keys = all_keys.reshape(X * Z * count, 2 * group)
    packed = packed.reshape(Z * count, 3 * group)
    mixed_local, log_total = attend(packed, all_keys, query_pos, key_pos, heads, count)
    mixed_send = mixed_local.reshape(Z, count, group).astype(BF)
    mixed_round = jnp.transpose(collect(mixed_send), (1, 0, 2)).reshape(count, D)

    middle = state + jnp.dot(mixed_round, w_mix, preferred_element_type=F32) + bias_mix.astype(F32)
    normed_mid, normed_two, inverse_two = norm_forward(middle, gain_two, shift_two)
    second = normed_mid.astype(BF)
    pre = jnp.dot(second, w_up, preferred_element_type=F32) + bias_up.astype(F32)
    hidden = gelu_value(pre).astype(BF)
    result = middle + jnp.dot(hidden, w_down, preferred_element_type=F32) + bias_down.astype(F32)
    block_out = result.astype(BF)[None]

    grad_state = cotangent[0]
    grad_proj_bias = jnp.sum(grad_state, axis=0)
    grad_round = grad_state.astype(BF)
    shard_proj = scatter(grid, [(hidden, grad_round)])
    grad_pre = jnp.einsum("td,fd->tf", grad_round, w_down, preferred_element_type=F32) * gelu_slope(pre)
    grad_fc_bias = jnp.sum(grad_pre, axis=0)
    grad_pre_round = grad_pre.astype(BF)
    grad_second = jnp.einsum("tf,df->td", grad_pre_round, w_up, preferred_element_type=F32)
    grad_mlp_gain = jnp.sum(grad_second * normed_two, axis=0)
    grad_mlp_shift = jnp.sum(grad_second, axis=0)
    grad_middle = grad_state + norm_backward(grad_second, normed_two, inverse_two, gain_two)
    grad_out_bias = jnp.sum(grad_middle, axis=0)
    middle_round = grad_middle.astype(BF)
    shard_mid = scatter(grid, [(mixed_round, middle_round), (second, grad_pre_round)])
    grad_mixed = jnp.einsum("td,cd->tc", middle_round, w_mix, preferred_element_type=F32).astype(BF)

    grad_local = spread(by_group(grad_mixed)).reshape(Z * count, group)
    grad_q, grad_own, grad_far = attend_back(
        packed, all_keys, query_pos, key_pos, mixed_local, log_total, grad_local, heads, count, X
    )
    held = grad_own
    for dx in range(1, X):
        held = held + grid.along_x(grad_far[dx - 1], -dx).astype(F32)
    back = jnp.concatenate([grad_q, held.astype(BF)], axis=1).reshape(Z, count, 3 * group)
    back = collect(back).reshape(Z, count, 3, group)
    grad_joint = jnp.transpose(back, (1, 2, 0, 3)).reshape(count, 3 * D)
    grad_query_bias = jnp.sum(grad_joint[:, :D].astype(F32), axis=0)
    grad_value_bias = jnp.sum(grad_joint[:, 2 * D :].astype(F32), axis=0)
    grad_first = jnp.einsum("te,de->td", grad_joint, w_joint, preferred_element_type=F32)
    grad_attn_gain = jnp.sum(grad_first * normed_one, axis=0)
    grad_attn_shift = jnp.sum(grad_first, axis=0)
    grad_in = grad_middle + norm_backward(grad_first, normed_one, inverse_one, gain_one)

    vectors = [
        grad_attn_gain,
        grad_attn_shift,
        grad_query_bias,
        grad_value_bias,
        grad_out_bias,
        grad_mlp_gain,
        grad_mlp_shift,
        grad_proj_bias,
    ]
    columns = jnp.concatenate([jnp.stack(vectors, axis=1), grad_fc_bias.reshape(D, -1)], axis=1)
    columns = jnp.pad(columns, ((0, 0), (0, EXT - used))).astype(BF)
    shard_first = scatter(grid, [(first, grad_joint)], columns)
    shard_qkv, ends = shard_first[:, : 3 * D], shard_first[:, 3 * D :]
    small = [ends[:, i][None] for i in range(8)]
    return (
        block_out,
        grad_in[None],
        small[0],
        small[1],
        shard_qkv[None],
        small[2],
        small[3],
        shard_mid[None, :, :D],
        small[4],
        small[5],
        small[6],
        shard_mid[None, :, D:],
        ends[:, 8:used].reshape(1, -1),
        shard_proj[None],
        small[7],
    )


def solution(mesh):
    grid = Grid(mesh)

    def local(*args):
        return local_step(grid, *args)

    placed = (
        P("fsdp", "ctx", None),
        P("fsdp", None),
        P(None, ("ctx", "fsdp")),
        P(None, ("ctx", "fsdp")),
        P(None, ("ctx", "fsdp"), None),
        P(None, ("ctx", "fsdp")),
        P(None, ("ctx", "fsdp")),
        P(None, ("ctx", "fsdp"), None),
        P(None, ("ctx", "fsdp")),
        P(None, ("ctx", "fsdp")),
        P(None, ("ctx", "fsdp")),
        P(None, ("ctx", "fsdp"), None),
        P(None, ("ctx", "fsdp")),
        P(None, ("ctx", "fsdp"), None),
        P(None, ("ctx", "fsdp")),
        P("fsdp", "ctx", None),
    )
    return jax.shard_map(
        local,
        mesh=mesh,
        in_specs=placed,
        out_specs=(
            P("fsdp", "ctx", None),
            P("fsdp", "ctx", None),
            P(None, ("ctx", "fsdp")),
            P(None, ("ctx", "fsdp")),
            P(None, ("ctx", "fsdp"), None),
            P(None, ("ctx", "fsdp")),
            P(None, ("ctx", "fsdp")),
            P(None, ("ctx", "fsdp"), None),
            P(None, ("ctx", "fsdp")),
            P(None, ("ctx", "fsdp")),
            P(None, ("ctx", "fsdp")),
            P(None, ("ctx", "fsdp"), None),
            P(None, ("ctx", "fsdp")),
            P(None, ("ctx", "fsdp"), None),
            P(None, ("ctx", "fsdp")),
        ),
        check_vma=False,
    )
```

```python
import functools

import jax
import jax.numpy as jnp
from jax import lax
from jax.experimental import pallas as pl
from jax.experimental.pallas import tpu as pltpu
from jax.sharding import PartitionSpec as P


D = 768
HEADS = 12
HEAD_DIM = 64


EPSILON = 1e-05
GELU_SCALE = 0.7978845608028654
GELU_CUBIC = 0.044715


def gelu_value(value):
    return 0.5 * value * (1.0 + jnp.tanh(GELU_SCALE * (value + GELU_CUBIC * value * value * value)))


def gelu_slope(value):
    tangent = jnp.tanh(GELU_SCALE * (value + GELU_CUBIC * value * value * value))
    return 0.5 * (1.0 + tangent) + 0.5 * value * (1.0 - tangent * tangent) * GELU_SCALE * (
        1.0 + 3.0 * GELU_CUBIC * value * value
    )


def true_positions(order, first, count, half):
    rows = first + jnp.arange(count, dtype=jnp.int32)
    blocks = rows // half
    table = blocks[:, None] == jnp.arange(order.shape[0], dtype=jnp.int32)[None, :]
    return jnp.sum(jnp.where(table, order[None, :], 0), axis=1) * half + rows % half


def norm_forward(state, gain, shift):
    centre = state - jnp.mean(state, axis=-1, keepdims=True)
    inverse = lax.rsqrt(jnp.mean(centre * centre, axis=-1, keepdims=True) + EPSILON)
    normed = centre * inverse
    return (normed * gain.astype(jnp.float32) + shift.astype(jnp.float32), normed, inverse)


def norm_backward(grad_out, normed, inverse, gain):
    scaled = grad_out * gain.astype(jnp.float32)
    return inverse * (
        scaled
        - jnp.mean(scaled, axis=-1, keepdims=True)
        - normed * jnp.mean(scaled * normed, axis=-1, keepdims=True)
    )


BF = jnp.bfloat16
F32 = jnp.float32
EXT = 128
AXES = ("ctx", "fsdp")


class Grid:
    def __init__(self, mesh):
        ctx, fsdp = mesh.shape["ctx"], mesh.shape["fsdp"]
        self.z = 4
        self.x = ctx // self.z
        self.y = fsdp // 2
        self.n = ctx * fsdp
        assert self.x == self.y and self.x * self.z == ctx

    def here(self):
        c, f = lax.axis_index("ctx"), lax.axis_index("fsdp")
        return c // self.x, c % self.x, f // 2, f % 2

    def index(self, z, x, y, k):
        return ((z % self.z * self.x + x % self.x) * self.y + y % self.y) * 2 + k % 2

    def send(self, value, move):
        pairs = [
            (self.index(z, x, y, k), self.index(*move(z, x, y, k)))
            for z in range(self.z)
            for x in range(self.x)
            for y in range(self.y)
            for k in range(2)
        ]
        return lax.ppermute(value, AXES, pairs)

    def core(self, value):
        return self.send(value, lambda z, x, y, k: (z, x, y, 1 - k))

    def along_z(self, value, step):
        return self.send(value, lambda z, x, y, k: (z + step, x, y, k))

    def along_x(self, value, step):
        return self.send(value, lambda z, x, y, k: (z, x + step, y, k))

    def first(self, value, step):
        return self.send(value, lambda z, x, y, k: (z, x + step, y, k) if k == 0 else (z, x, y + step, k))

    def second(self, value, step):
        return self.send(value, lambda z, x, y, k: (z, x, y + step, k) if k == 0 else (z, x + step, y, k))

    def z_far(self, value):
        return self.send(value, lambda z, x, y, k: (z, x, y, k) if k == 0 else (z + 2, x, y, k))

    def z_near(self, value):
        return self.send(value, lambda z, x, y, k: (z + 1, x, y, k) if k == 0 else (z + 3, x, y, k))


def gather(grid, shard, widths):
    rows, _ = shard.shape
    core = grid.here()[3]
    other = grid.core(shard)
    pair = jnp.where(core == 0, jnp.stack([shard, other]), jnp.stack([other, shard]))
    base = jnp.stack([grid.z_far(pair), grid.z_near(pair)])
    reached = {}
    for i in range(grid.x):
        reached[i, 0] = base if i == 0 else grid.first(base, i)
        for j in range(1, grid.y):
            reached[i, j] = grid.second(reached[i, 0], j)
    own = [reached[i, j] for i in range(grid.x) for j in range(grid.y)]
    parts = own + [grid.core(part) for part in own]
    offsets = [sum(widths[:at]) for at in range(len(widths))]
    X, Y, Z = grid.x, grid.y, grid.z

    def kernel(*refs):
        ins, outs, sem = refs[: len(parts)], refs[len(parts) : -1], refs[-1]
        z, x, y, k = grid.here()
        copies = []
        for at, part in enumerate(ins):
            route = k if at < len(own) else 1 - k
            i, j = (at % len(own)) // Y, (at % len(own)) % Y
            dx = jnp.where(route == 0, i, j)
            dy = jnp.where(route == 0, j, i)
            sx, sy = (x - dx + X) % X, (y - dy + Y) % Y
            for near in range(2):
                sz = (z - near - 2 * route + Z) % Z
                place = (sz * X + sx) * Y + sy
                for out, low, width in zip(outs, offsets, widths):
                    copies.append(
                        pltpu.make_async_copy(
                            part.at[near, :, :, pl.ds(low, width)],
                            out.at[place],
                            sem.at[len(copies)],
                        )
                    )
        for copy in copies:
            copy.start()
        for copy in copies:
            copy.wait()

    whole = pl.pallas_call(
        kernel,
        in_specs=[pl.BlockSpec(memory_space=pl.ANY)] * len(parts),
        out_specs=[pl.BlockSpec(memory_space=pltpu.VMEM)] * len(widths),
        out_shape=[jax.ShapeDtypeStruct((grid.n // 2, 2, rows, width), shard.dtype) for width in widths],
        scratch_shapes=[pltpu.SemaphoreType.DMA((len(parts) * 2 * len(widths),))],
    )(*parts)
    return [item.reshape(grid.n * rows, width) for item, width in zip(whole, widths)]


def add_parts(terms, lead, blocks):
    rows, width = terms[0][0].shape[-2:]

    def kernel(*refs):
        total = refs[0][...].astype(F32)
        for ref in refs[1:-1]:
            total = total + ref[...].astype(F32)
        refs[-1][...] = total.astype(BF)

    return pl.pallas_call(
        kernel,
        grid=(blocks,),
        in_specs=[pl.BlockSpec((None, lead, rows, width), where) for _, where in terms],
        out_specs=pl.BlockSpec((None, lead, rows, width), lambda g: (g, 0, 0, 0)),
        out_shape=jax.ShapeDtypeStruct((blocks, lead, rows, width), BF),
        compiler_params=pltpu.CompilerParams(vmem_limit_bytes=48 * 1024 * 1024),
    )(*[array for array, _ in terms])


def scatter(grid, pairs, extra=None):
    n = grid.n
    X, Y, Z = grid.x, grid.y, grid.z
    rows = pairs[0][0].shape[1] // n
    chunk = 2 * Y * rows
    widths = [right.shape[1] for _, right in pairs]
    offsets = [sum(widths[:at]) for at in range(len(widths))]
    lefts = [left for left, _ in pairs]
    rights = [right for _, right in pairs]
    tails = [] if extra is None else [extra.reshape(n, rows, extra.shape[1])]
    total = sum(widths) + sum(tail.shape[2] for tail in tails)
    inputs = 2 * len(pairs) + len(tails)

    def kernel(*refs):
        left_refs, right_refs, tail_refs = refs[: len(pairs)], refs[len(pairs) : 2 * len(pairs)], refs[2 * len(pairs) : inputs]
        outs, turned = refs[inputs : inputs + 2 * X], refs[inputs + 2 * X :]
        z, x, y, k = grid.here()
        for left, turn in zip(left_refs, turned):
            turn[...] = left[...].T
        for other in range(2):
            route = k if other == 0 else 1 - k
            for near in range(2):
                for dx in range(X):
                    tz, tx = (z + near + 2 * route) % Z, (x + dx) % X
                    base = tz * X + tx
                    made = []
                    for left, right in zip(turned, right_refs):
                        if rows % 8 == 0:
                            part = left[pl.ds(pl.multiple_of(base * chunk, chunk), chunk), :]
                        else:
                            part = left[pl.ds(base * chunk, chunk), :]
                        made.append(product(part, right[...], ((1,), (0,))))

                    def store(out, ty, spot):
                        for core in range(2):
                            at = 2 * ty + core
                            for value, low, width in zip(made, offsets, widths):
                                out[spot, 2 * near + core, :, low : low + width] = value[at * rows : (at + 1) * rows].astype(BF)
                            for tail in tail_refs:
                                out[spot, 2 * near + core, :, sum(widths) :] = tail[base * 2 * Y + at]

                    for ty in range(Y):
                        dy = (ty - y + Y) % Y
                        i = jnp.where(route == 0, dx, dy)
                        j = jnp.where(route == 0, dy, dx)
                        for at in range(X):
                            pl.when(i == at)(functools.partial(store, outs[other * X + at], ty, j))

    shape = jax.ShapeDtypeStruct((Y, 4, rows, total), BF)
    vmem = pl.BlockSpec(memory_space=pltpu.VMEM)
    made = pl.pallas_call(
        kernel,
        in_specs=[vmem] * inputs,
        out_specs=[vmem] * (2 * X),
        out_shape=[shape] * (2 * X),
        scratch_shapes=[pltpu.VMEM((left.shape[1], left.shape[0]), BF) for left in lefts],
        compiler_params=pltpu.CompilerParams(vmem_limit_bytes=48 * 1024 * 1024),
    )(*lefts, *rights, *tails)
    mine, theirs = made[:X], made[X:]
    came = [None] * X
    for i in list(range(1, X)) + [0]:
        came[i] = grid.core(theirs[i])
    got = []
    for i in range(1, X):
        one = add_parts([(item, lambda g: (g, 0, 0, 0)) for item in (mine[i], came[i])], 4, Y)
        got.append(grid.first(one, i))

    def pick(j):
        return lambda g: (j, g, 0, 0)

    held = [mine[0], came[0]] + got
    final = [(item, 0) for item in held]
    for j in range(1, Y):
        two = add_parts([(item, pick(j)) for item in held], 2, 2).reshape(1, 4, rows, total)
        final.append((grid.second(two, j), 0))
    half = [add_parts([(item, lambda g, near=near: (0, near, 0, 0)) for item, _ in final], 2, 1)[0] for near in range(2)]
    four = grid.z_far(half[0]).astype(F32) + grid.z_near(half[1]).astype(F32)
    core = grid.here()[3]
    kept = jnp.where(core == 0, four[0], four[1])
    sent = jnp.where(core == 0, four[1], four[0]).astype(BF)
    return kept + grid.core(sent).astype(F32)


def product(left, right, dims):
    return lax.dot_general(left, right, (dims, ((), ())), preferred_element_type=F32)


def attend(packed, all_keys, query_pos, key_pos, heads, step):
    count = packed.shape[0]
    group = heads * HEAD_DIM
    scale = HEAD_DIM ** (-0.5)

    def kernel(packed_ref, keys_ref, row_ref, col_ref, mixed_ref, lse_ref):
        for head in range(heads):
            low = head * HEAD_DIM
            k = keys_ref[:, low : low + HEAD_DIM]
            v = keys_ref[:, group + low : group + low + HEAD_DIM]
            for at in range(0, count, step):
                rows = slice(at, at + step)
                q = packed_ref[rows, low : low + HEAD_DIM]
                allowed = row_ref[rows] >= col_ref[...]
                scores = jnp.where(allowed, product(q, k, ((1,), (1,))) * scale, -jnp.inf)
                top = jnp.max(scores, axis=1, keepdims=True)
                probs = jnp.exp(scores - top)
                total = jnp.sum(probs, axis=1, keepdims=True)
                mixed_ref[rows, low : low + HEAD_DIM] = product(probs.astype(BF), v, ((1,), (0,))) / total
                lse_ref[rows, head : head + 1] = top + jnp.log(total)

    vmem = pl.BlockSpec(memory_space=pltpu.VMEM)
    return pl.pallas_call(
        kernel,
        in_specs=[vmem] * 4,
        out_specs=[vmem] * 2,
        out_shape=[jax.ShapeDtypeStruct((count, group), F32), jax.ShapeDtypeStruct((count, heads), F32)],
        compiler_params=pltpu.CompilerParams(vmem_limit_bytes=48 * 1024 * 1024),
    )(packed, all_keys, query_pos[:, None], key_pos[None])


def attend_back(packed, all_keys, query_pos, key_pos, mixed, lse, grad, heads, step, far):
    count, size = packed.shape[0], all_keys.shape[0]
    group = heads * HEAD_DIM
    scale = HEAD_DIM ** (-0.5)
    own = size // far

    def kernel(packed_ref, keys_ref, row_ref, col_ref, mixed_ref, lse_ref, grad_ref, dq_ref, own_ref, far_ref):
        for head in range(heads):
            low = head * HEAD_DIM
            cols = slice(low, low + HEAD_DIM)
            k = keys_ref[:, cols]
            v = keys_ref[:, group + low : group + low + HEAD_DIM]
            dk = jnp.zeros((size, HEAD_DIM), F32)
            dv = jnp.zeros((size, HEAD_DIM), F32)
            for at in range(0, count, step):
                rows = slice(at, at + step)
                q = packed_ref[rows, cols]
                g = grad_ref[rows, cols]
                delta = jnp.sum(g.astype(F32) * mixed_ref[rows, cols], axis=1, keepdims=True)
                allowed = row_ref[rows] >= col_ref[...]
                scores = product(q, k, ((1,), (1,))) * scale
                soft = jnp.where(allowed, jnp.exp(scores - lse_ref[rows, head : head + 1]), 0.0)
                inner = product(g, v, ((1,), (1,)))
                slope = (soft * (inner - delta)).astype(BF)
                dq_ref[rows, cols] = (product(slope, k, ((1,), (0,))) * scale).astype(BF)
                dk = dk + product(slope, q, ((0,), (0,)))
                dv = dv + product(soft.astype(BF), g, ((0,), (0,)))
            dk = dk * scale
            own_ref[:, cols] = dk[:own]
            own_ref[:, group + low : group + low + HEAD_DIM] = dv[:own]
            for at in range(far - 1):
                piece = slice((at + 1) * own, (at + 2) * own)
                far_ref[at, :, cols] = dk[piece].astype(BF)
                far_ref[at, :, group + low : group + low + HEAD_DIM] = dv[piece].astype(BF)

    vmem = pl.BlockSpec(memory_space=pltpu.VMEM)
    return pl.pallas_call(
        kernel,
        in_specs=[vmem] * 7,
        out_specs=[vmem] * 3,
        out_shape=[
            jax.ShapeDtypeStruct((count, group), BF),
            jax.ShapeDtypeStruct((own, 2 * group), F32),
            jax.ShapeDtypeStruct((far - 1, own, 2 * group), BF),
        ],
        compiler_params=pltpu.CompilerParams(vmem_limit_bytes=48 * 1024 * 1024),
    )(packed, all_keys, query_pos[:, None], key_pos[None], mixed, lse, grad)


def local_step(
    grid,
    tokens,
    block_order,
    attn_gain,
    attn_shift,
    w_qkv,
    query_bias,
    value_bias,
    w_out,
    out_bias,
    mlp_gain,
    mlp_shift,
    w_fc,
    fc_bias,
    w_proj,
    proj_bias,
    cotangent,
):
    count = tokens.shape[1]
    half = count // 2
    order = block_order[0]
    Z, X = grid.z, grid.x
    z, x, _, _ = grid.here()
    group = D // Z
    heads = HEADS // Z

    rows = w_qkv.shape[1]
    small = [attn_gain, attn_shift, query_bias, value_bias, out_bias, mlp_gain, mlp_shift, proj_bias]
    spare = fc_bias.reshape(-1, rows)
    used = 8 + spare.shape[0]
    lines = jnp.concatenate(small + [spare, jnp.zeros((EXT - used, rows), BF)], axis=0)
    eye = jnp.eye(rows, dtype=BF)
    extra = product(eye, lines, ((1,), (1,))).astype(BF)
    w_joint, extra = gather(grid, jnp.concatenate([w_qkv[0], extra], axis=1), [3 * D, EXT])
    w_mix, w_up = gather(grid, jnp.concatenate([w_out[0], w_fc[0]], axis=1), [D, w_fc.shape[2]])
    (w_down,) = gather(grid, w_proj[0], [D])
    extra = extra[:, :used].T
    gain_one, shift_one, bias_query, bias_value, bias_mix, gain_two, shift_two, bias_down = [extra[i] for i in range(8)]
    bias_up = jnp.transpose(extra[8:].reshape(used - 8, grid.n, rows), (1, 0, 2)).reshape(-1)

    def positions(dz, dx):
        owner = (z - dz + Z) % Z * X + (x - dx + X) % X
        return true_positions(order, owner * count, count, half)

    query_pos = jnp.concatenate([positions(dz, 0) for dz in range(Z)])
    key_pos = jnp.concatenate([positions(dz, dx) for dx in range(X) for dz in range(Z)])

    def spread(piece):
        doubled = jnp.concatenate([piece, piece], axis=0)
        moved = [lax.dynamic_index_in_dim(doubled, z + dz, 0, keepdims=False) for dz in range(Z)]
        return jnp.stack([moved[0]] + [grid.along_z(moved[dz], dz) for dz in range(1, Z)])

    def collect(piece):
        came = [piece[0]] + [grid.along_z(piece[dz], -dz) for dz in range(1, Z)]
        came = jnp.stack(came + came)
        return lax.dynamic_slice_in_dim(came, (Z - z) % Z, Z, 0)

    state = tokens[0].astype(F32)
    normed_in, normed_one, inverse_one = norm_forward(state, gain_one, shift_one)
    first = normed_in.astype(BF)
    joint = jnp.dot(first, w_joint, preferred_element_type=F32)
    query = (joint[:, :D] + bias_query.astype(F32)).astype(BF)
    keys = joint[:, D : 2 * D].astype(BF)
    values = (joint[:, 2 * D :] + bias_value.astype(F32)).astype(BF)

    def by_group(item):
        return jnp.transpose(item.reshape(count, Z, group), (1, 0, 2))

    packed = spread(jnp.concatenate([by_group(query), by_group(keys), by_group(values)], axis=2))
    packed_keys = packed[:, :, group:]
    all_keys = jnp.concatenate([packed_keys[None]] + [grid.along_x(packed_keys, dx)[None] for dx in range(1, X)])
    all_keys = all_keys.reshape(X * Z * count, 2 * group)
    packed = packed.reshape(Z * count, 3 * group)
    mixed_local, log_total = attend(packed, all_keys, query_pos, key_pos, heads, count)
    mixed_send = mixed_local.reshape(Z, count, group).astype(BF)
    mixed_round = jnp.transpose(collect(mixed_send), (1, 0, 2)).reshape(count, D)

    middle = state + jnp.dot(mixed_round, w_mix, preferred_element_type=F32) + bias_mix.astype(F32)
    normed_mid, normed_two, inverse_two = norm_forward(middle, gain_two, shift_two)
    second = normed_mid.astype(BF)
    pre = jnp.dot(second, w_up, preferred_element_type=F32) + bias_up.astype(F32)
    hidden = gelu_value(pre).astype(BF)
    result = middle + jnp.dot(hidden, w_down, preferred_element_type=F32) + bias_down.astype(F32)
    block_out = result.astype(BF)[None]

    grad_state = cotangent[0]
    grad_proj_bias = jnp.sum(grad_state, axis=0)
    grad_round = grad_state.astype(BF)
    shard_proj = scatter(grid, [(hidden, grad_round)])
    grad_pre = jnp.einsum("td,fd->tf", grad_round, w_down, preferred_element_type=F32) * gelu_slope(pre)
    grad_fc_bias = jnp.sum(grad_pre, axis=0)
    grad_pre_round = grad_pre.astype(BF)
    grad_second = jnp.einsum("tf,df->td", grad_pre_round, w_up, preferred_element_type=F32)
    grad_mlp_gain = jnp.sum(grad_second * normed_two, axis=0)
    grad_mlp_shift = jnp.sum(grad_second, axis=0)
    grad_middle = grad_state + norm_backward(grad_second, normed_two, inverse_two, gain_two)
    grad_out_bias = jnp.sum(grad_middle, axis=0)
    middle_round = grad_middle.astype(BF)
    shard_mid = scatter(grid, [(mixed_round, middle_round), (second, grad_pre_round)])
    grad_mixed = jnp.einsum("td,cd->tc", middle_round, w_mix, preferred_element_type=F32).astype(BF)

    grad_local = spread(by_group(grad_mixed)).reshape(Z * count, group)
    grad_q, grad_own, grad_far = attend_back(
        packed, all_keys, query_pos, key_pos, mixed_local, log_total, grad_local, heads, count, X
    )
    held = grad_own
    for dx in range(1, X):
        held = held + grid.along_x(grad_far[dx - 1], -dx).astype(F32)
    back = jnp.concatenate([grad_q, held.astype(BF)], axis=1).reshape(Z, count, 3 * group)
    back = collect(back).reshape(Z, count, 3, group)
    grad_joint = jnp.transpose(back, (1, 2, 0, 3)).reshape(count, 3 * D)
    grad_query_bias = jnp.sum(grad_joint[:, :D].astype(F32), axis=0)
    grad_value_bias = jnp.sum(grad_joint[:, 2 * D :].astype(F32), axis=0)
    grad_first = jnp.einsum("te,de->td", grad_joint, w_joint, preferred_element_type=F32)
    grad_attn_gain = jnp.sum(grad_first * normed_one, axis=0)
    grad_attn_shift = jnp.sum(grad_first, axis=0)
    grad_in = grad_middle + norm_backward(grad_first, normed_one, inverse_one, gain_one)

    vectors = [
        grad_attn_gain,
        grad_attn_shift,
        grad_query_bias,
        grad_value_bias,
        grad_out_bias,
        grad_mlp_gain,
        grad_mlp_shift,
        grad_proj_bias,
    ]
    columns = jnp.concatenate([jnp.stack(vectors, axis=1), jnp.transpose(grad_fc_bias.reshape(grid.n, used - 8, rows), (0, 2, 1)).reshape(D, -1)], axis=1)
    columns = jnp.pad(columns, ((0, 0), (0, EXT - used))).astype(BF)
    shard_first = scatter(grid, [(first, grad_joint)], columns)
    shard_qkv, ends = shard_first[:, : 3 * D], shard_first[:, 3 * D :]
    small = [ends[:, i][None] for i in range(8)]
    return (
        block_out,
        grad_in[None],
        small[0],
        small[1],
        shard_qkv[None],
        small[2],
        small[3],
        shard_mid[None, :, :D],
        small[4],
        small[5],
        small[6],
        shard_mid[None, :, D:],
        ends[:, 8:used].T.reshape(1, -1),
        shard_proj[None],
        small[7],
    )


def solution(mesh):
    grid = Grid(mesh)

    def local(*args):
        return local_step(grid, *args)

    placed = (
        P("fsdp", "ctx", None),
        P("fsdp", None),
        P(None, ("ctx", "fsdp")),
        P(None, ("ctx", "fsdp")),
        P(None, ("ctx", "fsdp"), None),
        P(None, ("ctx", "fsdp")),
        P(None, ("ctx", "fsdp")),
        P(None, ("ctx", "fsdp"), None),
        P(None, ("ctx", "fsdp")),
        P(None, ("ctx", "fsdp")),
        P(None, ("ctx", "fsdp")),
        P(None, ("ctx", "fsdp"), None),
        P(None, ("ctx", "fsdp")),
        P(None, ("ctx", "fsdp"), None),
        P(None, ("ctx", "fsdp")),
        P("fsdp", "ctx", None),
    )
    return jax.shard_map(
        local,
        mesh=mesh,
        in_specs=placed,
        out_specs=(
            P("fsdp", "ctx", None),
            P("fsdp", "ctx", None),
            P(None, ("ctx", "fsdp")),
            P(None, ("ctx", "fsdp")),
            P(None, ("ctx", "fsdp"), None),
            P(None, ("ctx", "fsdp")),
            P(None, ("ctx", "fsdp")),
            P(None, ("ctx", "fsdp"), None),
            P(None, ("ctx", "fsdp")),
            P(None, ("ctx", "fsdp")),
            P(None, ("ctx", "fsdp")),
            P(None, ("ctx", "fsdp"), None),
            P(None, ("ctx", "fsdp")),
            P(None, ("ctx", "fsdp"), None),
            P(None, ("ctx", "fsdp")),
        ),
        check_vma=False,
    )
```

```python
import functools

import jax
import jax.numpy as jnp
from jax import lax
from jax.experimental import pallas as pl
from jax.experimental.pallas import tpu as pltpu
from jax.sharding import PartitionSpec as P


D = 768
HEADS = 12
HEAD_DIM = 64


EPSILON = 1e-05
GELU_SCALE = 0.7978845608028654
GELU_CUBIC = 0.044715


def gelu_value(value):
    return 0.5 * value * (1.0 + jnp.tanh(GELU_SCALE * (value + GELU_CUBIC * value * value * value)))


def gelu_slope(value):
    tangent = jnp.tanh(GELU_SCALE * (value + GELU_CUBIC * value * value * value))
    return 0.5 * (1.0 + tangent) + 0.5 * value * (1.0 - tangent * tangent) * GELU_SCALE * (
        1.0 + 3.0 * GELU_CUBIC * value * value
    )


def true_positions(order, first, count, half):
    rows = first + jnp.arange(count, dtype=jnp.int32)
    blocks = rows // half
    table = blocks[:, None] == jnp.arange(order.shape[0], dtype=jnp.int32)[None, :]
    return jnp.sum(jnp.where(table, order[None, :], 0), axis=1) * half + rows % half


def norm_forward(state, gain, shift):
    centre = state - jnp.mean(state, axis=-1, keepdims=True)
    inverse = lax.rsqrt(jnp.mean(centre * centre, axis=-1, keepdims=True) + EPSILON)
    normed = centre * inverse
    return (normed * gain.astype(jnp.float32) + shift.astype(jnp.float32), normed, inverse)


def norm_backward(grad_out, normed, inverse, gain):
    scaled = grad_out * gain.astype(jnp.float32)
    return inverse * (
        scaled
        - jnp.mean(scaled, axis=-1, keepdims=True)
        - normed * jnp.mean(scaled * normed, axis=-1, keepdims=True)
    )


BF = jnp.bfloat16
F32 = jnp.float32
EXT = 128
AXES = ("ctx", "fsdp")


class Grid:
    def __init__(self, mesh):
        ctx, fsdp = mesh.shape["ctx"], mesh.shape["fsdp"]
        self.z = 4
        self.x = ctx // self.z
        self.y = fsdp // 2
        self.n = ctx * fsdp
        assert self.x == self.y and self.x * self.z == ctx

    def here(self):
        c, f = lax.axis_index("ctx"), lax.axis_index("fsdp")
        return c // self.x, c % self.x, f // 2, f % 2

    def index(self, z, x, y, k):
        return ((z % self.z * self.x + x % self.x) * self.y + y % self.y) * 2 + k % 2

    def send(self, value, move):
        pairs = [
            (self.index(z, x, y, k), self.index(*move(z, x, y, k)))
            for z in range(self.z)
            for x in range(self.x)
            for y in range(self.y)
            for k in range(2)
        ]
        return lax.ppermute(value, AXES, pairs)

    def core(self, value):
        return self.send(value, lambda z, x, y, k: (z, x, y, 1 - k))

    def along_z(self, value, step):
        return self.send(value, lambda z, x, y, k: (z + step, x, y, k))

    def along_x(self, value, step):
        return self.send(value, lambda z, x, y, k: (z, x + step, y, k))

    def first(self, value, step):
        return self.send(value, lambda z, x, y, k: (z, x + step, y, k) if k == 0 else (z, x, y + step, k))

    def second(self, value, step):
        return self.send(value, lambda z, x, y, k: (z, x, y + step, k) if k == 0 else (z, x + step, y, k))

    def z_far(self, value):
        return self.send(value, lambda z, x, y, k: (z, x, y, k) if k == 0 else (z + 1, x, y, k))

    def z_near(self, value):
        return self.send(value, lambda z, x, y, k: (z + 2, x, y, k) if k == 0 else (z + 3, x, y, k))


def gather(grid, shard, widths):
    rows, _ = shard.shape
    core = grid.here()[3]
    other = grid.core(shard)
    pair = jnp.where(core == 0, jnp.stack([shard, other]), jnp.stack([other, shard]))
    base = jnp.stack([grid.z_far(pair), grid.z_near(pair)])
    reached = {}
    for i in range(grid.x):
        reached[i, 0] = base if i == 0 else grid.first(base, i)
        for j in range(1, grid.y):
            reached[i, j] = grid.second(reached[i, 0], j)
    own = [reached[i, j] for i in range(grid.x) for j in range(grid.y)]
    parts = own + [grid.core(part) for part in own]
    offsets = [sum(widths[:at]) for at in range(len(widths))]
    X, Y, Z = grid.x, grid.y, grid.z

    def kernel(*refs):
        ins, outs, sem = refs[: len(parts)], refs[len(parts) : -1], refs[-1]
        z, x, y, k = grid.here()
        copies = []
        for at, part in enumerate(ins):
            route = k if at < len(own) else 1 - k
            i, j = (at % len(own)) // Y, (at % len(own)) % Y
            dx = jnp.where(route == 0, i, j)
            dy = jnp.where(route == 0, j, i)
            sx, sy = (x - dx + X) % X, (y - dy + Y) % Y
            for near in range(2):
                sz = (z - 2 * near - route + Z) % Z
                place = (sz * X + sx) * Y + sy
                for out, low, width in zip(outs, offsets, widths):
                    copies.append(
                        pltpu.make_async_copy(
                            part.at[near, :, :, pl.ds(low, width)],
                            out.at[place],
                            sem.at[len(copies)],
                        )
                    )
        for copy in copies:
            copy.start()
        for copy in copies:
            copy.wait()

    whole = pl.pallas_call(
        kernel,
        in_specs=[pl.BlockSpec(memory_space=pl.ANY)] * len(parts),
        out_specs=[pl.BlockSpec(memory_space=pltpu.VMEM)] * len(widths),
        out_shape=[jax.ShapeDtypeStruct((grid.n // 2, 2, rows, width), shard.dtype) for width in widths],
        scratch_shapes=[pltpu.SemaphoreType.DMA((len(parts) * 2 * len(widths),))],
        compiler_params=pltpu.CompilerParams(vmem_limit_bytes=16 * 1024 * 1024),
    )(*parts)
    return [item.reshape(grid.n * rows, width) for item, width in zip(whole, widths)]


def add_parts(terms, lead, blocks):
    rows, width = terms[0][0].shape[-2:]

    def kernel(*refs):
        total = refs[0][...].astype(F32)
        for ref in refs[1:-1]:
            total = total + ref[...].astype(F32)
        refs[-1][...] = total.astype(BF)

    return pl.pallas_call(
        kernel,
        grid=(blocks,),
        in_specs=[pl.BlockSpec((None, lead, rows, width), where) for _, where in terms],
        out_specs=pl.BlockSpec((None, lead, rows, width), lambda g: (g, 0, 0, 0)),
        out_shape=jax.ShapeDtypeStruct((blocks, lead, rows, width), BF),
        compiler_params=pltpu.CompilerParams(vmem_limit_bytes=24 * 1024 * 1024),
    )(*[array for array, _ in terms])


def scatter(grid, pairs, extra=()):
    n = grid.n
    X, Y, Z = grid.x, grid.y, grid.z
    rows = pairs[0][0].shape[1] // n
    chunk = 2 * Y * rows
    widths = [right.shape[1] for _, right in pairs]
    offsets = [sum(widths[:at]) for at in range(len(widths))]
    lefts = [left for left, _ in pairs]
    rights = [right for _, right in pairs]
    total = sum(widths) + (EXT if extra else 0)
    inputs = 2 * len(pairs) + len(extra)

    def kernel(*refs):
        left_refs, right_refs, line_refs = refs[: len(pairs)], refs[len(pairs) : 2 * len(pairs)], refs[2 * len(pairs) : inputs]
        outs, turned = refs[inputs : inputs + 2 * X], refs[inputs + 2 * X :]
        z, x, y, k = grid.here()
        for left, turn in zip(left_refs, turned):
            turn[...] = left[...].T
        if line_refs:
            lines, tail = turned[len(pairs) :]
            lines[...] = jnp.zeros(lines.shape, F32)
            at = 0
            for line in line_refs:
                lines[at : at + line.shape[0], :] = line[...]
                at += line.shape[0]
            tail[...] = lines[...].T
        for other in range(2):
            route = k if other == 0 else 1 - k

            def step(at, carry):
                near, dx = at // X, at % X
                tz, tx = (z + 2 * near + route) % Z, (x + dx) % X
                low_row = (tz * X + tx) * chunk
                if rows % 8 == 0:
                    low_row = pl.multiple_of(low_row, chunk)
                made = [
                    product(left[pl.ds(low_row, chunk), :], right[...], ((1,), (0,)))
                    for left, right in zip(turned, right_refs)
                ]
                ends = [tail[pl.ds(low_row, chunk), :]] if line_refs else []

                def store(out, ty, spot):
                    for core in range(2):
                        at = 2 * ty + core
                        span = slice(at * rows, (at + 1) * rows)
                        for value, low, width in zip(made, offsets, widths):
                            out[spot, 2 * near + core, :, low : low + width] = value[span].astype(BF)
                        for value in ends:
                            out[spot, 2 * near + core, :, sum(widths) :] = value[span].astype(BF)

                for ty in range(Y):
                    dy = (ty - y + Y) % Y
                    i = jnp.where(route == 0, dx, dy)
                    j = jnp.where(route == 0, dy, dx)
                    for at in range(X):
                        pl.when(i == at)(functools.partial(store, outs[other * X + at], ty, j))
                return carry

            lax.fori_loop(0, 2 * X, step, 0)

    shape = jax.ShapeDtypeStruct((Y, 4, rows, total), BF)
    vmem = pl.BlockSpec(memory_space=pltpu.VMEM)
    scratch = [pltpu.VMEM((left.shape[1], left.shape[0]), BF) for left in lefts]
    if extra:
        scratch += [pltpu.VMEM((EXT, n * rows), F32), pltpu.VMEM((n * rows, EXT), F32)]
    made = pl.pallas_call(
        kernel,
        in_specs=[vmem] * inputs,
        out_specs=[vmem] * (2 * X),
        out_shape=[shape] * (2 * X),
        scratch_shapes=scratch,
        compiler_params=pltpu.CompilerParams(vmem_limit_bytes=24 * 1024 * 1024),
    )(*lefts, *rights, *extra)
    mine, theirs = made[:X], made[X:]
    came = [None] * X
    for i in list(range(1, X)) + [0]:
        came[i] = grid.core(theirs[i])
    got = []
    for i in range(1, X):
        one = add_parts([(item, lambda g: (g, 0, 0, 0)) for item in (mine[i], came[i])], 4, Y)
        got.append(grid.first(one, i))

    def pick(j):
        return lambda g: (j, g, 0, 0)

    held = [mine[0], came[0]] + got
    final = [(item, 0) for item in held]
    for j in range(1, Y):
        two = add_parts([(item, pick(j)) for item in held], 2, 2).reshape(1, 4, rows, total)
        final.append((grid.second(two, j), 0))
    half = [add_parts([(item, lambda g, near=near: (0, near, 0, 0)) for item, _ in final], 2, 1)[0] for near in range(2)]
    four = grid.z_far(half[0]).astype(F32) + grid.z_near(half[1]).astype(F32)
    core = grid.here()[3]
    kept = jnp.where(core == 0, four[0], four[1])
    sent = jnp.where(core == 0, four[1], four[0]).astype(BF)
    return kept + grid.core(sent).astype(F32)


def product(left, right, dims):
    return lax.dot_general(left, right, (dims, ((), ())), preferred_element_type=F32)


def simple(kernel, ins, outs):
    vmem = pl.BlockSpec(memory_space=pltpu.VMEM)
    return pl.pallas_call(
        kernel,
        in_specs=[vmem] * len(ins),
        out_specs=[vmem] * len(outs),
        out_shape=[jax.ShapeDtypeStruct(shape, kind) for shape, kind in outs],
        compiler_params=pltpu.CompilerParams(vmem_limit_bytes=24 * 1024 * 1024),
    )(*ins)


def split_groups(grid, value, bias, sets):
    count, Z = value.shape[0], grid.z
    group = D // Z

    def kernel(*refs):
        outs = refs[-Z:]
        z = grid.here()[0]

        def write(first):
            for dz in range(Z):
                for part in range(sets):
                    low = part * D + (first + dz) % Z * group
                    item = refs[0][:, low : low + group]
                    if bias is not None:
                        item = item + refs[1][:, low : low + group]
                    outs[dz][:, part * group : (part + 1) * group] = item.astype(BF)

        for first in range(Z):
            pl.when(z == first)(functools.partial(write, first))

    ins = [value] if bias is None else [value, bias]
    return simple(kernel, ins, [((count, sets * group), BF)] * Z)


def join_groups(grid, pieces, sets):
    count, Z = pieces[0].shape[0], grid.z
    group = D // Z

    def kernel(*refs):
        out, sums = refs[Z:]
        z = grid.here()[0]

        def write(first):
            for dz in range(Z):
                for part in range(sets):
                    low = part * D + (first + dz) % Z * group
                    item = refs[dz][:, part * group : (part + 1) * group]
                    out[:, low : low + group] = item
                    sums[:, low : low + group] = jnp.sum(item.astype(F32), axis=0, keepdims=True)

        for first in range(Z):
            pl.when(z == first)(functools.partial(write, first))

    return simple(kernel, pieces, [((count, sets * D), BF), ((1, sets * D), F32)])


def attend(pieces, keys, query_pos, key_pos, heads):
    Z, step = len(pieces), pieces[0].shape[0]
    group = heads * HEAD_DIM
    scale = HEAD_DIM ** (-0.5)

    def kernel(*refs):
        piece_refs, key_refs = refs[:Z], refs[Z : Z + len(keys)]
        row_ref, col_ref, mixed_ref, lse_ref = refs[Z + len(keys) : Z + len(keys) + 4]
        sent = refs[Z + len(keys) + 4 :]
        for head in range(heads):
            low = head * HEAD_DIM
            cols = slice(low, low + HEAD_DIM)
            k = jnp.concatenate([ref[:, cols] for ref in key_refs], axis=0)
            v = jnp.concatenate([ref[:, group + low : group + low + HEAD_DIM] for ref in key_refs], axis=0)
            for at in range(Z):
                rows = slice(at * step, (at + 1) * step)
                q = piece_refs[at][:, cols]
                allowed = row_ref[rows] >= col_ref[...]
                scores = jnp.where(allowed, product(q, k, ((1,), (1,))) * scale, -jnp.inf)
                top = jnp.max(scores, axis=1, keepdims=True)
                probs = jnp.exp(scores - top)
                total = jnp.sum(probs, axis=1, keepdims=True)
                mixed = product(probs.astype(BF), v, ((1,), (0,))) / total
                mixed_ref[rows, cols] = mixed
                sent[at][:, cols] = mixed.astype(BF)
                lse_ref[rows, head : head + 1] = top + jnp.log(total)

    outs = [((Z * step, group), F32), ((Z * step, heads), F32)] + [((step, group), BF)] * Z
    made = simple(kernel, [*pieces, *keys, query_pos[:, None], key_pos[None]], outs)
    return made[0], made[1], made[2:]


def attend_back(pieces, keys, query_pos, key_pos, mixed, lse, grads, heads):
    Z, step = len(pieces), pieces[0].shape[0]
    group = heads * HEAD_DIM
    scale = HEAD_DIM ** (-0.5)
    own = keys[0].shape[0]
    far = len(keys)

    def kernel(*refs):
        piece_refs, key_refs = refs[:Z], refs[Z : Z + far]
        row_ref, col_ref, mixed_ref, lse_ref = refs[Z + far : Z + far + 4]
        grad_refs = refs[Z + far + 4 : 2 * Z + far + 4]
        dq_ref, own_ref = refs[2 * Z + far + 4 : 2 * Z + far + 6]
        far_refs = refs[2 * Z + far + 6 :]
        for head in range(heads):
            low = head * HEAD_DIM
            cols = slice(low, low + HEAD_DIM)
            later = slice(group + low, group + low + HEAD_DIM)
            k = jnp.concatenate([ref[:, cols] for ref in key_refs], axis=0)
            v = jnp.concatenate([ref[:, later] for ref in key_refs], axis=0)
            dk = jnp.zeros((own * far, HEAD_DIM), F32)
            dv = jnp.zeros((own * far, HEAD_DIM), F32)
            for at in range(Z):
                rows = slice(at * step, (at + 1) * step)
                q = piece_refs[at][:, cols]
                g = grad_refs[at][:, cols]
                delta = jnp.sum(g.astype(F32) * mixed_ref[rows, cols], axis=1, keepdims=True)
                allowed = row_ref[rows] >= col_ref[...]
                scores = product(q, k, ((1,), (1,))) * scale
                soft = jnp.where(allowed, jnp.exp(scores - lse_ref[rows, head : head + 1]), 0.0)
                inner = product(g, v, ((1,), (1,)))
                slope = (soft * (inner - delta)).astype(BF)
                dq_ref[rows, cols] = (product(slope, k, ((1,), (0,))) * scale).astype(BF)
                dk = dk + product(slope, q, ((0,), (0,)))
                dv = dv + product(soft.astype(BF), g, ((0,), (0,)))
            dk = dk * scale
            own_ref[:, cols] = dk[:own]
            own_ref[:, later] = dv[:own]
            for at, ref in enumerate(far_refs):
                piece = slice((at + 1) * own, (at + 2) * own)
                ref[:, cols] = dk[piece].astype(BF)
                ref[:, later] = dv[piece].astype(BF)

    outs = [((Z * step, group), BF), ((own, 2 * group), F32)] + [((own, 2 * group), BF)] * (far - 1)
    ins = [*pieces, *keys, query_pos[:, None], key_pos[None], mixed, lse, *grads]
    made = simple(kernel, ins, outs)
    return made[0], made[1], made[2:]


def return_pieces(grad_q, own, came, Z):
    step, group = grad_q.shape[0] // Z, grad_q.shape[1]

    def kernel(*refs):
        outs = refs[-Z:]
        for at, out in enumerate(outs):
            rows = slice(at * step, (at + 1) * step)
            out[:, :group] = refs[0][rows]
            total = refs[1][rows]
            for ref in refs[2:-Z]:
                total = total + ref[rows].astype(F32)
            out[:, group:] = total.astype(BF)

    return simple(kernel, [grad_q, own, *came], [((step, 3 * group), BF)] * Z)


def pack_first(w_qkv, lines, spare, rows):
    width = w_qkv.shape[1]
    used = len(lines) + spare.shape[1] // rows

    def kernel(*refs):
        out = refs[-1]
        out[:, :width] = refs[0][...]
        items = [ref[...] for ref in refs[2:-1]]
        items += [refs[1][:, at * rows : (at + 1) * rows] for at in range(used - len(lines))]
        stacked = jnp.concatenate([item.astype(F32) for item in items] + [jnp.zeros((EXT - used, rows), F32)], axis=0)
        across = lax.broadcasted_iota(jnp.int32, (rows, rows), 0) == lax.broadcasted_iota(jnp.int32, (rows, rows), 1)
        out[:, width:] = product(across.astype(BF), stacked.astype(BF), ((1,), (1,))).astype(BF)

    return simple(kernel, [w_qkv, spare, *lines], [((rows, width + EXT), BF)])[0]


def local_step(
    grid,
    tokens,
    block_order,
    attn_gain,
    attn_shift,
    w_qkv,
    query_bias,
    value_bias,
    w_out,
    out_bias,
    mlp_gain,
    mlp_shift,
    w_fc,
    fc_bias,
    w_proj,
    proj_bias,
    cotangent,
):
    count = tokens.shape[1]
    half = count // 2
    order = block_order[0]
    Z, X = grid.z, grid.x
    z, x, _, _ = grid.here()
    group = D // Z
    heads = HEADS // Z

    rows = w_qkv.shape[1]
    small = [attn_gain, attn_shift, query_bias, value_bias, out_bias, mlp_gain, mlp_shift, proj_bias]
    used = 8 + fc_bias.shape[1] // rows
    w_joint, extra = gather(grid, pack_first(w_qkv[0], small, fc_bias, rows), [3 * D, EXT])
    w_mix, w_up = gather(grid, jnp.concatenate([w_out[0], w_fc[0]], axis=1), [D, w_fc.shape[2]])
    (w_down,) = gather(grid, w_proj[0], [D])
    extra = extra[:, :used].T
    gain_one, shift_one, bias_query, bias_value, bias_mix, gain_two, shift_two, bias_down = [extra[i] for i in range(8)]
    bias_up = jnp.transpose(extra[8:].reshape(used - 8, grid.n, rows), (1, 0, 2)).reshape(-1)

    def positions(dz, dx):
        owner = (z - dz + Z) % Z * X + (x - dx + X) % X
        return true_positions(order, owner * count, count, half)

    query_pos = jnp.concatenate([positions(dz, 0) for dz in range(Z)])
    key_pos = jnp.concatenate([positions(dz, dx) for dx in range(X) for dz in range(Z)])

    def spread(pieces):
        return [pieces[0]] + [grid.along_z(pieces[dz], dz) for dz in range(1, Z)]

    def collect(pieces):
        return [pieces[0]] + [grid.along_z(pieces[dz], -dz) for dz in range(1, Z)]

    state = tokens[0].astype(F32)
    normed_in, normed_one, inverse_one = norm_forward(state, gain_one, shift_one)
    first = normed_in.astype(BF)
    joint = jnp.dot(first, w_joint, preferred_element_type=F32)
    joint_bias = jnp.concatenate([bias_query, jnp.zeros_like(bias_query), bias_value]).astype(F32)[None]
    packed = spread(split_groups(grid, joint, joint_bias, 3))
    own_keys = jnp.concatenate([piece[:, group:] for piece in packed])
    all_keys = [own_keys] + [grid.along_x(own_keys, dx) for dx in range(1, X)]
    mixed_local, log_total, mixed_send = attend(packed, all_keys, query_pos, key_pos, heads)
    mixed_round, _ = join_groups(grid, collect(mixed_send), 1)

    middle = state + jnp.dot(mixed_round, w_mix, preferred_element_type=F32) + bias_mix.astype(F32)
    normed_mid, normed_two, inverse_two = norm_forward(middle, gain_two, shift_two)
    second = normed_mid.astype(BF)
    pre = jnp.dot(second, w_up, preferred_element_type=F32) + bias_up.astype(F32)
    hidden = gelu_value(pre).astype(BF)
    result = middle + jnp.dot(hidden, w_down, preferred_element_type=F32) + bias_down.astype(F32)
    block_out = result.astype(BF)[None]

    grad_state = cotangent[0]
    grad_proj_bias = jnp.sum(grad_state, axis=0)
    grad_round = grad_state.astype(BF)
    shard_proj = scatter(grid, [(hidden, grad_round)])
    grad_pre = jnp.einsum("td,fd->tf", grad_round, w_down, preferred_element_type=F32) * gelu_slope(pre)
    grad_fc_bias = jnp.sum(grad_pre, axis=0)
    grad_pre_round = grad_pre.astype(BF)
    grad_second = jnp.einsum("tf,df->td", grad_pre_round, w_up, preferred_element_type=F32)
    grad_mlp_gain = jnp.sum(grad_second * normed_two, axis=0)
    grad_mlp_shift = jnp.sum(grad_second, axis=0)
    grad_middle = grad_state + norm_backward(grad_second, normed_two, inverse_two, gain_two)
    grad_out_bias = jnp.sum(grad_middle, axis=0)
    middle_round = grad_middle.astype(BF)
    shard_mid = scatter(grid, [(mixed_round, middle_round), (second, grad_pre_round)])
    grad_mixed = jnp.einsum("td,cd->tc", middle_round, w_mix, preferred_element_type=F32).astype(BF)

    grad_local = spread(split_groups(grid, grad_mixed, None, 1))
    grad_q, grad_own, grad_far = attend_back(
        packed, all_keys, query_pos, key_pos, mixed_local, log_total, grad_local, heads
    )
    came = [grid.along_x(grad_far[dx - 1], -dx) for dx in range(1, X)]
    back = collect(return_pieces(grad_q, grad_own, came, Z))
    grad_joint, joint_sums = join_groups(grid, back, 3)
    grad_query_bias = joint_sums[:, :D]
    grad_value_bias = joint_sums[:, 2 * D :]
    grad_first = jnp.einsum("te,de->td", grad_joint, w_joint, preferred_element_type=F32)
    grad_attn_gain = jnp.sum(grad_first * normed_one, axis=0)
    grad_attn_shift = jnp.sum(grad_first, axis=0)
    grad_in = grad_middle + norm_backward(grad_first, normed_one, inverse_one, gain_one)

    vectors = [
        grad_attn_gain,
        grad_attn_shift,
        grad_query_bias,
        grad_value_bias,
        grad_out_bias,
        grad_mlp_gain,
        grad_mlp_shift,
        grad_proj_bias,
    ]
    vectors = [item.reshape(1, D) for item in vectors]
    vectors.append(jnp.transpose(grad_fc_bias.reshape(grid.n, used - 8, rows), (1, 0, 2)).reshape(used - 8, D))
    shard_first = scatter(grid, [(first, grad_joint)], vectors)
    shard_qkv, ends = shard_first[:, : 3 * D], shard_first[:, 3 * D :]
    small = [ends[:, i][None] for i in range(8)]
    return (
        block_out,
        grad_in[None],
        small[0],
        small[1],
        shard_qkv[None],
        small[2],
        small[3],
        shard_mid[None, :, :D],
        small[4],
        small[5],
        small[6],
        shard_mid[None, :, D:],
        ends[:, 8:used].T.reshape(1, -1),
        shard_proj[None],
        small[7],
    )


def solution(mesh):
    grid = Grid(mesh)

    def local(*args):
        return local_step(grid, *args)

    placed = (
        P("fsdp", "ctx", None),
        P("fsdp", None),
        P(None, ("ctx", "fsdp")),
        P(None, ("ctx", "fsdp")),
        P(None, ("ctx", "fsdp"), None),
        P(None, ("ctx", "fsdp")),
        P(None, ("ctx", "fsdp")),
        P(None, ("ctx", "fsdp"), None),
        P(None, ("ctx", "fsdp")),
        P(None, ("ctx", "fsdp")),
        P(None, ("ctx", "fsdp")),
        P(None, ("ctx", "fsdp"), None),
        P(None, ("ctx", "fsdp")),
        P(None, ("ctx", "fsdp"), None),
        P(None, ("ctx", "fsdp")),
        P("fsdp", "ctx", None),
    )
    return jax.shard_map(
        local,
        mesh=mesh,
        in_specs=placed,
        out_specs=(
            P("fsdp", "ctx", None),
            P("fsdp", "ctx", None),
            P(None, ("ctx", "fsdp")),
            P(None, ("ctx", "fsdp")),
            P(None, ("ctx", "fsdp"), None),
            P(None, ("ctx", "fsdp")),
            P(None, ("ctx", "fsdp")),
            P(None, ("ctx", "fsdp"), None),
            P(None, ("ctx", "fsdp")),
            P(None, ("ctx", "fsdp")),
            P(None, ("ctx", "fsdp")),
            P(None, ("ctx", "fsdp"), None),
            P(None, ("ctx", "fsdp")),
            P(None, ("ctx", "fsdp"), None),
            P(None, ("ctx", "fsdp")),
        ),
        check_vma=False,
    )
```

```python
import functools

import jax
import jax.numpy as jnp
from jax import lax
from jax.experimental import pallas as pl
from jax.experimental.pallas import tpu as pltpu
from jax.sharding import PartitionSpec as P


D = 768
HEADS = 12
HEAD_DIM = 64


EPSILON = 1e-05
GELU_SCALE = 0.7978845608028654
GELU_CUBIC = 0.044715


def gelu_value(value):
    return 0.5 * value * (1.0 + jnp.tanh(GELU_SCALE * (value + GELU_CUBIC * value * value * value)))


def gelu_slope(value):
    tangent = jnp.tanh(GELU_SCALE * (value + GELU_CUBIC * value * value * value))
    return 0.5 * (1.0 + tangent) + 0.5 * value * (1.0 - tangent * tangent) * GELU_SCALE * (
        1.0 + 3.0 * GELU_CUBIC * value * value
    )


def true_positions(order, first, count, half):
    rows = first + jnp.arange(count, dtype=jnp.int32)
    blocks = rows // half
    table = blocks[:, None] == jnp.arange(order.shape[0], dtype=jnp.int32)[None, :]
    return jnp.sum(jnp.where(table, order[None, :], 0), axis=1) * half + rows % half


def norm_forward(state, gain, shift):
    centre = state - jnp.mean(state, axis=-1, keepdims=True)
    inverse = lax.rsqrt(jnp.mean(centre * centre, axis=-1, keepdims=True) + EPSILON)
    normed = centre * inverse
    return (normed * gain.astype(jnp.float32) + shift.astype(jnp.float32), normed, inverse)


def norm_backward(grad_out, normed, inverse, gain):
    scaled = grad_out * gain.astype(jnp.float32)
    return inverse * (
        scaled
        - jnp.mean(scaled, axis=-1, keepdims=True)
        - normed * jnp.mean(scaled * normed, axis=-1, keepdims=True)
    )


BF = jnp.bfloat16
F32 = jnp.float32
EXT = 128
AXES = ("ctx", "fsdp")


class Grid:
    def __init__(self, mesh):
        ctx, fsdp = mesh.shape["ctx"], mesh.shape["fsdp"]
        self.z = 4
        self.x = ctx // self.z
        self.y = fsdp // 2
        self.n = ctx * fsdp
        assert self.x == self.y and self.x * self.z == ctx

    def here(self):
        c, f = lax.axis_index("ctx"), lax.axis_index("fsdp")
        return c // self.x, c % self.x, f // 2, f % 2

    def index(self, z, x, y, k):
        return ((z % self.z * self.x + x % self.x) * self.y + y % self.y) * 2 + k % 2

    def send(self, value, move):
        pairs = [
            (self.index(z, x, y, k), self.index(*move(z, x, y, k)))
            for z in range(self.z)
            for x in range(self.x)
            for y in range(self.y)
            for k in range(2)
        ]
        return lax.ppermute(value, AXES, pairs)

    def core(self, value):
        return self.send(value, lambda z, x, y, k: (z, x, y, 1 - k))

    def along_z(self, value, step):
        return self.send(value, lambda z, x, y, k: (z + step, x, y, k))

    def along_x(self, value, step):
        return self.send(value, lambda z, x, y, k: (z, x + step, y, k))

    def first(self, value, step):
        return self.send(value, lambda z, x, y, k: (z, x + step, y, k) if k == 0 else (z, x, y + step, k))

    def second(self, value, step):
        return self.send(value, lambda z, x, y, k: (z, x, y + step, k) if k == 0 else (z, x + step, y, k))

    def z_far(self, value):
        return self.send(value, lambda z, x, y, k: (z, x, y, k) if k == 0 else (z + 1, x, y, k))

    def z_near(self, value):
        return self.send(value, lambda z, x, y, k: (z + 2, x, y, k) if k == 0 else (z + 3, x, y, k))


def gather_z(grid, shard):
    core = grid.here()[3]
    other = grid.core(shard)
    pair = jnp.where(core == 0, jnp.stack([shard, other]), jnp.stack([other, shard]))
    return grid.z_far(pair), grid.z_near(pair)


def gather(grid, lines, widths):
    base = jnp.stack(lines)
    rows = base.shape[2]
    reached = {}
    for i in range(grid.x):
        reached[i, 0] = base if i == 0 else grid.first(base, i)
        for j in range(1, grid.y):
            reached[i, j] = grid.second(reached[i, 0], j)
    own = [reached[i, j] for i in range(grid.x) for j in range(grid.y)]
    parts = own + [grid.core(part) for part in own]
    offsets = [sum(widths[:at]) for at in range(len(widths))]
    X, Y, Z = grid.x, grid.y, grid.z

    def kernel(*refs):
        ins, outs, sem = refs[: len(parts)], refs[len(parts) : -1], refs[-1]
        z, x, y, k = grid.here()
        copies = []
        for at, part in enumerate(ins):
            route = k if at < len(own) else 1 - k
            i, j = (at % len(own)) // Y, (at % len(own)) % Y
            dx = jnp.where(route == 0, i, j)
            dy = jnp.where(route == 0, j, i)
            sx, sy = (x - dx + X) % X, (y - dy + Y) % Y
            for near in range(2):
                sz = (z - 2 * near - route + Z) % Z
                place = (sz * X + sx) * Y + sy
                for out, low, width in zip(outs, offsets, widths):
                    copies.append(
                        pltpu.make_async_copy(
                            part.at[near, :, :, pl.ds(low, width)],
                            out.at[place],
                            sem.at[len(copies)],
                        )
                    )
        for copy in copies:
            copy.start()
        for copy in copies:
            copy.wait()

    whole = pl.pallas_call(
        kernel,
        in_specs=[pl.BlockSpec(memory_space=pl.ANY)] * len(parts),
        out_specs=[pl.BlockSpec(memory_space=pltpu.VMEM)] * len(widths),
        out_shape=[jax.ShapeDtypeStruct((grid.n // 2, 2, rows, width), base.dtype) for width in widths],
        scratch_shapes=[pltpu.SemaphoreType.DMA((len(parts) * 2 * len(widths),))],
        compiler_params=pltpu.CompilerParams(vmem_limit_bytes=12 * 1024 * 1024),
    )(*parts)
    return [item.reshape(grid.n * rows, width) for item, width in zip(whole, widths)]


def add_parts(terms, lead, blocks):
    rows, width = terms[0][0].shape[-2:]

    def kernel(*refs):
        total = refs[0][...].astype(F32)
        for ref in refs[1:-1]:
            total = total + ref[...].astype(F32)
        refs[-1][...] = total.astype(BF)

    return pl.pallas_call(
        kernel,
        grid=(blocks,),
        in_specs=[pl.BlockSpec((None, lead, rows, width), where) for _, where in terms],
        out_specs=pl.BlockSpec((None, lead, rows, width), lambda g: (g, 0, 0, 0)),
        out_shape=jax.ShapeDtypeStruct((blocks, lead, rows, width), BF),
        compiler_params=pltpu.CompilerParams(vmem_limit_bytes=24 * 1024 * 1024),
    )(*[array for array, _ in terms])


def scatter(grid, pairs, extra=()):
    n = grid.n
    X, Y, Z = grid.x, grid.y, grid.z
    rows = pairs[0][0].shape[1] // n
    chunk = 2 * Y * rows
    widths = [right.shape[1] for _, right in pairs]
    offsets = [sum(widths[:at]) for at in range(len(widths))]
    lefts = [left for left, _ in pairs]
    rights = [right for _, right in pairs]
    total = sum(widths) + (EXT if extra else 0)
    inputs = 2 * len(pairs) + len(extra)

    def kernel(*refs):
        left_refs, right_refs, line_refs = refs[: len(pairs)], refs[len(pairs) : 2 * len(pairs)], refs[2 * len(pairs) : inputs]
        outs, turned = refs[inputs : inputs + 2 * X], refs[inputs + 2 * X :]
        z, x, y, k = grid.here()
        for left, turn in zip(left_refs, turned):
            turn[...] = left[...].T
        if line_refs:
            lines, tail = turned[len(pairs) :]
            lines[...] = jnp.zeros(lines.shape, F32)
            at = 0
            for line in line_refs:
                lines[at : at + line.shape[0], :] = line[...]
                at += line.shape[0]
            tail[...] = lines[...].T
        for other in range(2):
            route = k if other == 0 else 1 - k

            def step(at, carry):
                near, dx = at // X, at % X
                tz, tx = (z + 2 * near + route) % Z, (x + dx) % X
                low_row = (tz * X + tx) * chunk
                if rows % 8 == 0:
                    low_row = pl.multiple_of(low_row, chunk)
                made = [
                    product(left[pl.ds(low_row, chunk), :], right[...], ((1,), (0,)))
                    for left, right in zip(turned, right_refs)
                ]
                ends = [tail[pl.ds(low_row, chunk), :]] if line_refs else []

                def store(out, ty, spot):
                    for core in range(2):
                        at = 2 * ty + core
                        span = slice(at * rows, (at + 1) * rows)
                        for value, low, width in zip(made, offsets, widths):
                            out[spot, 2 * near + core, :, low : low + width] = value[span].astype(BF)
                        for value in ends:
                            out[spot, 2 * near + core, :, sum(widths) :] = value[span].astype(BF)

                for ty in range(Y):
                    dy = (ty - y + Y) % Y
                    i = jnp.where(route == 0, dx, dy)
                    j = jnp.where(route == 0, dy, dx)
                    for at in range(X):
                        pl.when(i == at)(functools.partial(store, outs[other * X + at], ty, j))
                return carry

            lax.fori_loop(0, 2 * X, step, 0)

    shape = jax.ShapeDtypeStruct((Y, 4, rows, total), BF)
    vmem = pl.BlockSpec(memory_space=pltpu.VMEM)
    scratch = [pltpu.VMEM((left.shape[1], left.shape[0]), BF) for left in lefts]
    if extra:
        scratch += [pltpu.VMEM((EXT, n * rows), F32), pltpu.VMEM((n * rows, EXT), F32)]
    made = pl.pallas_call(
        kernel,
        in_specs=[vmem] * inputs,
        out_specs=[vmem] * (2 * X),
        out_shape=[shape] * (2 * X),
        scratch_shapes=scratch,
        compiler_params=pltpu.CompilerParams(vmem_limit_bytes=24 * 1024 * 1024),
    )(*lefts, *rights, *extra)
    mine, theirs = made[:X], made[X:]
    came = [None] * X
    for i in list(range(1, X)) + [0]:
        came[i] = grid.core(theirs[i])
    got = []
    for i in range(1, X):
        one = add_parts([(item, lambda g: (g, 0, 0, 0)) for item in (mine[i], came[i])], 4, Y)
        got.append(grid.first(one, i))

    def pick(j):
        return lambda g: (j, g, 0, 0)

    held = [mine[0], came[0]] + got
    final = [(item, 0) for item in held]
    for j in range(1, Y):
        two = add_parts([(item, pick(j)) for item in held], 2, 2).reshape(1, 4, rows, total)
        final.append((grid.second(two, j), 0))
    half = [add_parts([(item, lambda g, near=near: (0, near, 0, 0)) for item, _ in final], 2, 1)[0] for near in range(2)]
    four = grid.z_far(half[0]).astype(F32) + grid.z_near(half[1]).astype(F32)
    core = grid.here()[3]
    kept = jnp.where(core == 0, four[0], four[1])
    sent = jnp.where(core == 0, four[1], four[0]).astype(BF)
    return kept + grid.core(sent).astype(F32)


def product(left, right, dims):
    return lax.dot_general(left, right, (dims, ((), ())), preferred_element_type=F32)


def simple(kernel, ins, outs, scratch=()):
    vmem = pl.BlockSpec(memory_space=pltpu.VMEM)
    return pl.pallas_call(
        kernel,
        in_specs=[vmem] * len(ins),
        out_specs=[vmem] * len(outs),
        out_shape=[jax.ShapeDtypeStruct(shape, kind) for shape, kind in outs],
        scratch_shapes=scratch,
        compiler_params=pltpu.CompilerParams(vmem_limit_bytes=12 * 1024 * 1024),
    )(*ins)


def split_groups(grid, value, bias, sets):
    count, Z = value.shape[0], grid.z
    group = D // Z

    def kernel(*refs):
        outs = refs[-Z:]
        z = grid.here()[0]

        def write(first):
            for dz in range(Z):
                for part in range(sets):
                    low = part * D + (first + dz) % Z * group
                    item = refs[0][:, low : low + group]
                    if bias is not None:
                        item = item + refs[1][:, low : low + group]
                    outs[dz][:, part * group : (part + 1) * group] = item.astype(BF)

        for first in range(Z):
            pl.when(z == first)(functools.partial(write, first))

    ins = [value] if bias is None else [value, bias]
    return simple(kernel, ins, [((count, sets * group), BF)] * Z)


def join_groups(grid, pieces, sets):
    count, Z = pieces[0].shape[0], grid.z
    group = D // Z

    def kernel(*refs):
        out, sums = refs[Z:]
        z = grid.here()[0]

        def write(first):
            for dz in range(Z):
                for part in range(sets):
                    low = part * D + (first + dz) % Z * group
                    item = refs[dz][:, part * group : (part + 1) * group]
                    out[:, low : low + group] = item
                    sums[:, low : low + group] = jnp.sum(item.astype(F32), axis=0, keepdims=True)

        for first in range(Z):
            pl.when(z == first)(functools.partial(write, first))

    return simple(kernel, pieces, [((count, sets * D), BF), ((1, sets * D), F32)])


def attend(pieces, keys, query_pos, key_pos, heads):
    Z, step = len(pieces), pieces[0].shape[0]
    group = heads * HEAD_DIM
    scale = HEAD_DIM ** (-0.5)

    def kernel(*refs):
        piece_refs, key_refs = refs[:Z], refs[Z : Z + len(keys)]
        row_ref, col_ref, mixed_ref, lse_ref = refs[Z + len(keys) : Z + len(keys) + 4]
        sent = refs[Z + len(keys) + 4 :]
        for head in range(heads):
            low = head * HEAD_DIM
            cols = slice(low, low + HEAD_DIM)
            k = jnp.concatenate([ref[:, cols] for ref in key_refs], axis=0)
            v = jnp.concatenate([ref[:, group + low : group + low + HEAD_DIM] for ref in key_refs], axis=0)
            for at in range(Z):
                rows = slice(at * step, (at + 1) * step)
                q = piece_refs[at][:, cols]
                allowed = row_ref[rows] >= col_ref[...]
                scores = jnp.where(allowed, product(q, k, ((1,), (1,))) * scale, -jnp.inf)
                top = jnp.max(scores, axis=1, keepdims=True)
                probs = jnp.exp(scores - top)
                total = jnp.sum(probs, axis=1, keepdims=True)
                mixed = product(probs.astype(BF), v, ((1,), (0,))) / total
                mixed_ref[rows, cols] = mixed
                sent[at][:, cols] = mixed.astype(BF)
                lse_ref[rows, head : head + 1] = top + jnp.log(total)

    outs = [((Z * step, group), F32), ((Z * step, heads), F32)] + [((step, group), BF)] * Z
    made = simple(kernel, [*pieces, *keys, query_pos[:, None], key_pos[None]], outs)
    return made[0], made[1], made[2:]


def attend_back(pieces, keys, query_pos, key_pos, mixed, lse, grads, heads):
    Z, step = len(pieces), pieces[0].shape[0]
    group = heads * HEAD_DIM
    scale = HEAD_DIM ** (-0.5)
    own = keys[0].shape[0]
    far = len(keys)

    def kernel(*refs):
        piece_refs, key_refs = refs[:Z], refs[Z : Z + far]
        row_ref, col_ref, mixed_ref, lse_ref = refs[Z + far : Z + far + 4]
        grad_refs = refs[Z + far + 4 : 2 * Z + far + 4]
        dq_ref, own_ref = refs[2 * Z + far + 4 : 2 * Z + far + 6]
        far_refs = refs[2 * Z + far + 6 :]
        for head in range(heads):
            low = head * HEAD_DIM
            cols = slice(low, low + HEAD_DIM)
            later = slice(group + low, group + low + HEAD_DIM)
            k = jnp.concatenate([ref[:, cols] for ref in key_refs], axis=0)
            v = jnp.concatenate([ref[:, later] for ref in key_refs], axis=0)
            dk = jnp.zeros((own * far, HEAD_DIM), F32)
            dv = jnp.zeros((own * far, HEAD_DIM), F32)
            for at in range(Z):
                rows = slice(at * step, (at + 1) * step)
                q = piece_refs[at][:, cols]
                g = grad_refs[at][:, cols]
                delta = jnp.sum(g.astype(F32) * mixed_ref[rows, cols], axis=1, keepdims=True)
                allowed = row_ref[rows] >= col_ref[...]
                scores = product(q, k, ((1,), (1,))) * scale
                soft = jnp.where(allowed, jnp.exp(scores - lse_ref[rows, head : head + 1]), 0.0)
                inner = product(g, v, ((1,), (1,)))
                slope = (soft * (inner - delta)).astype(BF)
                dq_ref[rows, cols] = (product(slope, k, ((1,), (0,))) * scale).astype(BF)
                dk = dk + product(slope, q, ((0,), (0,)))
                dv = dv + product(soft.astype(BF), g, ((0,), (0,)))
            dk = dk * scale
            own_ref[:, cols] = dk[:own]
            own_ref[:, later] = dv[:own]
            for at, ref in enumerate(far_refs):
                piece = slice((at + 1) * own, (at + 2) * own)
                ref[:, cols] = dk[piece].astype(BF)
                ref[:, later] = dv[piece].astype(BF)

    outs = [((Z * step, group), BF), ((own, 2 * group), F32)] + [((own, 2 * group), BF)] * (far - 1)
    ins = [*pieces, *keys, query_pos[:, None], key_pos[None], mixed, lse, *grads]
    made = simple(kernel, ins, outs)
    return made[0], made[1], made[2:]


def return_pieces(grad_q, own, came, Z):
    step, group = grad_q.shape[0] // Z, grad_q.shape[1]

    def kernel(*refs):
        outs = refs[-Z:]
        for at, out in enumerate(outs):
            rows = slice(at * step, (at + 1) * step)
            out[:, :group] = refs[0][rows]
            total = refs[1][rows]
            for ref in refs[2:-Z]:
                total = total + ref[rows].astype(F32)
            out[:, group:] = total.astype(BF)

    return simple(kernel, [grad_q, own, *came], [((step, 3 * group), BF)] * Z)


def unpack_lines(extra, used, rows):
    spare = used - 8
    n = extra.shape[0] // rows

    def kernel(extra_ref, lines_ref, up_ref, joint_ref, turned):
        turned[...] = extra_ref[...].astype(F32).T
        lines_ref[...] = turned[:8]
        joint_ref[:, :D] = turned[2:3]
        joint_ref[:, D : 2 * D] = jnp.zeros((1, D), F32)
        joint_ref[:, 2 * D :] = turned[3:4]
        for at in range(n):
            for part in range(spare):
                low = (at * spare + part) * rows
                up_ref[:, low : low + rows] = turned[8 + part : 9 + part, at * rows : (at + 1) * rows]

    outs = [((8, D), F32), ((1, spare * D), F32), ((1, 3 * D), F32)]
    return simple(kernel, [extra], outs, [pltpu.VMEM((EXT, D), F32)])


def fold_lines(vector, spare, rows):
    n = D // rows

    def kernel(vector_ref, out_ref):
        for at in range(n):
            for part in range(spare):
                low = (at * spare + part) * rows
                out_ref[part : part + 1, at * rows : (at + 1) * rows] = vector_ref[:, low : low + rows]

    return simple(kernel, [vector], [((spare, D), F32)])[0]


def pack_first(w_qkv, lines, spare, rows):
    width = w_qkv.shape[1]
    used = len(lines) + spare.shape[1] // rows

    def kernel(*refs):
        out = refs[-1]
        out[:, :width] = refs[0][...]
        items = [ref[...] for ref in refs[2:-1]]
        items += [refs[1][:, at * rows : (at + 1) * rows] for at in range(used - len(lines))]
        stacked = jnp.concatenate([item.astype(F32) for item in items] + [jnp.zeros((EXT - used, rows), F32)], axis=0)
        across = lax.broadcasted_iota(jnp.int32, (rows, rows), 0) == lax.broadcasted_iota(jnp.int32, (rows, rows), 1)
        out[:, width:] = product(across.astype(BF), stacked.astype(BF), ((1,), (1,))).astype(BF)

    return simple(kernel, [w_qkv, spare, *lines], [((rows, width + EXT), BF)])[0]


def local_step(
    grid,
    tokens,
    block_order,
    attn_gain,
    attn_shift,
    w_qkv,
    query_bias,
    value_bias,
    w_out,
    out_bias,
    mlp_gain,
    mlp_shift,
    w_fc,
    fc_bias,
    w_proj,
    proj_bias,
    cotangent,
):
    count = tokens.shape[1]
    half = count // 2
    order = block_order[0]
    Z, X = grid.z, grid.x
    z, x, _, _ = grid.here()
    group = D // Z
    heads = HEADS // Z

    rows = w_qkv.shape[1]
    small = [attn_gain, attn_shift, query_bias, value_bias, out_bias, mlp_gain, mlp_shift, proj_bias]
    used = 8 + fc_bias.shape[1] // rows
    first_z = gather_z(grid, pack_first(w_qkv[0], small, fc_bias, rows))
    mid_z = gather_z(grid, jnp.concatenate([w_out[0], w_fc[0]], axis=1))
    last_z = gather_z(grid, w_proj[0])
    w_joint, extra = gather(grid, first_z, [3 * D, EXT])
    w_mix, w_up = gather(grid, mid_z, [D, w_fc.shape[2]])
    lines, bias_up, joint_bias = unpack_lines(extra, used, rows)
    gain_one, shift_one, _, _, bias_mix, gain_two, shift_two, bias_down = [lines[i : i + 1] for i in range(8)]

    def positions(dz, dx):
        owner = (z - dz + Z) % Z * X + (x - dx + X) % X
        return true_positions(order, owner * count, count, half)

    query_pos = jnp.concatenate([positions(dz, 0) for dz in range(Z)])
    key_pos = jnp.concatenate([positions(dz, dx) for dx in range(X) for dz in range(Z)])

    def spread(pieces):
        return [pieces[0]] + [grid.along_z(pieces[dz], dz) for dz in range(1, Z)]

    def collect(pieces):
        return [pieces[0]] + [grid.along_z(pieces[dz], -dz) for dz in range(1, Z)]

    state = tokens[0].astype(F32)
    normed_in, normed_one, inverse_one = norm_forward(state, gain_one, shift_one)
    first = normed_in.astype(BF)
    joint = jnp.dot(first, w_joint, preferred_element_type=F32)
    packed = spread(split_groups(grid, joint, joint_bias, 3))
    own_keys = jnp.concatenate([piece[:, group:] for piece in packed])
    all_keys = [own_keys] + [grid.along_x(own_keys, dx) for dx in range(1, X)]
    mixed_local, log_total, mixed_send = attend(packed, all_keys, query_pos, key_pos, heads)
    log_total, *last_z = lax.optimization_barrier((log_total, *last_z))
    (w_down,) = gather(grid, last_z, [D])
    mixed_round, _ = join_groups(grid, collect(mixed_send), 1)

    middle = state + jnp.dot(mixed_round, w_mix, preferred_element_type=F32) + bias_mix.astype(F32)
    normed_mid, normed_two, inverse_two = norm_forward(middle, gain_two, shift_two)
    second = normed_mid.astype(BF)
    pre = jnp.dot(second, w_up, preferred_element_type=F32) + bias_up.astype(F32)
    hidden = gelu_value(pre).astype(BF)
    result = middle + jnp.dot(hidden, w_down, preferred_element_type=F32) + bias_down.astype(F32)
    block_out = result.astype(BF)[None]

    grad_state = cotangent[0]
    grad_proj_bias = jnp.sum(grad_state, axis=0)
    grad_round = grad_state.astype(BF)
    shard_proj = scatter(grid, [(hidden, grad_round)])
    grad_pre = jnp.einsum("td,fd->tf", grad_round, w_down, preferred_element_type=F32) * gelu_slope(pre)
    grad_fc_bias = jnp.sum(grad_pre, axis=0)
    grad_pre_round = grad_pre.astype(BF)
    grad_second = jnp.einsum("tf,df->td", grad_pre_round, w_up, preferred_element_type=F32)
    grad_mlp_gain = jnp.sum(grad_second * normed_two, axis=0)
    grad_mlp_shift = jnp.sum(grad_second, axis=0)
    grad_middle = grad_state + norm_backward(grad_second, normed_two, inverse_two, gain_two)
    grad_out_bias = jnp.sum(grad_middle, axis=0)
    middle_round = grad_middle.astype(BF)
    shard_mid = scatter(grid, [(mixed_round, middle_round), (second, grad_pre_round)])
    grad_mixed = jnp.einsum("td,cd->tc", middle_round, w_mix, preferred_element_type=F32).astype(BF)

    grad_local = spread(split_groups(grid, grad_mixed, None, 1))
    grad_q, grad_own, grad_far = attend_back(
        packed, all_keys, query_pos, key_pos, mixed_local, log_total, grad_local, heads
    )
    came = [grid.along_x(grad_far[dx - 1], -dx) for dx in range(1, X)]
    back = collect(return_pieces(grad_q, grad_own, came, Z))
    grad_joint, joint_sums = join_groups(grid, back, 3)
    grad_query_bias = joint_sums[:, :D]
    grad_value_bias = joint_sums[:, 2 * D :]
    grad_first = jnp.einsum("te,de->td", grad_joint, w_joint, preferred_element_type=F32)
    grad_attn_gain = jnp.sum(grad_first * normed_one, axis=0)
    grad_attn_shift = jnp.sum(grad_first, axis=0)
    grad_in = grad_middle + norm_backward(grad_first, normed_one, inverse_one, gain_one)

    vectors = [
        grad_attn_gain,
        grad_attn_shift,
        grad_query_bias,
        grad_value_bias,
        grad_out_bias,
        grad_mlp_gain,
        grad_mlp_shift,
        grad_proj_bias,
    ]
    vectors = [item.reshape(1, D) for item in vectors]
    vectors.append(fold_lines(grad_fc_bias.reshape(1, -1), used - 8, rows))
    shard_first = scatter(grid, [(first, grad_joint)], vectors)
    shard_qkv, ends = shard_first[:, : 3 * D], shard_first[:, 3 * D :]
    small = [ends[:, i][None] for i in range(8)]
    return (
        block_out,
        grad_in[None],
        small[0],
        small[1],
        shard_qkv[None],
        small[2],
        small[3],
        shard_mid[None, :, :D],
        small[4],
        small[5],
        small[6],
        shard_mid[None, :, D:],
        ends[:, 8:used].T.reshape(1, -1),
        shard_proj[None],
        small[7],
    )


def solution(mesh):
    grid = Grid(mesh)

    def local(*args):
        return local_step(grid, *args)

    placed = (
        P("fsdp", "ctx", None),
        P("fsdp", None),
        P(None, ("ctx", "fsdp")),
        P(None, ("ctx", "fsdp")),
        P(None, ("ctx", "fsdp"), None),
        P(None, ("ctx", "fsdp")),
        P(None, ("ctx", "fsdp")),
        P(None, ("ctx", "fsdp"), None),
        P(None, ("ctx", "fsdp")),
        P(None, ("ctx", "fsdp")),
        P(None, ("ctx", "fsdp")),
        P(None, ("ctx", "fsdp"), None),
        P(None, ("ctx", "fsdp")),
        P(None, ("ctx", "fsdp"), None),
        P(None, ("ctx", "fsdp")),
        P("fsdp", "ctx", None),
    )
    return jax.shard_map(
        local,
        mesh=mesh,
        in_specs=placed,
        out_specs=(
            P("fsdp", "ctx", None),
            P("fsdp", "ctx", None),
            P(None, ("ctx", "fsdp")),
            P(None, ("ctx", "fsdp")),
            P(None, ("ctx", "fsdp"), None),
            P(None, ("ctx", "fsdp")),
            P(None, ("ctx", "fsdp")),
            P(None, ("ctx", "fsdp"), None),
            P(None, ("ctx", "fsdp")),
            P(None, ("ctx", "fsdp")),
            P(None, ("ctx", "fsdp")),
            P(None, ("ctx", "fsdp"), None),
            P(None, ("ctx", "fsdp")),
            P(None, ("ctx", "fsdp"), None),
            P(None, ("ctx", "fsdp")),
        ),
        check_vma=False,
    )
```

```python
import functools

import jax
import jax.numpy as jnp
from jax import lax
from jax.experimental import pallas as pl
from jax.experimental.pallas import tpu as pltpu
from jax.sharding import PartitionSpec as P


D = 768
HEADS = 12
HEAD_DIM = 64


EPSILON = 1e-05
GELU_SCALE = 0.7978845608028654
GELU_CUBIC = 0.044715


def gelu_value(value):
    return 0.5 * value * (1.0 + jnp.tanh(GELU_SCALE * (value + GELU_CUBIC * value * value * value)))


def gelu_slope(value):
    tangent = jnp.tanh(GELU_SCALE * (value + GELU_CUBIC * value * value * value))
    return 0.5 * (1.0 + tangent) + 0.5 * value * (1.0 - tangent * tangent) * GELU_SCALE * (
        1.0 + 3.0 * GELU_CUBIC * value * value
    )


def true_positions(order, first, count, half):
    rows = first + jnp.arange(count, dtype=jnp.int32)
    blocks = rows // half
    table = blocks[:, None] == jnp.arange(order.shape[0], dtype=jnp.int32)[None, :]
    return jnp.sum(jnp.where(table, order[None, :], 0), axis=1) * half + rows % half


def norm_forward(state, gain, shift):
    centre = state - jnp.mean(state, axis=-1, keepdims=True)
    inverse = lax.rsqrt(jnp.mean(centre * centre, axis=-1, keepdims=True) + EPSILON)
    normed = centre * inverse
    return (normed * gain.astype(jnp.float32) + shift.astype(jnp.float32), normed, inverse)


def norm_backward(grad_out, normed, inverse, gain):
    scaled = grad_out * gain.astype(jnp.float32)
    return inverse * (
        scaled
        - jnp.mean(scaled, axis=-1, keepdims=True)
        - normed * jnp.mean(scaled * normed, axis=-1, keepdims=True)
    )


BF = jnp.bfloat16
F32 = jnp.float32
EXT = 128
AXES = ("ctx", "fsdp")


class Grid:
    def __init__(self, mesh):
        ctx, fsdp = mesh.shape["ctx"], mesh.shape["fsdp"]
        self.z = 4
        self.x = ctx // self.z
        self.y = fsdp // 2
        self.n = ctx * fsdp
        assert self.x == self.y and self.x * self.z == ctx

    def here(self):
        c, f = lax.axis_index("ctx"), lax.axis_index("fsdp")
        return c // self.x, c % self.x, f // 2, f % 2

    def index(self, z, x, y, k):
        return ((z % self.z * self.x + x % self.x) * self.y + y % self.y) * 2 + k % 2

    def send(self, value, move):
        pairs = [
            (self.index(z, x, y, k), self.index(*move(z, x, y, k)))
            for z in range(self.z)
            for x in range(self.x)
            for y in range(self.y)
            for k in range(2)
        ]
        return lax.ppermute(value, AXES, pairs)

    def core(self, value):
        return self.send(value, lambda z, x, y, k: (z, x, y, 1 - k))

    def along_z(self, value, step):
        return self.send(value, lambda z, x, y, k: (z + step, x, y, k))

    def along_x(self, value, step):
        return self.send(value, lambda z, x, y, k: (z, x + step, y, k))

    def first(self, value, step):
        return self.send(value, lambda z, x, y, k: (z, x + step, y, k) if k == 0 else (z, x, y + step, k))

    def second(self, value, step):
        return self.send(value, lambda z, x, y, k: (z, x, y + step, k) if k == 0 else (z, x + step, y, k))

    def z_far(self, value):
        return self.send(value, lambda z, x, y, k: (z, x, y, k) if k == 0 else (z + 1, x, y, k))

    def z_near(self, value):
        return self.send(value, lambda z, x, y, k: (z + 2, x, y, k) if k == 0 else (z + 3, x, y, k))


def gather_z(grid, shard):
    core = grid.here()[3]
    other = grid.core(shard)
    pair = jnp.where(core == 0, jnp.stack([shard, other]), jnp.stack([other, shard]))
    return grid.z_far(pair), grid.z_near(pair)


def gather(grid, lines, widths):
    base = jnp.stack(lines)
    rows = base.shape[2]
    reached = {}
    for i in range(grid.x):
        reached[i, 0] = base if i == 0 else grid.first(base, i)
        for j in range(1, grid.y):
            reached[i, j] = grid.second(reached[i, 0], j)
    own = [reached[i, j] for i in range(grid.x) for j in range(grid.y)]
    parts = own + [grid.core(part) for part in own]
    offsets = [sum(widths[:at]) for at in range(len(widths))]
    X, Y, Z = grid.x, grid.y, grid.z

    def kernel(*refs):
        ins, outs, sem = refs[: len(parts)], refs[len(parts) : -1], refs[-1]
        z, x, y, k = grid.here()
        copies = []
        for at, part in enumerate(ins):
            route = k if at < len(own) else 1 - k
            i, j = (at % len(own)) // Y, (at % len(own)) % Y
            dx = jnp.where(route == 0, i, j)
            dy = jnp.where(route == 0, j, i)
            sx, sy = (x - dx + X) % X, (y - dy + Y) % Y
            for near in range(2):
                sz = (z - 2 * near - route + Z) % Z
                place = (sz * X + sx) * Y + sy
                for out, low, width in zip(outs, offsets, widths):
                    copies.append(
                        pltpu.make_async_copy(
                            part.at[near, :, :, pl.ds(low, width)],
                            out.at[place],
                            sem.at[len(copies)],
                        )
                    )
        for copy in copies:
            copy.start()
        for copy in copies:
            copy.wait()

    whole = pl.pallas_call(
        kernel,
        in_specs=[pl.BlockSpec(memory_space=pl.ANY)] * len(parts),
        out_specs=[pl.BlockSpec(memory_space=pltpu.VMEM)] * len(widths),
        out_shape=[jax.ShapeDtypeStruct((grid.n // 2, 2, rows, width), base.dtype) for width in widths],
        scratch_shapes=[pltpu.SemaphoreType.DMA((len(parts) * 2 * len(widths),))],
        compiler_params=pltpu.CompilerParams(vmem_limit_bytes=12 * 1024 * 1024),
    )(*parts)
    return [item.reshape(grid.n * rows, width) for item, width in zip(whole, widths)]


def add_parts(terms, lead, blocks):
    rows, width = terms[0][0].shape[-2:]

    def kernel(*refs):
        total = refs[0][...].astype(F32)
        for ref in refs[1:-1]:
            total = total + ref[...].astype(F32)
        refs[-1][...] = total.astype(BF)

    return pl.pallas_call(
        kernel,
        grid=(blocks,),
        in_specs=[pl.BlockSpec((None, lead, rows, width), where) for _, where in terms],
        out_specs=pl.BlockSpec((None, lead, rows, width), lambda g: (g, 0, 0, 0)),
        out_shape=jax.ShapeDtypeStruct((blocks, lead, rows, width), BF),
        compiler_params=pltpu.CompilerParams(vmem_limit_bytes=24 * 1024 * 1024),
    )(*[array for array, _ in terms])


def scatter(grid, pairs, extra=()):
    n = grid.n
    X, Y, Z = grid.x, grid.y, grid.z
    rows = pairs[0][0].shape[1] // n
    chunk = 2 * Y * rows
    widths = [right.shape[1] for _, right in pairs]
    offsets = [sum(widths[:at]) for at in range(len(widths))]
    lefts = [left for left, _ in pairs]
    rights = [right for _, right in pairs]
    total = sum(widths) + (EXT if extra else 0)
    inputs = 2 * len(pairs) + len(extra)

    def kernel(*refs):
        left_refs, right_refs, line_refs = refs[: len(pairs)], refs[len(pairs) : 2 * len(pairs)], refs[2 * len(pairs) : inputs]
        outs, turned = refs[inputs : inputs + 2 * X], refs[inputs + 2 * X :]
        z, x, y, k = grid.here()
        for left, turn in zip(left_refs, turned):
            turn[...] = left[...].T
        if line_refs:
            lines, tail = turned[len(pairs) :]
            lines[...] = jnp.zeros(lines.shape, F32)
            at = 0
            for line in line_refs:
                lines[at : at + line.shape[0], :] = line[...]
                at += line.shape[0]
            tail[...] = lines[...].T
        for other in range(2):
            route = k if other == 0 else 1 - k

            def step(at, carry):
                near, dx = at // X, at % X
                tz, tx = (z + 2 * near + route) % Z, (x + dx) % X
                low_row = (tz * X + tx) * chunk
                if rows % 8 == 0:
                    low_row = pl.multiple_of(low_row, chunk)
                made = [
                    product(left[pl.ds(low_row, chunk), :], right[...], ((1,), (0,)))
                    for left, right in zip(turned, right_refs)
                ]
                ends = [tail[pl.ds(low_row, chunk), :]] if line_refs else []

                def store(out, ty, spot):
                    for core in range(2):
                        at = 2 * ty + core
                        span = slice(at * rows, (at + 1) * rows)
                        for value, low, width in zip(made, offsets, widths):
                            out[spot, 2 * near + core, :, low : low + width] = value[span].astype(BF)
                        for value in ends:
                            out[spot, 2 * near + core, :, sum(widths) :] = value[span].astype(BF)

                for ty in range(Y):
                    dy = (ty - y + Y) % Y
                    i = jnp.where(route == 0, dx, dy)
                    j = jnp.where(route == 0, dy, dx)
                    for at in range(X):
                        pl.when(i == at)(functools.partial(store, outs[other * X + at], ty, j))
                return carry

            lax.fori_loop(0, 2 * X, step, 0)

    shape = jax.ShapeDtypeStruct((Y, 4, rows, total), BF)
    vmem = pl.BlockSpec(memory_space=pltpu.VMEM)
    scratch = [pltpu.VMEM((left.shape[1], left.shape[0]), BF) for left in lefts]
    if extra:
        scratch += [pltpu.VMEM((EXT, n * rows), F32), pltpu.VMEM((n * rows, EXT), F32)]
    made = pl.pallas_call(
        kernel,
        in_specs=[vmem] * inputs,
        out_specs=[vmem] * (2 * X),
        out_shape=[shape] * (2 * X),
        scratch_shapes=scratch,
        compiler_params=pltpu.CompilerParams(vmem_limit_bytes=24 * 1024 * 1024),
    )(*lefts, *rights, *extra)
    mine, theirs = made[:X], made[X:]
    came = [None] * X
    for i in list(range(1, X)) + [0]:
        came[i] = grid.core(theirs[i])
    got = []
    for i in range(1, X):
        one = add_parts([(item, lambda g: (g, 0, 0, 0)) for item in (mine[i], came[i])], 4, Y)
        got.append(grid.first(one, i))

    def pick(j):
        return lambda g: (j, g, 0, 0)

    held = [mine[0], came[0]] + got
    final = [(item, 0) for item in held]
    for j in range(1, Y):
        two = add_parts([(item, pick(j)) for item in held], 2, 2).reshape(1, 4, rows, total)
        final.append((grid.second(two, j), 0))
    half = [add_parts([(item, lambda g, near=near: (0, near, 0, 0)) for item, _ in final], 2, 1)[0] for near in range(2)]
    four = [grid.z_far(half[0]), grid.z_near(half[1])]
    core = grid.here()[3]
    four = four[0].astype(F32) + four[1].astype(F32)
    kept = jnp.where(core == 0, four[0], four[1])
    sent = jnp.where(core == 0, four[1], four[0]).astype(BF)
    return kept + grid.core(sent).astype(F32)


def product(left, right, dims):
    return lax.dot_general(left, right, (dims, ((), ())), preferred_element_type=F32)


def simple(kernel, ins, outs, scratch=(), fetch=False):
    vmem = pl.BlockSpec(memory_space=pltpu.VMEM)
    specs = [vmem] * len(ins)
    if fetch:
        specs = [pl.BlockSpec(item.shape, lambda g, item=item: (0,) * item.ndim) for item in ins]
    return pl.pallas_call(
        kernel,
        grid=(1,) if fetch else (),
        in_specs=specs,
        out_specs=[vmem] * len(outs),
        out_shape=[jax.ShapeDtypeStruct(shape, kind) for shape, kind in outs],
        scratch_shapes=scratch,
        compiler_params=pltpu.CompilerParams(vmem_limit_bytes=12 * 1024 * 1024),
    )(*ins)


def split_groups(grid, value, bias, sets):
    count, Z = value.shape[0], grid.z
    group = D // Z

    def kernel(*refs):
        outs = refs[-Z:]
        z = grid.here()[0]

        def write(first):
            for dz in range(Z):
                for part in range(sets):
                    low = part * D + (first + dz) % Z * group
                    item = refs[0][:, low : low + group]
                    if bias is not None:
                        item = item + refs[1][:, low : low + group]
                    outs[dz][:, part * group : (part + 1) * group] = item.astype(BF)

        for first in range(Z):
            pl.when(z == first)(functools.partial(write, first))

    ins = [value] if bias is None else [value, bias]
    return simple(kernel, ins, [((count, sets * group), BF)] * Z)


def join_groups(grid, pieces, sets):
    count, Z = pieces[0].shape[0], grid.z
    group = D // Z

    def kernel(*refs):
        out, sums = refs[Z:]
        z = grid.here()[0]

        def write(first):
            for dz in range(Z):
                for part in range(sets):
                    low = part * D + (first + dz) % Z * group
                    item = refs[dz][:, part * group : (part + 1) * group]
                    out[:, low : low + group] = item
                    sums[:, low : low + group] = jnp.sum(item.astype(F32), axis=0, keepdims=True)

        for first in range(Z):
            pl.when(z == first)(functools.partial(write, first))

    return simple(kernel, pieces, [((count, sets * D), BF), ((1, sets * D), F32)])


def attend(pieces, keys, query_pos, key_pos, heads):
    Z, step = len(pieces), pieces[0].shape[0]
    group = heads * HEAD_DIM
    scale = HEAD_DIM ** (-0.5)

    def kernel(*refs):
        piece_refs, key_refs = refs[:Z], refs[Z : Z + len(keys)]
        row_ref, col_ref, mixed_ref, lse_ref = refs[Z + len(keys) : Z + len(keys) + 4]
        sent = refs[Z + len(keys) + 4 :]
        for head in range(heads):
            low = head * HEAD_DIM
            cols = slice(low, low + HEAD_DIM)
            k = jnp.concatenate([ref[:, cols] for ref in key_refs], axis=0)
            v = jnp.concatenate([ref[:, group + low : group + low + HEAD_DIM] for ref in key_refs], axis=0)
            for at in range(Z):
                rows = slice(at * step, (at + 1) * step)
                q = piece_refs[at][:, cols]
                allowed = row_ref[rows] >= col_ref[...]
                scores = jnp.where(allowed, product(q, k, ((1,), (1,))) * scale, -jnp.inf)
                top = jnp.max(scores, axis=1, keepdims=True)
                probs = jnp.exp(scores - top)
                total = jnp.sum(probs, axis=1, keepdims=True)
                mixed = product(probs.astype(BF), v, ((1,), (0,))) / total
                mixed_ref[rows, cols] = mixed
                sent[at][:, cols] = mixed.astype(BF)
                lse_ref[rows, head : head + 1] = top + jnp.log(total)

    outs = [((Z * step, group), F32), ((Z * step, heads), F32)] + [((step, group), BF)] * Z
    made = simple(kernel, [*pieces, *keys, query_pos[:, None], key_pos[None]], outs, fetch=True)
    return made[0], made[1], made[2:]


def attend_back(pieces, keys, query_pos, key_pos, mixed, lse, grads, heads):
    Z, step = len(pieces), pieces[0].shape[0]
    group = heads * HEAD_DIM
    scale = HEAD_DIM ** (-0.5)
    own = keys[0].shape[0]
    far = len(keys)

    def kernel(*refs):
        piece_refs, key_refs = refs[:Z], refs[Z : Z + far]
        row_ref, col_ref, mixed_ref, lse_ref = refs[Z + far : Z + far + 4]
        grad_refs = refs[Z + far + 4 : 2 * Z + far + 4]
        dq_ref, own_ref = refs[2 * Z + far + 4 : 2 * Z + far + 6]
        far_refs = refs[2 * Z + far + 6 :]
        for head in range(heads):
            low = head * HEAD_DIM
            cols = slice(low, low + HEAD_DIM)
            later = slice(group + low, group + low + HEAD_DIM)
            k = jnp.concatenate([ref[:, cols] for ref in key_refs], axis=0)
            v = jnp.concatenate([ref[:, later] for ref in key_refs], axis=0)
            dk = jnp.zeros((own * far, HEAD_DIM), F32)
            dv = jnp.zeros((own * far, HEAD_DIM), F32)
            for at in range(Z):
                rows = slice(at * step, (at + 1) * step)
                q = piece_refs[at][:, cols]
                g = grad_refs[at][:, cols]
                delta = jnp.sum(g.astype(F32) * mixed_ref[rows, cols], axis=1, keepdims=True)
                allowed = row_ref[rows] >= col_ref[...]
                scores = product(q, k, ((1,), (1,))) * scale
                soft = jnp.where(allowed, jnp.exp(scores - lse_ref[rows, head : head + 1]), 0.0)
                inner = product(g, v, ((1,), (1,)))
                slope = (soft * (inner - delta)).astype(BF)
                dq_ref[rows, cols] = (product(slope, k, ((1,), (0,))) * scale).astype(BF)
                dk = dk + product(slope, q, ((0,), (0,)))
                dv = dv + product(soft.astype(BF), g, ((0,), (0,)))
            dk = dk * scale
            own_ref[:, cols] = dk[:own]
            own_ref[:, later] = dv[:own]
            for at, ref in enumerate(far_refs):
                piece = slice((at + 1) * own, (at + 2) * own)
                ref[:, cols] = dk[piece].astype(BF)
                ref[:, later] = dv[piece].astype(BF)

    outs = [((Z * step, group), BF), ((own, 2 * group), F32)] + [((own, 2 * group), BF)] * (far - 1)
    ins = [*pieces, *keys, query_pos[:, None], key_pos[None], mixed, lse, *grads]
    made = simple(kernel, ins, outs)
    return made[0], made[1], made[2:]


def return_pieces(grad_q, own, came, Z):
    step, group = grad_q.shape[0] // Z, grad_q.shape[1]

    def kernel(*refs):
        outs = refs[-Z:]
        for at, out in enumerate(outs):
            rows = slice(at * step, (at + 1) * step)
            out[:, :group] = refs[0][rows]
            total = refs[1][rows]
            for ref in refs[2:-Z]:
                total = total + ref[rows].astype(F32)
            out[:, group:] = total.astype(BF)

    return simple(kernel, [grad_q, own, *came], [((step, 3 * group), BF)] * Z)


def unpack_lines(extra, used, rows):
    spare = used - 8
    n = extra.shape[0] // rows

    def kernel(extra_ref, lines_ref, up_ref, joint_ref, turned):
        turned[...] = extra_ref[...].astype(F32).T
        lines_ref[...] = turned[:8]
        joint_ref[:, :D] = turned[2:3]
        joint_ref[:, D : 2 * D] = jnp.zeros((1, D), F32)
        joint_ref[:, 2 * D :] = turned[3:4]
        for at in range(n):
            for part in range(spare):
                low = (at * spare + part) * rows
                up_ref[:, low : low + rows] = turned[8 + part : 9 + part, at * rows : (at + 1) * rows]

    outs = [((8, D), F32), ((1, spare * D), F32), ((1, 3 * D), F32)]
    return simple(kernel, [extra], outs, [pltpu.VMEM((EXT, D), F32)])


def fold_lines(vector, spare, rows):
    n = D // rows

    def kernel(vector_ref, out_ref):
        for at in range(n):
            for part in range(spare):
                low = (at * spare + part) * rows
                out_ref[part : part + 1, at * rows : (at + 1) * rows] = vector_ref[:, low : low + rows]

    return simple(kernel, [vector], [((spare, D), F32)])[0]


def pack_first(w_qkv, lines, spare, rows):
    width = w_qkv.shape[1]
    used = len(lines) + spare.shape[1] // rows

    def kernel(*refs):
        out = refs[-1]
        out[:, :width] = refs[0][...]
        items = [ref[...] for ref in refs[2:-1]]
        items += [refs[1][:, at * rows : (at + 1) * rows] for at in range(used - len(lines))]
        stacked = jnp.concatenate([item.astype(F32) for item in items] + [jnp.zeros((EXT - used, rows), F32)], axis=0)
        across = lax.broadcasted_iota(jnp.int32, (rows, rows), 0) == lax.broadcasted_iota(jnp.int32, (rows, rows), 1)
        out[:, width:] = product(across.astype(BF), stacked.astype(BF), ((1,), (1,))).astype(BF)

    return simple(kernel, [w_qkv, spare, *lines], [((rows, width + EXT), BF)], fetch=True)[0]


def local_step(
    grid,
    tokens,
    block_order,
    attn_gain,
    attn_shift,
    w_qkv,
    query_bias,
    value_bias,
    w_out,
    out_bias,
    mlp_gain,
    mlp_shift,
    w_fc,
    fc_bias,
    w_proj,
    proj_bias,
    cotangent,
):
    count = tokens.shape[1]
    half = count // 2
    order = block_order[0]
    Z, X = grid.z, grid.x
    z, x, _, _ = grid.here()
    group = D // Z
    heads = HEADS // Z

    rows = w_qkv.shape[1]
    small = [attn_gain, attn_shift, query_bias, value_bias, out_bias, mlp_gain, mlp_shift, proj_bias]
    used = 8 + fc_bias.shape[1] // rows
    first_z = gather_z(grid, pack_first(w_qkv[0], small, fc_bias, rows))
    mid_z = gather_z(grid, jnp.concatenate([w_out[0], w_fc[0]], axis=1))
    last_z = gather_z(grid, w_proj[0])
    w_joint, extra = gather(grid, first_z, [3 * D, EXT])
    w_mix, w_up = gather(grid, mid_z, [D, w_fc.shape[2]])
    lines, bias_up, joint_bias = unpack_lines(extra, used, rows)
    gain_one, shift_one, _, _, bias_mix, gain_two, shift_two, bias_down = [lines[i : i + 1] for i in range(8)]

    def positions(dz, dx):
        owner = (z - dz + Z) % Z * X + (x - dx + X) % X
        return true_positions(order, owner * count, count, half)

    query_pos = jnp.concatenate([positions(dz, 0) for dz in range(Z)])
    key_pos = jnp.concatenate([positions(dz, dx) for dx in range(X) for dz in range(Z)])

    def spread(pieces):
        return [pieces[0]] + [grid.along_z(pieces[dz], dz) for dz in range(1, Z)]

    def collect(pieces):
        return [pieces[0]] + [grid.along_z(pieces[dz], -dz) for dz in range(1, Z)]

    state = tokens[0].astype(F32)
    normed_in, normed_one, inverse_one = norm_forward(state, gain_one, shift_one)
    first = normed_in.astype(BF)
    joint = jnp.dot(first, w_joint, preferred_element_type=F32)
    packed = spread(split_groups(grid, joint, joint_bias, 3))
    own_keys = jnp.concatenate([piece[:, group:] for piece in packed])
    all_keys = [own_keys] + [grid.along_x(own_keys, dx) for dx in range(1, X)]
    mixed_local, log_total, mixed_send = attend(packed, all_keys, query_pos, key_pos, heads)
    log_total, *last_z = lax.optimization_barrier((log_total, *last_z))
    (w_down,) = gather(grid, last_z, [D])
    mixed_round, _ = join_groups(grid, collect(mixed_send), 1)

    middle = state + jnp.dot(mixed_round, w_mix, preferred_element_type=F32) + bias_mix.astype(F32)
    normed_mid, normed_two, inverse_two = norm_forward(middle, gain_two, shift_two)
    second = normed_mid.astype(BF)
    pre = jnp.dot(second, w_up, preferred_element_type=F32) + bias_up.astype(F32)
    hidden = gelu_value(pre).astype(BF)
    result = middle + jnp.dot(hidden, w_down, preferred_element_type=F32) + bias_down.astype(F32)
    block_out = result.astype(BF)[None]

    grad_state = cotangent[0]
    grad_proj_bias = jnp.sum(grad_state, axis=0)
    grad_round = grad_state.astype(BF)
    shard_proj = scatter(grid, [(hidden, grad_round)])
    grad_pre = jnp.einsum("td,fd->tf", grad_round, w_down, preferred_element_type=F32) * gelu_slope(pre)
    grad_fc_bias = jnp.sum(grad_pre, axis=0)
    grad_pre_round = grad_pre.astype(BF)
    grad_second = jnp.einsum("tf,df->td", grad_pre_round, w_up, preferred_element_type=F32)
    grad_mlp_gain = jnp.sum(grad_second * normed_two, axis=0)
    grad_mlp_shift = jnp.sum(grad_second, axis=0)
    grad_middle = grad_state + norm_backward(grad_second, normed_two, inverse_two, gain_two)
    grad_out_bias = jnp.sum(grad_middle, axis=0)
    middle_round = grad_middle.astype(BF)
    shard_mid = scatter(grid, [(mixed_round, middle_round), (second, grad_pre_round)])
    grad_mixed = jnp.einsum("td,cd->tc", middle_round, w_mix, preferred_element_type=F32).astype(BF)

    grad_local = spread(split_groups(grid, grad_mixed, None, 1))
    grad_q, grad_own, grad_far = attend_back(
        packed, all_keys, query_pos, key_pos, mixed_local, log_total, grad_local, heads
    )
    came = [grid.along_x(grad_far[dx - 1], -dx) for dx in range(1, X)]
    back = collect(return_pieces(grad_q, grad_own, came, Z))
    grad_joint, joint_sums = join_groups(grid, back, 3)
    grad_query_bias = joint_sums[:, :D]
    grad_value_bias = joint_sums[:, 2 * D :]
    grad_first = jnp.einsum("te,de->td", grad_joint, w_joint, preferred_element_type=F32)
    grad_attn_gain = jnp.sum(grad_first * normed_one, axis=0)
    grad_attn_shift = jnp.sum(grad_first, axis=0)
    grad_in = grad_middle + norm_backward(grad_first, normed_one, inverse_one, gain_one)

    vectors = [
        grad_attn_gain,
        grad_attn_shift,
        grad_query_bias,
        grad_value_bias,
        grad_out_bias,
        grad_mlp_gain,
        grad_mlp_shift,
        grad_proj_bias,
    ]
    vectors = [item.reshape(1, D) for item in vectors]
    vectors.append(fold_lines(grad_fc_bias.reshape(1, -1), used - 8, rows))
    shard_first = scatter(grid, [(first, grad_joint)], vectors)
    shard_qkv, ends = shard_first[:, : 3 * D], shard_first[:, 3 * D :]
    small = [ends[:, i][None] for i in range(8)]
    return (
        block_out,
        grad_in[None],
        small[0],
        small[1],
        shard_qkv[None],
        small[2],
        small[3],
        shard_mid[None, :, :D],
        small[4],
        small[5],
        small[6],
        shard_mid[None, :, D:],
        ends[:, 8:used].T.reshape(1, -1),
        shard_proj[None],
        small[7],
    )


def solution(mesh):
    grid = Grid(mesh)

    def local(*args):
        return local_step(grid, *args)

    placed = (
        P("fsdp", "ctx", None),
        P("fsdp", None),
        P(None, ("ctx", "fsdp")),
        P(None, ("ctx", "fsdp")),
        P(None, ("ctx", "fsdp"), None),
        P(None, ("ctx", "fsdp")),
        P(None, ("ctx", "fsdp")),
        P(None, ("ctx", "fsdp"), None),
        P(None, ("ctx", "fsdp")),
        P(None, ("ctx", "fsdp")),
        P(None, ("ctx", "fsdp")),
        P(None, ("ctx", "fsdp"), None),
        P(None, ("ctx", "fsdp")),
        P(None, ("ctx", "fsdp"), None),
        P(None, ("ctx", "fsdp")),
        P("fsdp", "ctx", None),
    )
    return jax.shard_map(
        local,
        mesh=mesh,
        in_specs=placed,
        out_specs=(
            P("fsdp", "ctx", None),
            P("fsdp", "ctx", None),
            P(None, ("ctx", "fsdp")),
            P(None, ("ctx", "fsdp")),
            P(None, ("ctx", "fsdp"), None),
            P(None, ("ctx", "fsdp")),
            P(None, ("ctx", "fsdp")),
            P(None, ("ctx", "fsdp"), None),
            P(None, ("ctx", "fsdp")),
            P(None, ("ctx", "fsdp")),
            P(None, ("ctx", "fsdp")),
            P(None, ("ctx", "fsdp"), None),
            P(None, ("ctx", "fsdp")),
            P(None, ("ctx", "fsdp"), None),
            P(None, ("ctx", "fsdp")),
        ),
        check_vma=False,
    )
```

```python
import functools

import jax
import jax.numpy as jnp
from jax import lax
from jax.experimental import pallas as pl
from jax.experimental.pallas import tpu as pltpu
from jax.sharding import PartitionSpec as P


D = 768
HEADS = 12
HEAD_DIM = 64


EPSILON = 1e-05
GELU_SCALE = 0.7978845608028654
GELU_CUBIC = 0.044715


def gelu_value(value):
    return 0.5 * value * (1.0 + jnp.tanh(GELU_SCALE * (value + GELU_CUBIC * value * value * value)))


def gelu_slope(value):
    tangent = jnp.tanh(GELU_SCALE * (value + GELU_CUBIC * value * value * value))
    return 0.5 * (1.0 + tangent) + 0.5 * value * (1.0 - tangent * tangent) * GELU_SCALE * (
        1.0 + 3.0 * GELU_CUBIC * value * value
    )


def true_positions(order, first, count, half):
    rows = first + jnp.arange(count, dtype=jnp.int32)
    blocks = rows // half
    table = blocks[:, None] == jnp.arange(order.shape[0], dtype=jnp.int32)[None, :]
    return jnp.sum(jnp.where(table, order[None, :], 0), axis=1) * half + rows % half


def norm_forward(state, gain, shift):
    centre = state - jnp.mean(state, axis=-1, keepdims=True)
    inverse = lax.rsqrt(jnp.mean(centre * centre, axis=-1, keepdims=True) + EPSILON)
    normed = centre * inverse
    return (normed * gain.astype(jnp.float32) + shift.astype(jnp.float32), normed, inverse)


def norm_backward(grad_out, normed, inverse, gain):
    scaled = grad_out * gain.astype(jnp.float32)
    return inverse * (
        scaled
        - jnp.mean(scaled, axis=-1, keepdims=True)
        - normed * jnp.mean(scaled * normed, axis=-1, keepdims=True)
    )


BF = jnp.bfloat16
F32 = jnp.float32
EXT = 128
AXES = ("ctx", "fsdp")


class Grid:
    def __init__(self, mesh):
        ctx, fsdp = mesh.shape["ctx"], mesh.shape["fsdp"]
        self.z = 4
        self.x = ctx // self.z
        self.y = fsdp // 2
        self.n = ctx * fsdp
        assert self.x == self.y and self.x * self.z == ctx

    def here(self):
        c, f = lax.axis_index("ctx"), lax.axis_index("fsdp")
        return c // self.x, c % self.x, f // 2, f % 2

    def index(self, z, x, y, k):
        return ((z % self.z * self.x + x % self.x) * self.y + y % self.y) * 2 + k % 2

    def send(self, value, move):
        pairs = [
            (self.index(z, x, y, k), self.index(*move(z, x, y, k)))
            for z in range(self.z)
            for x in range(self.x)
            for y in range(self.y)
            for k in range(2)
        ]
        return lax.ppermute(value, AXES, pairs)

    def core(self, value):
        return self.send(value, lambda z, x, y, k: (z, x, y, 1 - k))

    def along_z(self, value, step):
        return self.send(value, lambda z, x, y, k: (z + step, x, y, k))

    def along_x(self, value, step):
        return self.send(value, lambda z, x, y, k: (z, x + step, y, k))

    def first(self, value, step):
        return self.send(value, lambda z, x, y, k: (z, x + step, y, k) if k == 0 else (z, x, y + step, k))

    def second(self, value, step):
        return self.send(value, lambda z, x, y, k: (z, x, y + step, k) if k == 0 else (z, x + step, y, k))

    def z_far(self, value):
        return self.send(value, lambda z, x, y, k: (z, x, y, k) if k == 0 else (z + 1, x, y, k))

    def z_near(self, value):
        return self.send(value, lambda z, x, y, k: (z + 2, x, y, k) if k == 0 else (z + 3, x, y, k))


def gather_z(grid, shard):
    core = grid.here()[3]
    other = grid.core(shard)
    pair = jnp.where(core == 0, jnp.stack([shard, other]), jnp.stack([other, shard]))
    return grid.z_far(pair), grid.z_near(pair)


def gather(grid, lines, widths):
    base = jnp.stack(lines)
    rows = base.shape[2]
    reached = {}
    for i in range(grid.x):
        reached[i, 0] = base if i == 0 else grid.first(base, i)
        for j in range(1, grid.y):
            reached[i, j] = grid.second(reached[i, 0], j)
    own = [reached[i, j] for i in range(grid.x) for j in range(grid.y)]
    parts = own + [grid.core(part) for part in own]
    offsets = [sum(widths[:at]) for at in range(len(widths))]
    X, Y, Z = grid.x, grid.y, grid.z

    def kernel(*refs):
        ins, outs, sem = refs[: len(parts)], refs[len(parts) : -1], refs[-1]
        z, x, y, k = grid.here()
        copies = []
        for at, part in enumerate(ins):
            route = k if at < len(own) else 1 - k
            i, j = (at % len(own)) // Y, (at % len(own)) % Y
            dx = jnp.where(route == 0, i, j)
            dy = jnp.where(route == 0, j, i)
            sx, sy = (x - dx + X) % X, (y - dy + Y) % Y
            for near in range(2):
                sz = (z - 2 * near - route + Z) % Z
                place = (sz * X + sx) * Y + sy
                for out, low, width in zip(outs, offsets, widths):
                    copies.append(
                        pltpu.make_async_copy(
                            part.at[near, :, :, pl.ds(low, width)],
                            out.at[place],
                            sem.at[len(copies)],
                        )
                    )
        for copy in copies:
            copy.start()
        for copy in copies:
            copy.wait()

    whole = pl.pallas_call(
        kernel,
        in_specs=[pl.BlockSpec(memory_space=pl.ANY)] * len(parts),
        out_specs=[pl.BlockSpec(memory_space=pltpu.VMEM)] * len(widths),
        out_shape=[jax.ShapeDtypeStruct((grid.n // 2, 2, rows, width), base.dtype) for width in widths],
        scratch_shapes=[pltpu.SemaphoreType.DMA((len(parts) * 2 * len(widths),))],
        compiler_params=pltpu.CompilerParams(vmem_limit_bytes=12 * 1024 * 1024),
    )(*parts)
    return [item.reshape(grid.n * rows, width) for item, width in zip(whole, widths)]


def add_parts(terms, lead, blocks):
    rows, width = terms[0][0].shape[-2:]

    def kernel(*refs):
        total = refs[0][...].astype(F32)
        for ref in refs[1:-1]:
            total = total + ref[...].astype(F32)
        refs[-1][...] = total.astype(BF)

    return pl.pallas_call(
        kernel,
        grid=(blocks,),
        in_specs=[pl.BlockSpec((None, lead, rows, width), where) for _, where in terms],
        out_specs=pl.BlockSpec((None, lead, rows, width), lambda g: (g, 0, 0, 0)),
        out_shape=jax.ShapeDtypeStruct((blocks, lead, rows, width), BF),
        compiler_params=pltpu.CompilerParams(vmem_limit_bytes=24 * 1024 * 1024),
    )(*[array for array, _ in terms])


def scatter(grid, pairs, extra=()):
    n = grid.n
    X, Y, Z = grid.x, grid.y, grid.z
    rows = pairs[0][0].shape[1] // n
    chunk = 2 * Y * rows
    widths = [right.shape[1] for _, right in pairs]
    offsets = [sum(widths[:at]) for at in range(len(widths))]
    lefts = [left for left, _ in pairs]
    rights = [right for _, right in pairs]
    total = sum(widths) + (EXT if extra else 0)
    inputs = 2 * len(pairs) + len(extra)

    def kernel(*refs):
        left_refs, right_refs, line_refs = refs[: len(pairs)], refs[len(pairs) : 2 * len(pairs)], refs[2 * len(pairs) : inputs]
        outs, turned = refs[inputs : inputs + 2 * X], refs[inputs + 2 * X :]
        z, x, y, k = grid.here()
        for left, turn in zip(left_refs, turned):
            turn[...] = left[...].T
        if line_refs:
            lines, tail = turned[len(pairs) :]
            lines[...] = jnp.zeros(lines.shape, F32)
            at = 0
            for line in line_refs:
                lines[at : at + line.shape[0], :] = line[...]
                at += line.shape[0]
            tail[...] = lines[...].T
        for other in range(2):
            route = k if other == 0 else 1 - k

            def step(at, carry):
                near, dx = at // X, at % X
                tz, tx = (z + 2 * near + route) % Z, (x + dx) % X
                low_row = (tz * X + tx) * chunk
                if rows % 8 == 0:
                    low_row = pl.multiple_of(low_row, chunk)
                made = [
                    product(left[pl.ds(low_row, chunk), :], right[...], ((1,), (0,)))
                    for left, right in zip(turned, right_refs)
                ]
                ends = [tail[pl.ds(low_row, chunk), :]] if line_refs else []

                def store(out, ty, spot):
                    for core in range(2):
                        at = 2 * ty + core
                        span = slice(at * rows, (at + 1) * rows)
                        for value, low, width in zip(made, offsets, widths):
                            out[spot, 2 * near + core, :, low : low + width] = value[span].astype(BF)
                        for value in ends:
                            out[spot, 2 * near + core, :, sum(widths) :] = value[span].astype(BF)

                for ty in range(Y):
                    dy = (ty - y + Y) % Y
                    i = jnp.where(route == 0, dx, dy)
                    j = jnp.where(route == 0, dy, dx)
                    for at in range(X):
                        pl.when(i == at)(functools.partial(store, outs[other * X + at], ty, j))
                return carry

            lax.fori_loop(0, 2 * X, step, 0)

    shape = jax.ShapeDtypeStruct((Y, 4, rows, total), BF)
    vmem = pl.BlockSpec(memory_space=pltpu.VMEM)
    scratch = [pltpu.VMEM((left.shape[1], left.shape[0]), BF) for left in lefts]
    if extra:
        scratch += [pltpu.VMEM((EXT, n * rows), F32), pltpu.VMEM((n * rows, EXT), F32)]
    made = pl.pallas_call(
        kernel,
        in_specs=[vmem] * inputs,
        out_specs=[vmem] * (2 * X),
        out_shape=[shape] * (2 * X),
        scratch_shapes=scratch,
        compiler_params=pltpu.CompilerParams(vmem_limit_bytes=24 * 1024 * 1024),
    )(*lefts, *rights, *extra)
    mine, theirs = made[:X], made[X:]
    came = [None] * X
    for i in list(range(1, X)) + [0]:
        came[i] = grid.core(theirs[i])
    got = []
    for i in range(1, X):
        one = add_parts([(item, lambda g: (g, 0, 0, 0)) for item in (mine[i], came[i])], 4, Y)
        got.append(grid.first(one, i))

    def pick(j):
        return lambda g: (j, g, 0, 0)

    held = [mine[0], came[0]] + got
    final = [(item, 0) for item in held]
    for j in range(1, Y):
        two = add_parts([(item, pick(j)) for item in held], 2, 2).reshape(1, 4, rows, total)
        final.append((grid.second(two, j), 0))
    half = [add_parts([(item, lambda g, near=near: (0, near, 0, 0)) for item, _ in final], 2, 1)[0] for near in range(2)]
    four = [grid.z_far(half[0]), grid.z_near(half[1])]
    core = grid.here()[3]
    four = four[0].astype(F32) + four[1].astype(F32)
    kept = jnp.where(core == 0, four[0], four[1])
    sent = jnp.where(core == 0, four[1], four[0]).astype(BF)
    return kept + grid.core(sent).astype(F32)


def product(left, right, dims):
    return lax.dot_general(left, right, (dims, ((), ())), preferred_element_type=F32)


def simple(kernel, ins, outs, scratch=(), fetch=0):
    vmem = pl.BlockSpec(memory_space=pltpu.VMEM)
    held = [pltpu.VMEM(item.shape, item.dtype) for item in ins[:fetch]]

    def fetched(*refs):
        body = refs[: len(refs) - fetch - 1]
        slots, sem = refs[len(body) : -1], refs[-1]
        copies = [pltpu.make_async_copy(ref, slot, sem.at[at]) for at, (ref, slot) in enumerate(zip(body, slots))]
        for copy in copies:
            copy.start()
        for copy in copies:
            copy.wait()
        kernel(*slots, *body[fetch:])

    extra = held + [pltpu.SemaphoreType.DMA((fetch,))] if fetch else []
    return pl.pallas_call(
        fetched if fetch else kernel,
        in_specs=[pl.BlockSpec(memory_space=pltpu.HBM)] * fetch + [vmem] * (len(ins) - fetch),
        out_specs=[vmem] * len(outs),
        out_shape=[jax.ShapeDtypeStruct(shape, kind) for shape, kind in outs],
        scratch_shapes=list(scratch) + extra,
        compiler_params=pltpu.CompilerParams(vmem_limit_bytes=12 * 1024 * 1024),
    )(*ins)


def split_groups(grid, value, bias, sets):
    count, Z = value.shape[0], grid.z
    group = D // Z

    def kernel(*refs):
        outs = refs[-Z:]
        z = grid.here()[0]

        def write(first):
            for dz in range(Z):
                for part in range(sets):
                    low = part * D + (first + dz) % Z * group
                    item = refs[0][:, low : low + group]
                    if bias is not None:
                        item = item + refs[1][:, low : low + group]
                    outs[dz][:, part * group : (part + 1) * group] = item.astype(BF)

        for first in range(Z):
            pl.when(z == first)(functools.partial(write, first))

    ins = [value] if bias is None else [value, bias]
    return simple(kernel, ins, [((count, sets * group), BF)] * Z)


def join_groups(grid, pieces, sets):
    count, Z = pieces[0].shape[0], grid.z
    group = D // Z

    def kernel(*refs):
        out, sums = refs[Z:]
        z = grid.here()[0]

        def write(first):
            for dz in range(Z):
                for part in range(sets):
                    low = part * D + (first + dz) % Z * group
                    item = refs[dz][:, part * group : (part + 1) * group]
                    out[:, low : low + group] = item
                    sums[:, low : low + group] = jnp.sum(item.astype(F32), axis=0, keepdims=True)

        for first in range(Z):
            pl.when(z == first)(functools.partial(write, first))

    return simple(kernel, pieces, [((count, sets * D), BF), ((1, sets * D), F32)])


def attend(pieces, keys, query_pos, key_pos, heads):
    Z, step = len(pieces), pieces[0].shape[0]
    group = heads * HEAD_DIM
    scale = HEAD_DIM ** (-0.5)

    def kernel(*refs):
        piece_refs, row_ref, key_refs = refs[:Z], refs[Z], refs[Z + 1 : Z + 1 + len(keys)]
        col_ref, mixed_ref, lse_ref = refs[Z + 1 + len(keys) : Z + len(keys) + 4]
        sent = refs[Z + len(keys) + 4 :]
        for head in range(heads):
            low = head * HEAD_DIM
            cols = slice(low, low + HEAD_DIM)
            k = jnp.concatenate([ref[:, cols] for ref in key_refs], axis=0)
            v = jnp.concatenate([ref[:, group + low : group + low + HEAD_DIM] for ref in key_refs], axis=0)
            for at in range(Z):
                rows = slice(at * step, (at + 1) * step)
                q = piece_refs[at][:, cols]
                allowed = row_ref[rows] >= col_ref[...]
                scores = jnp.where(allowed, product(q, k, ((1,), (1,))) * scale, -jnp.inf)
                top = jnp.max(scores, axis=1, keepdims=True)
                probs = jnp.exp(scores - top)
                total = jnp.sum(probs, axis=1, keepdims=True)
                mixed = product(probs.astype(BF), v, ((1,), (0,))) / total
                mixed_ref[rows, cols] = mixed
                sent[at][:, cols] = mixed.astype(BF)
                lse_ref[rows, head : head + 1] = top + jnp.log(total)

    outs = [((Z * step, group), F32), ((Z * step, heads), F32)] + [((step, group), BF)] * Z
    made = simple(kernel, [*pieces, query_pos[:, None], *keys, key_pos[None]], outs, fetch=Z + 1)
    return made[0], made[1], made[2:]


def attend_back(pieces, keys, query_pos, key_pos, mixed, lse, grads, heads):
    Z, step = len(pieces), pieces[0].shape[0]
    group = heads * HEAD_DIM
    scale = HEAD_DIM ** (-0.5)
    own = keys[0].shape[0]
    far = len(keys)

    def kernel(*refs):
        piece_refs, key_refs = refs[:Z], refs[Z : Z + far]
        row_ref, col_ref, mixed_ref, lse_ref = refs[Z + far : Z + far + 4]
        grad_refs = refs[Z + far + 4 : 2 * Z + far + 4]
        dq_ref, own_ref = refs[2 * Z + far + 4 : 2 * Z + far + 6]
        far_refs = refs[2 * Z + far + 6 :]
        for head in range(heads):
            low = head * HEAD_DIM
            cols = slice(low, low + HEAD_DIM)
            later = slice(group + low, group + low + HEAD_DIM)
            k = jnp.concatenate([ref[:, cols] for ref in key_refs], axis=0)
            v = jnp.concatenate([ref[:, later] for ref in key_refs], axis=0)
            dk = jnp.zeros((own * far, HEAD_DIM), F32)
            dv = jnp.zeros((own * far, HEAD_DIM), F32)
            for at in range(Z):
                rows = slice(at * step, (at + 1) * step)
                q = piece_refs[at][:, cols]
                g = grad_refs[at][:, cols]
                delta = jnp.sum(g.astype(F32) * mixed_ref[rows, cols], axis=1, keepdims=True)
                allowed = row_ref[rows] >= col_ref[...]
                scores = product(q, k, ((1,), (1,))) * scale
                soft = jnp.where(allowed, jnp.exp(scores - lse_ref[rows, head : head + 1]), 0.0)
                inner = product(g, v, ((1,), (1,)))
                slope = (soft * (inner - delta)).astype(BF)
                dq_ref[rows, cols] = (product(slope, k, ((1,), (0,))) * scale).astype(BF)
                dk = dk + product(slope, q, ((0,), (0,)))
                dv = dv + product(soft.astype(BF), g, ((0,), (0,)))
            dk = dk * scale
            own_ref[:, cols] = dk[:own]
            own_ref[:, later] = dv[:own]
            for at, ref in enumerate(far_refs):
                piece = slice((at + 1) * own, (at + 2) * own)
                ref[:, cols] = dk[piece].astype(BF)
                ref[:, later] = dv[piece].astype(BF)

    outs = [((Z * step, group), BF), ((own, 2 * group), F32)] + [((own, 2 * group), BF)] * (far - 1)
    ins = [*pieces, *keys, query_pos[:, None], key_pos[None], mixed, lse, *grads]
    made = simple(kernel, ins, outs)
    return made[0], made[1], made[2:]


def return_pieces(grad_q, own, came, Z):
    step, group = grad_q.shape[0] // Z, grad_q.shape[1]

    def kernel(*refs):
        outs = refs[-Z:]
        for at, out in enumerate(outs):
            rows = slice(at * step, (at + 1) * step)
            out[:, :group] = refs[0][rows]
            total = refs[1][rows]
            for ref in refs[2:-Z]:
                total = total + ref[rows].astype(F32)
            out[:, group:] = total.astype(BF)

    return simple(kernel, [grad_q, own, *came], [((step, 3 * group), BF)] * Z)


def unpack_lines(extra, used, rows):
    spare = used - 8
    n = extra.shape[0] // rows

    def kernel(extra_ref, lines_ref, up_ref, joint_ref, turned):
        turned[...] = extra_ref[...].astype(F32).T
        lines_ref[...] = turned[:8]
        joint_ref[:, :D] = turned[2:3]
        joint_ref[:, D : 2 * D] = jnp.zeros((1, D), F32)
        joint_ref[:, 2 * D :] = turned[3:4]
        for at in range(n):
            for part in range(spare):
                low = (at * spare + part) * rows
                up_ref[:, low : low + rows] = turned[8 + part : 9 + part, at * rows : (at + 1) * rows]

    outs = [((8, D), F32), ((1, spare * D), F32), ((1, 3 * D), F32)]
    return simple(kernel, [extra], outs, [pltpu.VMEM((EXT, D), F32)])


def fold_lines(vector, spare, rows):
    n = D // rows

    def kernel(vector_ref, out_ref):
        for at in range(n):
            for part in range(spare):
                low = (at * spare + part) * rows
                out_ref[part : part + 1, at * rows : (at + 1) * rows] = vector_ref[:, low : low + rows]

    return simple(kernel, [vector], [((spare, D), F32)])[0]


def pack_first(w_qkv, lines, spare, rows):
    width = w_qkv.shape[1]
    used = len(lines) + spare.shape[1] // rows

    def kernel(*refs):
        out = refs[-1]
        out[:, :width] = refs[0][...]
        items = [ref[...] for ref in refs[2:-1]]
        items += [refs[1][:, at * rows : (at + 1) * rows] for at in range(used - len(lines))]
        stacked = jnp.concatenate([item.astype(F32) for item in items] + [jnp.zeros((EXT - used, rows), F32)], axis=0)
        across = lax.broadcasted_iota(jnp.int32, (rows, rows), 0) == lax.broadcasted_iota(jnp.int32, (rows, rows), 1)
        out[:, width:] = product(across.astype(BF), stacked.astype(BF), ((1,), (1,))).astype(BF)

    return simple(kernel, [w_qkv, spare, *lines], [((rows, width + EXT), BF)], fetch=len(lines) + 2)[0]


def local_step(
    grid,
    tokens,
    block_order,
    attn_gain,
    attn_shift,
    w_qkv,
    query_bias,
    value_bias,
    w_out,
    out_bias,
    mlp_gain,
    mlp_shift,
    w_fc,
    fc_bias,
    w_proj,
    proj_bias,
    cotangent,
):
    count = tokens.shape[1]
    half = count // 2
    order = block_order[0]
    Z, X = grid.z, grid.x
    z, x, _, _ = grid.here()
    group = D // Z
    heads = HEADS // Z

    rows = w_qkv.shape[1]
    small = [attn_gain, attn_shift, query_bias, value_bias, out_bias, mlp_gain, mlp_shift, proj_bias]
    used = 8 + fc_bias.shape[1] // rows
    first_z = gather_z(grid, pack_first(w_qkv[0], small, fc_bias, rows))
    mid_z = gather_z(grid, jnp.concatenate([w_out[0], w_fc[0]], axis=1))
    last_z = gather_z(grid, w_proj[0])
    w_joint, extra = gather(grid, first_z, [3 * D, EXT])
    w_mix, w_up = gather(grid, mid_z, [D, w_fc.shape[2]])
    lines, bias_up, joint_bias = unpack_lines(extra, used, rows)
    gain_one, shift_one, _, _, bias_mix, gain_two, shift_two, bias_down = [lines[i : i + 1] for i in range(8)]

    def positions(dz, dx):
        owner = (z - dz + Z) % Z * X + (x - dx + X) % X
        return true_positions(order, owner * count, count, half)

    query_pos = jnp.concatenate([positions(dz, 0) for dz in range(Z)])
    key_pos = jnp.concatenate([positions(dz, dx) for dx in range(X) for dz in range(Z)])

    def spread(pieces):
        return [pieces[0]] + [grid.along_z(pieces[dz], dz) for dz in range(1, Z)]

    def collect(pieces):
        return [pieces[0]] + [grid.along_z(pieces[dz], -dz) for dz in range(1, Z)]

    state = tokens[0].astype(F32)
    normed_in, normed_one, inverse_one = norm_forward(state, gain_one, shift_one)
    first = normed_in.astype(BF)
    joint = jnp.dot(first, w_joint, preferred_element_type=F32)
    packed = spread(split_groups(grid, joint, joint_bias, 3))
    own_keys = jnp.concatenate([piece[:, group:] for piece in packed])
    all_keys = [own_keys] + [grid.along_x(own_keys, dx) for dx in range(1, X)]
    mixed_local, log_total, mixed_send = attend(packed, all_keys, query_pos, key_pos, heads)
    (w_down,) = gather(grid, last_z, [D])
    mixed_round, _ = join_groups(grid, collect(mixed_send), 1)

    middle = state + jnp.dot(mixed_round, w_mix, preferred_element_type=F32) + bias_mix.astype(F32)
    normed_mid, normed_two, inverse_two = norm_forward(middle, gain_two, shift_two)
    second = normed_mid.astype(BF)
    pre = jnp.dot(second, w_up, preferred_element_type=F32) + bias_up.astype(F32)
    hidden = gelu_value(pre).astype(BF)
    result = middle + jnp.dot(hidden, w_down, preferred_element_type=F32) + bias_down.astype(F32)
    block_out = result.astype(BF)[None]

    grad_state = cotangent[0]
    grad_proj_bias = jnp.sum(grad_state, axis=0)
    grad_round = grad_state.astype(BF)
    shard_proj = scatter(grid, [(hidden, grad_round)])
    grad_pre = jnp.einsum("td,fd->tf", grad_round, w_down, preferred_element_type=F32) * gelu_slope(pre)
    grad_fc_bias = jnp.sum(grad_pre, axis=0)
    grad_pre_round = grad_pre.astype(BF)
    grad_second = jnp.einsum("tf,df->td", grad_pre_round, w_up, preferred_element_type=F32)
    grad_mlp_gain = jnp.sum(grad_second * normed_two, axis=0)
    grad_mlp_shift = jnp.sum(grad_second, axis=0)
    grad_middle = grad_state + norm_backward(grad_second, normed_two, inverse_two, gain_two)
    grad_out_bias = jnp.sum(grad_middle, axis=0)
    middle_round = grad_middle.astype(BF)
    shard_mid = scatter(grid, [(mixed_round, middle_round), (second, grad_pre_round)])
    grad_mixed = jnp.einsum("td,cd->tc", middle_round, w_mix, preferred_element_type=F32).astype(BF)

    grad_local = spread(split_groups(grid, grad_mixed, None, 1))
    grad_q, grad_own, grad_far = attend_back(
        packed, all_keys, query_pos, key_pos, mixed_local, log_total, grad_local, heads
    )
    came = [grid.along_x(grad_far[dx - 1], -dx) for dx in range(1, X)]
    back = collect(return_pieces(grad_q, grad_own, came, Z))
    grad_joint, joint_sums = join_groups(grid, back, 3)
    grad_query_bias = joint_sums[:, :D]
    grad_value_bias = joint_sums[:, 2 * D :]
    grad_first = jnp.einsum("te,de->td", grad_joint, w_joint, preferred_element_type=F32)
    grad_attn_gain = jnp.sum(grad_first * normed_one, axis=0)
    grad_attn_shift = jnp.sum(grad_first, axis=0)
    grad_in = grad_middle + norm_backward(grad_first, normed_one, inverse_one, gain_one)

    vectors = [
        grad_attn_gain,
        grad_attn_shift,
        grad_query_bias,
        grad_value_bias,
        grad_out_bias,
        grad_mlp_gain,
        grad_mlp_shift,
        grad_proj_bias,
    ]
    vectors = [item.reshape(1, D) for item in vectors]
    vectors.append(fold_lines(grad_fc_bias.reshape(1, -1), used - 8, rows))
    shard_first = scatter(grid, [(first, grad_joint)], vectors)
    shard_qkv, ends = shard_first[:, : 3 * D], shard_first[:, 3 * D :]
    small = [ends[:, i][None] for i in range(8)]
    return (
        block_out,
        grad_in[None],
        small[0],
        small[1],
        shard_qkv[None],
        small[2],
        small[3],
        shard_mid[None, :, :D],
        small[4],
        small[5],
        small[6],
        shard_mid[None, :, D:],
        ends[:, 8:used].T.reshape(1, -1),
        shard_proj[None],
        small[7],
    )


def solution(mesh):
    grid = Grid(mesh)

    def local(*args):
        return local_step(grid, *args)

    placed = (
        P("fsdp", "ctx", None),
        P("fsdp", None),
        P(None, ("ctx", "fsdp")),
        P(None, ("ctx", "fsdp")),
        P(None, ("ctx", "fsdp"), None),
        P(None, ("ctx", "fsdp")),
        P(None, ("ctx", "fsdp")),
        P(None, ("ctx", "fsdp"), None),
        P(None, ("ctx", "fsdp")),
        P(None, ("ctx", "fsdp")),
        P(None, ("ctx", "fsdp")),
        P(None, ("ctx", "fsdp"), None),
        P(None, ("ctx", "fsdp")),
        P(None, ("ctx", "fsdp"), None),
        P(None, ("ctx", "fsdp")),
        P("fsdp", "ctx", None),
    )
    return jax.shard_map(
        local,
        mesh=mesh,
        in_specs=placed,
        out_specs=(
            P("fsdp", "ctx", None),
            P("fsdp", "ctx", None),
            P(None, ("ctx", "fsdp")),
            P(None, ("ctx", "fsdp")),
            P(None, ("ctx", "fsdp"), None),
            P(None, ("ctx", "fsdp")),
            P(None, ("ctx", "fsdp")),
            P(None, ("ctx", "fsdp"), None),
            P(None, ("ctx", "fsdp")),
            P(None, ("ctx", "fsdp")),
            P(None, ("ctx", "fsdp")),
            P(None, ("ctx", "fsdp"), None),
            P(None, ("ctx", "fsdp")),
            P(None, ("ctx", "fsdp"), None),
            P(None, ("ctx", "fsdp")),
        ),
        check_vma=False,
    )
```

```python
import functools

import jax
import jax.numpy as jnp
from jax import lax
from jax.experimental import pallas as pl
from jax.experimental.pallas import tpu as pltpu
from jax.sharding import PartitionSpec as P


D = 768
HEADS = 12
HEAD_DIM = 64


EPSILON = 1e-05
GELU_SCALE = 0.7978845608028654
GELU_CUBIC = 0.044715


def gelu_value(value):
    return 0.5 * value * (1.0 + jnp.tanh(GELU_SCALE * (value + GELU_CUBIC * value * value * value)))


def gelu_slope(value):
    tangent = jnp.tanh(GELU_SCALE * (value + GELU_CUBIC * value * value * value))
    return 0.5 * (1.0 + tangent) + 0.5 * value * (1.0 - tangent * tangent) * GELU_SCALE * (
        1.0 + 3.0 * GELU_CUBIC * value * value
    )


def true_positions(order, first, count, half):
    rows = first + jnp.arange(count, dtype=jnp.int32)
    blocks = rows // half
    table = blocks[:, None] == jnp.arange(order.shape[0], dtype=jnp.int32)[None, :]
    return jnp.sum(jnp.where(table, order[None, :], 0), axis=1) * half + rows % half


def norm_forward(state, gain, shift):
    centre = state - jnp.mean(state, axis=-1, keepdims=True)
    inverse = lax.rsqrt(jnp.mean(centre * centre, axis=-1, keepdims=True) + EPSILON)
    normed = centre * inverse
    return (normed * gain.astype(jnp.float32) + shift.astype(jnp.float32), normed, inverse)


def norm_backward(grad_out, normed, inverse, gain):
    scaled = grad_out * gain.astype(jnp.float32)
    return inverse * (
        scaled
        - jnp.mean(scaled, axis=-1, keepdims=True)
        - normed * jnp.mean(scaled * normed, axis=-1, keepdims=True)
    )


BF = jnp.bfloat16
F32 = jnp.float32
EXT = 128
AXES = ("ctx", "fsdp")


class Grid:
    def __init__(self, mesh):
        ctx, fsdp = mesh.shape["ctx"], mesh.shape["fsdp"]
        self.z = 4
        self.x = ctx // self.z
        self.y = fsdp // 2
        self.n = ctx * fsdp
        assert self.x == self.y and self.x * self.z == ctx

    def here(self):
        c, f = lax.axis_index("ctx"), lax.axis_index("fsdp")
        return c // self.x, c % self.x, f // 2, f % 2

    def index(self, z, x, y, k):
        return ((z % self.z * self.x + x % self.x) * self.y + y % self.y) * 2 + k % 2

    def send(self, value, move):
        pairs = [
            (self.index(z, x, y, k), self.index(*move(z, x, y, k)))
            for z in range(self.z)
            for x in range(self.x)
            for y in range(self.y)
            for k in range(2)
        ]
        return lax.ppermute(value, AXES, pairs)

    def core(self, value):
        return self.send(value, lambda z, x, y, k: (z, x, y, 1 - k))

    def along_z(self, value, step):
        return self.send(value, lambda z, x, y, k: (z + step, x, y, k))

    def along_x(self, value, step):
        return self.send(value, lambda z, x, y, k: (z, x + step, y, k))

    def first(self, value, step):
        return self.send(value, lambda z, x, y, k: (z, x + step, y, k) if k == 0 else (z, x, y + step, k))

    def second(self, value, step):
        return self.send(value, lambda z, x, y, k: (z, x, y + step, k) if k == 0 else (z, x + step, y, k))

    def z_far(self, value):
        return self.send(value, lambda z, x, y, k: (z, x, y, k) if k == 0 else (z + 1, x, y, k))

    def z_near(self, value):
        return self.send(value, lambda z, x, y, k: (z + 2, x, y, k) if k == 0 else (z + 3, x, y, k))


def gather_z(grid, shard):
    core = grid.here()[3]
    other = grid.core(shard)
    pair = jnp.where(core == 0, jnp.stack([shard, other]), jnp.stack([other, shard]))
    return grid.z_far(pair), grid.z_near(pair)


def gather(grid, lines, widths):
    base = jnp.stack(lines)
    rows = base.shape[2]
    reached = {}
    for i in range(grid.x):
        reached[i, 0] = base if i == 0 else grid.first(base, i)
        for j in range(1, grid.y):
            reached[i, j] = grid.second(reached[i, 0], j)
    own = [reached[i, j] for i in range(grid.x) for j in range(grid.y)]
    parts = own + [grid.core(part) for part in own]
    offsets = [sum(widths[:at]) for at in range(len(widths))]
    X, Y, Z = grid.x, grid.y, grid.z

    def kernel(*refs):
        ins, outs, sem = refs[: len(parts)], refs[len(parts) : -1], refs[-1]
        z, x, y, k = grid.here()
        copies = []
        for at, part in enumerate(ins):
            route = k if at < len(own) else 1 - k
            i, j = (at % len(own)) // Y, (at % len(own)) % Y
            dx = jnp.where(route == 0, i, j)
            dy = jnp.where(route == 0, j, i)
            sx, sy = (x - dx + X) % X, (y - dy + Y) % Y
            for near in range(2):
                sz = (z - 2 * near - route + Z) % Z
                place = (sz * X + sx) * Y + sy
                for out, low, width in zip(outs, offsets, widths):
                    copies.append(
                        pltpu.make_async_copy(
                            part.at[near, :, :, pl.ds(low, width)],
                            out.at[place],
                            sem.at[len(copies)],
                        )
                    )
        for copy in copies:
            copy.start()
        for copy in copies:
            copy.wait()

    whole = pl.pallas_call(
        kernel,
        in_specs=[pl.BlockSpec(memory_space=pl.ANY)] * len(parts),
        out_specs=[pl.BlockSpec(memory_space=pltpu.VMEM)] * len(widths),
        out_shape=[jax.ShapeDtypeStruct((grid.n // 2, 2, rows, width), base.dtype) for width in widths],
        scratch_shapes=[pltpu.SemaphoreType.DMA((len(parts) * 2 * len(widths),))],
        compiler_params=pltpu.CompilerParams(vmem_limit_bytes=12 * 1024 * 1024),
    )(*parts)
    return [item.reshape(grid.n * rows, width) for item, width in zip(whole, widths)]


def add_parts(terms, lead, blocks):
    rows, width = terms[0][0].shape[-2:]

    def kernel(*refs):
        total = refs[0][...].astype(F32)
        for ref in refs[1:-1]:
            total = total + ref[...].astype(F32)
        refs[-1][...] = total.astype(BF)

    return pl.pallas_call(
        kernel,
        grid=(blocks,),
        in_specs=[pl.BlockSpec((None, lead, rows, width), where) for _, where in terms],
        out_specs=pl.BlockSpec((None, lead, rows, width), lambda g: (g, 0, 0, 0)),
        out_shape=jax.ShapeDtypeStruct((blocks, lead, rows, width), BF),
        compiler_params=pltpu.CompilerParams(vmem_limit_bytes=24 * 1024 * 1024),
    )(*[array for array, _ in terms])


def scatter(grid, pairs, extra=()):
    n = grid.n
    X, Y, Z = grid.x, grid.y, grid.z
    rows = pairs[0][0].shape[1] // n
    chunk = 2 * Y * rows
    widths = [right.shape[1] for _, right in pairs]
    offsets = [sum(widths[:at]) for at in range(len(widths))]
    lefts = [left for left, _ in pairs]
    rights = [right for _, right in pairs]
    total = sum(widths) + (EXT if extra else 0)
    inputs = 2 * len(pairs) + len(extra)

    def kernel(*refs):
        left_refs, right_refs, line_refs = refs[: len(pairs)], refs[len(pairs) : 2 * len(pairs)], refs[2 * len(pairs) : inputs]
        outs, turned = refs[inputs : inputs + 2 * X], refs[inputs + 2 * X :]
        z, x, y, k = grid.here()
        for left, turn in zip(left_refs, turned):
            turn[...] = left[...].T
        if line_refs:
            lines, tail = turned[len(pairs) :]
            lines[...] = jnp.zeros(lines.shape, F32)
            at = 0
            for line in line_refs:
                lines[at : at + line.shape[0], :] = line[...]
                at += line.shape[0]
            tail[...] = lines[...].T
        for other in range(2):
            route = k if other == 0 else 1 - k

            def step(at, carry):
                near, dx = at // X, at % X
                tz, tx = (z + 2 * near + route) % Z, (x + dx) % X
                low_row = (tz * X + tx) * chunk
                if rows % 8 == 0:
                    low_row = pl.multiple_of(low_row, chunk)
                made = [
                    product(left[pl.ds(low_row, chunk), :], right[...], ((1,), (0,)))
                    for left, right in zip(turned, right_refs)
                ]
                ends = [tail[pl.ds(low_row, chunk), :]] if line_refs else []

                def store(out, ty, spot):
                    for core in range(2):
                        at = 2 * ty + core
                        span = slice(at * rows, (at + 1) * rows)
                        for value, low, width in zip(made, offsets, widths):
                            out[spot, 2 * near + core, :, low : low + width] = value[span].astype(BF)
                        for value in ends:
                            out[spot, 2 * near + core, :, sum(widths) :] = value[span].astype(BF)

                for ty in range(Y):
                    dy = (ty - y + Y) % Y
                    i = jnp.where(route == 0, dx, dy)
                    j = jnp.where(route == 0, dy, dx)
                    for at in range(X):
                        pl.when(i == at)(functools.partial(store, outs[other * X + at], ty, j))
                return carry

            lax.fori_loop(0, 2 * X, step, 0)

    shape = jax.ShapeDtypeStruct((Y, 4, rows, total), BF)
    vmem = pl.BlockSpec(memory_space=pltpu.VMEM)
    scratch = [pltpu.VMEM((left.shape[1], left.shape[0]), BF) for left in lefts]
    if extra:
        scratch += [pltpu.VMEM((EXT, n * rows), F32), pltpu.VMEM((n * rows, EXT), F32)]
    made = pl.pallas_call(
        kernel,
        in_specs=[vmem] * inputs,
        out_specs=[vmem] * (2 * X),
        out_shape=[shape] * (2 * X),
        scratch_shapes=scratch,
        compiler_params=pltpu.CompilerParams(vmem_limit_bytes=24 * 1024 * 1024),
    )(*lefts, *rights, *extra)
    mine, theirs = made[:X], made[X:]
    came = [None] * X
    for i in list(range(1, X)) + [0]:
        came[i] = grid.core(theirs[i])
    got = []
    for i in range(1, X):
        one = add_parts([(item, lambda g: (g, 0, 0, 0)) for item in (mine[i], came[i])], 4, Y)
        got.append(grid.first(one, i))

    def pick(j):
        return lambda g: (j, g, 0, 0)

    held = [mine[0], came[0]] + got
    final = [(item, 0) for item in held]
    for j in range(1, Y):
        two = add_parts([(item, pick(j)) for item in held], 2, 2).reshape(1, 4, rows, total)
        final.append((grid.second(two, j), 0))
    half = [add_parts([(item, lambda g, near=near: (0, near, 0, 0)) for item, _ in final], 2, 1)[0] for near in range(2)]
    four = [grid.z_far(half[0]), grid.z_near(half[1])]
    core = grid.here()[3]
    four = four[0].astype(F32) + four[1].astype(F32)
    kept = jnp.where(core == 0, four[0], four[1])
    sent = jnp.where(core == 0, four[1], four[0]).astype(BF)
    return kept + grid.core(sent).astype(F32)


def product(left, right, dims):
    return lax.dot_general(left, right, (dims, ((), ())), preferred_element_type=F32)


def simple(kernel, ins, outs, scratch=(), fetch=0):
    vmem = pl.BlockSpec(memory_space=pltpu.VMEM)
    held = [pltpu.VMEM(item.shape, item.dtype) for item in ins[:fetch]]

    def fetched(*refs):
        body = refs[: len(refs) - fetch - 1]
        slots, sem = refs[len(body) : -1], refs[-1]
        copies = [pltpu.make_async_copy(ref, slot, sem.at[at]) for at, (ref, slot) in enumerate(zip(body, slots))]
        for copy in copies:
            copy.start()
        for copy in copies:
            copy.wait()
        kernel(*slots, *body[fetch:])

    extra = held + [pltpu.SemaphoreType.DMA((fetch,))] if fetch else []
    return pl.pallas_call(
        fetched if fetch else kernel,
        in_specs=[pl.BlockSpec(memory_space=pltpu.HBM)] * fetch + [vmem] * (len(ins) - fetch),
        out_specs=[vmem] * len(outs),
        out_shape=[jax.ShapeDtypeStruct(shape, kind) for shape, kind in outs],
        scratch_shapes=list(scratch) + extra,
        compiler_params=pltpu.CompilerParams(vmem_limit_bytes=12 * 1024 * 1024),
    )(*ins)


def split_groups(grid, value, bias, sets):
    count, Z = value.shape[0], grid.z
    group = D // Z

    def kernel(*refs):
        outs = refs[-Z:]
        z = grid.here()[0]

        def write(first):
            for dz in range(Z):
                for part in range(sets):
                    low = part * D + (first + dz) % Z * group
                    item = refs[0][:, low : low + group]
                    if bias is not None:
                        item = item + refs[1][:, low : low + group]
                    outs[dz][:, part * group : (part + 1) * group] = item.astype(BF)

        for first in range(Z):
            pl.when(z == first)(functools.partial(write, first))

    ins = [value] if bias is None else [value, bias]
    return simple(kernel, ins, [((count, sets * group), BF)] * Z)


def join_groups(grid, pieces, sets):
    count, Z = pieces[0].shape[0], grid.z
    group = D // Z

    def kernel(*refs):
        out, sums = refs[Z:]
        z = grid.here()[0]

        def write(first):
            for dz in range(Z):
                for part in range(sets):
                    low = part * D + (first + dz) % Z * group
                    item = refs[dz][:, part * group : (part + 1) * group]
                    out[:, low : low + group] = item
                    sums[:, low : low + group] = jnp.sum(item.astype(F32), axis=0, keepdims=True)

        for first in range(Z):
            pl.when(z == first)(functools.partial(write, first))

    return simple(kernel, pieces, [((count, sets * D), BF), ((1, sets * D), F32)])


def attend(pieces, keys, query_pos, key_pos, heads):
    Z, step = len(pieces), pieces[0].shape[0]
    group = heads * HEAD_DIM
    scale = HEAD_DIM ** (-0.5)

    def kernel(*refs):
        piece_refs, row_ref, key_refs = refs[:Z], refs[Z], refs[Z + 1 : Z + 1 + len(keys)]
        col_ref, mixed_ref, lse_ref = refs[Z + 1 + len(keys) : Z + len(keys) + 4]
        sent = refs[Z + len(keys) + 4 :]
        for head in range(heads):
            low = head * HEAD_DIM
            cols = slice(low, low + HEAD_DIM)
            k = jnp.concatenate([ref[:, cols] for ref in key_refs], axis=0)
            v = jnp.concatenate([ref[:, group + low : group + low + HEAD_DIM] for ref in key_refs], axis=0)
            for at in range(Z):
                rows = slice(at * step, (at + 1) * step)
                q = piece_refs[at][:, cols]
                allowed = row_ref[rows] >= col_ref[...]
                scores = jnp.where(allowed, product(q, k, ((1,), (1,))) * scale, -jnp.inf)
                top = jnp.max(scores, axis=1, keepdims=True)
                probs = jnp.exp(scores - top)
                total = jnp.sum(probs, axis=1, keepdims=True)
                mixed = product(probs.astype(BF), v, ((1,), (0,))) / total
                mixed_ref[rows, cols] = mixed
                sent[at][:, cols] = mixed.astype(BF)
                lse_ref[rows, head : head + 1] = top + jnp.log(total)

    outs = [((Z * step, group), F32), ((Z * step, heads), F32)] + [((step, group), BF)] * Z
    made = simple(kernel, [*pieces, query_pos[:, None], *keys, key_pos[None]], outs, fetch=Z + 1)
    return made[0], made[1], made[2:]


def attend_back(pieces, keys, query_pos, key_pos, mixed, lse, grads, heads):
    Z, step = len(pieces), pieces[0].shape[0]
    group = heads * HEAD_DIM
    scale = HEAD_DIM ** (-0.5)
    own = keys[0].shape[0]
    far = len(keys)

    def kernel(*refs):
        piece_refs, key_refs = refs[:Z], refs[Z : Z + far]
        row_ref, col_ref, mixed_ref, lse_ref = refs[Z + far : Z + far + 4]
        grad_refs = refs[Z + far + 4 : 2 * Z + far + 4]
        dq_ref, own_ref = refs[2 * Z + far + 4 : 2 * Z + far + 6]
        far_refs = refs[2 * Z + far + 6 :]
        for head in range(heads):
            low = head * HEAD_DIM
            cols = slice(low, low + HEAD_DIM)
            later = slice(group + low, group + low + HEAD_DIM)
            k = jnp.concatenate([ref[:, cols] for ref in key_refs], axis=0)
            v = jnp.concatenate([ref[:, later] for ref in key_refs], axis=0)
            dk = jnp.zeros((own * far, HEAD_DIM), F32)
            dv = jnp.zeros((own * far, HEAD_DIM), F32)
            for at in range(Z):
                rows = slice(at * step, (at + 1) * step)
                q = piece_refs[at][:, cols]
                g = grad_refs[at][:, cols]
                delta = jnp.sum(g.astype(F32) * mixed_ref[rows, cols], axis=1, keepdims=True)
                allowed = row_ref[rows] >= col_ref[...]
                scores = product(q, k, ((1,), (1,))) * scale
                soft = jnp.where(allowed, jnp.exp(scores - lse_ref[rows, head : head + 1]), 0.0)
                inner = product(g, v, ((1,), (1,)))
                slope = (soft * (inner - delta)).astype(BF)
                dq_ref[rows, cols] = (product(slope, k, ((1,), (0,))) * scale).astype(BF)
                dk = dk + product(slope, q, ((0,), (0,)))
                dv = dv + product(soft.astype(BF), g, ((0,), (0,)))
            dk = dk * scale
            own_ref[:, cols] = dk[:own]
            own_ref[:, later] = dv[:own]
            for at, ref in enumerate(far_refs):
                piece = slice((at + 1) * own, (at + 2) * own)
                ref[:, cols] = dk[piece].astype(BF)
                ref[:, later] = dv[piece].astype(BF)

    outs = [((Z * step, group), BF), ((own, 2 * group), F32)] + [((own, 2 * group), BF)] * (far - 1)
    ins = [*pieces, *keys, query_pos[:, None], key_pos[None], mixed, lse, *grads]
    made = simple(kernel, ins, outs)
    return made[0], made[1], made[2:]


def return_pieces(grad_q, own, came, Z):
    step, group = grad_q.shape[0] // Z, grad_q.shape[1]

    def kernel(*refs):
        outs = refs[-Z:]
        for at, out in enumerate(outs):
            rows = slice(at * step, (at + 1) * step)
            out[:, :group] = refs[0][rows]
            total = refs[1][rows]
            for ref in refs[2:-Z]:
                total = total + ref[rows].astype(F32)
            out[:, group:] = total.astype(BF)

    return simple(kernel, [grad_q, own, *came], [((step, 3 * group), BF)] * Z)


def unpack_lines(extra, used, rows):
    spare = used - 8
    n = extra.shape[0] // rows

    def kernel(extra_ref, lines_ref, up_ref, joint_ref, turned):
        turned[...] = extra_ref[...].astype(F32).T
        lines_ref[...] = turned[:8]
        joint_ref[:, :D] = turned[2:3]
        joint_ref[:, D : 2 * D] = jnp.zeros((1, D), F32)
        joint_ref[:, 2 * D :] = turned[3:4]
        for at in range(n):
            for part in range(spare):
                low = (at * spare + part) * rows
                up_ref[:, low : low + rows] = turned[8 + part : 9 + part, at * rows : (at + 1) * rows]

    outs = [((8, D), F32), ((1, spare * D), F32), ((1, 3 * D), F32)]
    return simple(kernel, [extra], outs, [pltpu.VMEM((EXT, D), F32)])


def fold_lines(vector, spare, rows):
    n = D // rows

    def kernel(vector_ref, out_ref):
        for at in range(n):
            for part in range(spare):
                low = (at * spare + part) * rows
                out_ref[part : part + 1, at * rows : (at + 1) * rows] = vector_ref[:, low : low + rows]

    return simple(kernel, [vector], [((spare, D), F32)])[0]


def pack_first(w_qkv, lines, spare, rows):
    width = w_qkv.shape[1]
    count = lines.shape[0]
    used = count + spare.shape[1] // rows

    def kernel(*refs):
        out = refs[-1]
        out[:, :width] = refs[0][...]
        items = [refs[2][...]]
        items += [refs[1][:, at * rows : (at + 1) * rows] for at in range(used - count)]
        stacked = jnp.concatenate([item.astype(F32) for item in items] + [jnp.zeros((EXT - used, rows), F32)], axis=0)
        across = lax.broadcasted_iota(jnp.int32, (rows, rows), 0) == lax.broadcasted_iota(jnp.int32, (rows, rows), 1)
        out[:, width:] = product(across.astype(BF), stacked.astype(BF), ((1,), (1,))).astype(BF)

    return simple(kernel, [w_qkv, spare, lines], [((rows, width + EXT), BF)])[0]


def pack_keys(pieces):
    step, group = pieces[0].shape[0], pieces[0].shape[1] // 3

    def kernel(*refs):
        for at, ref in enumerate(refs[:-1]):
            refs[-1][at * step : (at + 1) * step, :] = ref[:, group:]

    return simple(kernel, pieces, [((len(pieces) * step, 2 * group), BF)], fetch=len(pieces))[0]


def local_step(
    grid,
    tokens,
    block_order,
    attn_gain,
    attn_shift,
    w_qkv,
    query_bias,
    value_bias,
    w_out,
    out_bias,
    mlp_gain,
    mlp_shift,
    w_fc,
    fc_bias,
    w_proj,
    proj_bias,
    cotangent,
):
    count = tokens.shape[1]
    half = count // 2
    order = block_order[0]
    Z, X = grid.z, grid.x
    z, x, _, _ = grid.here()
    heads = HEADS // Z

    rows = w_qkv.shape[1]
    small = [attn_gain, attn_shift, query_bias, value_bias, out_bias, mlp_gain, mlp_shift, proj_bias]
    used = 8 + fc_bias.shape[1] // rows
    first_z = gather_z(grid, pack_first(w_qkv[0], jnp.concatenate(small), fc_bias, rows))
    mid_z = gather_z(grid, jnp.concatenate([w_out[0], w_fc[0]], axis=1))
    last_z = gather_z(grid, w_proj[0])
    w_joint, extra = gather(grid, first_z, [3 * D, EXT])
    w_mix, w_up = gather(grid, mid_z, [D, w_fc.shape[2]])
    lines, bias_up, joint_bias = unpack_lines(extra, used, rows)
    gain_one, shift_one, _, _, bias_mix, gain_two, shift_two, bias_down = [lines[i : i + 1] for i in range(8)]

    def positions(dz, dx):
        owner = (z - dz + Z) % Z * X + (x - dx + X) % X
        return true_positions(order, owner * count, count, half)

    query_pos = jnp.concatenate([positions(dz, 0) for dz in range(Z)])
    key_pos = jnp.concatenate([positions(dz, dx) for dx in range(X) for dz in range(Z)])

    def spread(pieces):
        return [pieces[0]] + [grid.along_z(pieces[dz], dz) for dz in range(1, Z)]

    def collect(pieces):
        return [pieces[0]] + [grid.along_z(pieces[dz], -dz) for dz in range(1, Z)]

    state = tokens[0].astype(F32)
    normed_in, normed_one, inverse_one = norm_forward(state, gain_one, shift_one)
    first = normed_in.astype(BF)
    joint = jnp.dot(first, w_joint, preferred_element_type=F32)
    packed = spread(split_groups(grid, joint, joint_bias, 3))
    own_keys = pack_keys(packed)
    all_keys = [own_keys] + [grid.along_x(own_keys, dx) for dx in range(1, X)]
    mixed_local, log_total, mixed_send = attend(packed, all_keys, query_pos, key_pos, heads)
    (w_down,) = gather(grid, last_z, [D])
    mixed_round, _ = join_groups(grid, collect(mixed_send), 1)

    middle = state + jnp.dot(mixed_round, w_mix, preferred_element_type=F32) + bias_mix.astype(F32)
    normed_mid, normed_two, inverse_two = norm_forward(middle, gain_two, shift_two)
    second = normed_mid.astype(BF)
    pre = jnp.dot(second, w_up, preferred_element_type=F32) + bias_up.astype(F32)
    hidden = gelu_value(pre).astype(BF)
    result = middle + jnp.dot(hidden, w_down, preferred_element_type=F32) + bias_down.astype(F32)
    block_out = result.astype(BF)[None]

    grad_state = cotangent[0]
    grad_proj_bias = jnp.sum(grad_state, axis=0)
    grad_round = grad_state.astype(BF)
    shard_proj = scatter(grid, [(hidden, grad_round)])
    grad_pre = jnp.einsum("td,fd->tf", grad_round, w_down, preferred_element_type=F32) * gelu_slope(pre)
    grad_fc_bias = jnp.sum(grad_pre, axis=0)
    grad_pre_round = grad_pre.astype(BF)
    grad_second = jnp.einsum("tf,df->td", grad_pre_round, w_up, preferred_element_type=F32)
    grad_mlp_gain = jnp.sum(grad_second * normed_two, axis=0)
    grad_mlp_shift = jnp.sum(grad_second, axis=0)
    grad_middle = grad_state + norm_backward(grad_second, normed_two, inverse_two, gain_two)
    grad_out_bias = jnp.sum(grad_middle, axis=0)
    middle_round = grad_middle.astype(BF)
    shard_mid = scatter(grid, [(mixed_round, middle_round), (second, grad_pre_round)])
    grad_mixed = jnp.einsum("td,cd->tc", middle_round, w_mix, preferred_element_type=F32).astype(BF)

    grad_local = spread(split_groups(grid, grad_mixed, None, 1))
    grad_q, grad_own, grad_far = attend_back(
        packed, all_keys, query_pos, key_pos, mixed_local, log_total, grad_local, heads
    )
    came = [grid.along_x(grad_far[dx - 1], -dx) for dx in range(1, X)]
    back = collect(return_pieces(grad_q, grad_own, came, Z))
    grad_joint, joint_sums = join_groups(grid, back, 3)
    grad_query_bias = joint_sums[:, :D]
    grad_value_bias = joint_sums[:, 2 * D :]
    grad_first = jnp.einsum("te,de->td", grad_joint, w_joint, preferred_element_type=F32)
    grad_attn_gain = jnp.sum(grad_first * normed_one, axis=0)
    grad_attn_shift = jnp.sum(grad_first, axis=0)
    grad_in = grad_middle + norm_backward(grad_first, normed_one, inverse_one, gain_one)

    vectors = [
        grad_attn_gain,
        grad_attn_shift,
        grad_query_bias,
        grad_value_bias,
        grad_out_bias,
        grad_mlp_gain,
        grad_mlp_shift,
        grad_proj_bias,
    ]
    vectors = [item.reshape(1, D) for item in vectors]
    vectors.append(fold_lines(grad_fc_bias.reshape(1, -1), used - 8, rows))
    shard_first = scatter(grid, [(first, grad_joint)], vectors)
    shard_qkv, ends = shard_first[:, : 3 * D], shard_first[:, 3 * D :]
    small = [ends[:, i][None] for i in range(8)]
    return (
        block_out,
        grad_in[None],
        small[0],
        small[1],
        shard_qkv[None],
        small[2],
        small[3],
        shard_mid[None, :, :D],
        small[4],
        small[5],
        small[6],
        shard_mid[None, :, D:],
        ends[:, 8:used].T.reshape(1, -1),
        shard_proj[None],
        small[7],
    )


def solution(mesh):
    grid = Grid(mesh)

    def local(*args):
        return local_step(grid, *args)

    placed = (
        P("fsdp", "ctx", None),
        P("fsdp", None),
        P(None, ("ctx", "fsdp")),
        P(None, ("ctx", "fsdp")),
        P(None, ("ctx", "fsdp"), None),
        P(None, ("ctx", "fsdp")),
        P(None, ("ctx", "fsdp")),
        P(None, ("ctx", "fsdp"), None),
        P(None, ("ctx", "fsdp")),
        P(None, ("ctx", "fsdp")),
        P(None, ("ctx", "fsdp")),
        P(None, ("ctx", "fsdp"), None),
        P(None, ("ctx", "fsdp")),
        P(None, ("ctx", "fsdp"), None),
        P(None, ("ctx", "fsdp")),
        P("fsdp", "ctx", None),
    )
    return jax.shard_map(
        local,
        mesh=mesh,
        in_specs=placed,
        out_specs=(
            P("fsdp", "ctx", None),
            P("fsdp", "ctx", None),
            P(None, ("ctx", "fsdp")),
            P(None, ("ctx", "fsdp")),
            P(None, ("ctx", "fsdp"), None),
            P(None, ("ctx", "fsdp")),
            P(None, ("ctx", "fsdp")),
            P(None, ("ctx", "fsdp"), None),
            P(None, ("ctx", "fsdp")),
            P(None, ("ctx", "fsdp")),
            P(None, ("ctx", "fsdp")),
            P(None, ("ctx", "fsdp"), None),
            P(None, ("ctx", "fsdp")),
            P(None, ("ctx", "fsdp"), None),
            P(None, ("ctx", "fsdp")),
        ),
        check_vma=False,
    )
```
